128 devices in a mesh: row: 16 (over y, z_hi, core), col: 8 (over x, z_lo).
Axes of the slice: x: 4, y: 4, z: 4 (z_hi: 2, z_lo: 2; z = z_hi * 2 + z_lo), core: 2. Of those that a mesh axis runs over, the one named last changes fastest.
Arguments:
- aligned_family_embedding: bfloat16 [512, 768, 256], P('row', 'col'), may hold values from -24 to 24
- aligned_slot_available: int32 [512, 768], P('row', 'col'), may hold values from 0 to 1, as said below
- chain_site_available: int32 [768], replicated, may hold values 0 or 1
- duo_embedding: float32 [768, 768, 128], P('row', 'col'), may hold values from -1.2 to 1.2
- averaging_layernorm_stretch: float32 [256], replicated, may hold values from 0.1 to 1.9
- lineup_layernorm_stretch: float32 [256], replicated, may hold values from 0.1 to 1.9
- duo_layernorm_stretch: float32 [128], replicated, may hold values from 0.1 to 1.9
- lefthand_linear_kernel: bfloat16 [256, 32], replicated, may hold values from -0.375 to 0.375
- righthand_linear_kernel: bfloat16 [256, 32], replicated, may hold values from -0.375 to 0.375
- kronecker_linear_kernel: bfloat16 [1024, 128], replicated, may hold values from -0.1875 to 0.1875
- duo_logit_kernel: bfloat16 [128, 8], replicated, may hold values from -0.75 to 0.75
- asker_lookup_sigmoid_kernel: bfloat16 [256, 1024], replicated, may hold values from -8 to 8
- closing_linear_kernel: bfloat16 [256, 256], replicated, may hold values from -0.375 to 0.375
Outputs:
- refreshed_family_embedding: bfloat16 [512, 768, 256], P('row', 'col')
- duo_after_averaging: float32 [768, 768, 128], P('row', 'col')
The draws below stay inside these ranges and needn't reach their ends.
Inputs may be any that keep to these rules, and one draw needn't show every extreme that they name: `aligned_slot_available`: 0 or 1; sequence 0 is present at every residue.
All inputs are finite; a program needn't handle non-finite values.
Results may differ from the reference program's by a relative error of at most 0.0052.
Values may be sent and summed in bfloat16 or wider, within the bound.
A program may use at most 192 MiB of HBM per device.

```python
import math
import jax
import jax.numpy as jnp
from jax import lax

C_M = 256
C_Z = 128
C_OPM = 32
HEADS = 8
HEAD_DIM = 32
R = 768
S = 512
N_ROW = 16


latent_rank = 8


def draw_aligned_family_embedding(key, part):
    subkeys = jax.random.split(key, 6)
    consensus = jnp.clip(jax.random.normal(subkeys[0], (1, R, C_M), jnp.float32), -5.0, 5.0) * 0.4
    factors = jnp.clip(jax.random.normal(subkeys[4], (S, latent_rank), jnp.float32), -4.0, 4.0)
    loadings = jnp.clip(jax.random.normal(subkeys[5], (latent_rank, R * C_M), jnp.float32), -4.0, 4.0) / math.sqrt(latent_rank)
    shared = jnp.dot(factors, loadings).reshape(S, R, C_M) * 1.5
    noise_part = jnp.clip(jax.random.normal(subkeys[1], (S, R, C_M), jnp.float32), -5.0, 5.0)
    values = consensus + shared + noise_part
    return jnp.clip(values, -24.0, 24.0).astype(jnp.bfloat16)


def draw_aligned_slot_available(key, part):
    subkeys = jax.random.split(key, 2)
    row_ids = jnp.arange(S, dtype=jnp.int32)[:, None]
    limits = 3 + 9 * row_ids // S + jax.random.randint(subkeys[0], (S, 1), 0, 4, dtype=jnp.int32)
    sampled = jax.random.randint(subkeys[1], (S, R), 0, 16, dtype=jnp.int32)
    kept_ones = jnp.where(sampled < limits, 1, 0)
    return jnp.where(row_ids == 0, 1, kept_ones).astype(jnp.int32)


def draw_asker_lookup_sigmoid_kernel(key, part):
    inner_width = HEADS * HEAD_DIM
    subkeys = jax.random.split(key, 2)
    base_part = jnp.clip(jax.random.normal(subkeys[0], (C_M, inner_width), jnp.float32), -5.0, 5.0) / math.sqrt(C_M)
    rest_part = jnp.clip(jax.random.normal(subkeys[1], (C_M, 3 * inner_width), jnp.float32), -5.0, 5.0) / math.sqrt(C_M)
    values = jnp.concatenate([base_part, rest_part], axis=1)
    return values.astype(jnp.bfloat16)


def set_ends(entries, key, low, high):
    longest = entries.shape.index(max(entries.shape))
    spots = []
    for shift in (0, 1):
        where = [jax.random.randint(jax.random.fold_in(key, axis), (), 0, length) for axis, length in enumerate(entries.shape)]
        where[longest] = (where[longest] + shift) % entries.shape[longest]
        spots.append(tuple(where))
    return entries.at[spots[0]].set(low).at[spots[1]].set(high)


def shard_levels(rng, shape, pieces, smallest, top_value):
    loudness, own = 1.0, jax.random.fold_in(rng, 6)
    for position, shards_of in pieces:
        heights = jnp.exp(jax.random.uniform(jax.random.fold_in(own, position), (shards_of,), jnp.float32, smallest / len(pieces), top_value / len(pieces)))
        loudness = loudness * jnp.repeat(heights, shape[position] // shards_of).reshape([-1 if axis == position else 1 for axis in range(len(shape))])
    return loudness


def noise(own_key, dims, spread, bound, pieces=(), held_as=jnp.bfloat16):
    values = jax.random.normal(own_key, dims, jnp.float32) * spread
    if len(pieces) > 0:
        values = shard_levels(own_key, dims, pieces, -0.22, 0.18) * values
    return jnp.clip(values, min=-bound, max=bound).astype(held_as)


def setup_inputs(seed: int = 0) -> dict:
    key_of = jax.random.split(jax.random.key(seed), 14)
    return {
        "aligned_family_embedding": draw_aligned_family_embedding(jax.random.fold_in(key_of[13], 71), 0),
        "aligned_slot_available": draw_aligned_slot_available(jax.random.fold_in(key_of[13], 71), 0),
        "chain_site_available": set_ends((jax.random.randint(key_of[2], (R,), 0, 8) < 7).astype(jnp.int32), jax.random.fold_in(key_of[2], 1), 0, 1),
        "duo_embedding": noise(key_of[3], (R, R, C_Z), 0.15, 1.2, ((0, 16), (1, 8)), jnp.float32),
        "averaging_layernorm_stretch": jnp.clip(1.0 + 0.18 * jax.random.normal(key_of[4], (C_M,), jnp.float32), 0.1, 1.9),
        "lineup_layernorm_stretch": jnp.clip(1.0 + 0.18 * jax.random.normal(key_of[5], (C_M,), jnp.float32), 0.1, 1.9),
        "duo_layernorm_stretch": jnp.clip(1.0 + 0.18 * jax.random.normal(key_of[6], (C_Z,), jnp.float32), 0.1, 1.9),
        "lefthand_linear_kernel": noise(key_of[7], (C_M, C_OPM), C_M ** -0.5, 0.375),
        "righthand_linear_kernel": noise(key_of[8], (C_M, C_OPM), C_M ** -0.5, 0.375),
        "kronecker_linear_kernel": noise(key_of[9], (C_OPM * C_OPM, C_Z), (C_OPM * C_OPM) ** -0.5, 0.1875),
        "duo_logit_kernel": noise(key_of[10], (C_Z, HEADS), (C_Z // 2) ** -0.5, 0.75),
        "asker_lookup_sigmoid_kernel": draw_asker_lookup_sigmoid_kernel(jax.random.fold_in(key_of[13], 71), 0),
        "closing_linear_kernel": noise(key_of[12], (HEADS * HEAD_DIM, C_M), (HEADS * HEAD_DIM) ** -0.5, 0.375),
    }


EPSILON = 1e-05
CONTRACT_FIRST = (((0,), (0,)), ((), ()))

def standardize_features(values):
    average = lax.optimization_barrier(jnp.mean(values, axis=-1, keepdims=True))
    centred = values - average
    variance = lax.optimization_barrier(jnp.mean(centred * centred, axis=-1, keepdims=True))
    return centred * lax.rsqrt(variance + EPSILON)

def rounded(values):
    return lax.optimization_barrier(values.astype(jnp.bfloat16)).astype(jnp.float32)

def reference(aligned_family_embedding, aligned_slot_available, chain_site_available, duo_embedding, averaging_layernorm_stretch, lineup_layernorm_stretch, duo_layernorm_stretch, lefthand_linear_kernel, righthand_linear_kernel, kronecker_linear_kernel, duo_logit_kernel, asker_lookup_sigmoid_kernel, closing_linear_kernel):
    standardized_features = standardize_features(aligned_family_embedding.astype(jnp.float32))
    availability_real = aligned_slot_available.astype(jnp.float32)
    opm_input = rounded(standardized_features * averaging_layernorm_stretch)
    left_flat = (jnp.einsum('src,ca->sra', opm_input, lefthand_linear_kernel.astype(jnp.float32)) * availability_real[:, :, None]).astype(jnp.bfloat16).reshape(S, R * C_OPM)
    right_flat = (jnp.einsum('src,ca->sra', opm_input, righthand_linear_kernel.astype(jnp.float32)) * availability_real[:, :, None]).astype(jnp.bfloat16).reshape(S, R * C_OPM)
    row_block = R // N_ROW
    left_blocks = left_flat.reshape(S, N_ROW, row_block * C_OPM).transpose(1, 0, 2)
    mask_blocks = availability_real.reshape(S, N_ROW, row_block).transpose(1, 0, 2)
    mixing = kronecker_linear_kernel.astype(jnp.float32).reshape(C_OPM, C_OPM, C_Z)

    def pair_block(group_members):
        left_part, mask_part = group_members
        outer_sum = lax.dot_general(left_part, right_flat, CONTRACT_FIRST, preferred_element_type=jnp.float32)
        counts = lax.dot_general(mask_part, availability_real, CONTRACT_FIRST, preferred_element_type=jnp.float32)
        outer_round = rounded(outer_sum).reshape(row_block, C_OPM, R, C_OPM)
        update = jnp.einsum('iajb,abk->ijk', outer_round, mixing)
        return update / (counts + 0.001)[:, :, None]
    update = lax.map(pair_block, (left_blocks, mask_blocks)).reshape(R, R, C_Z)
    residue_float = chain_site_available.astype(jnp.float32)
    duo_after_averaging = duo_embedding + update * (residue_float[:, None] * residue_float[None, :])[:, :, None]
    pair_input = rounded(standardize_features(duo_after_averaging) * duo_layernorm_stretch)
    pair_bias = rounded(jnp.einsum('ijc,ch->hij', pair_input, duo_logit_kernel.astype(jnp.float32)))
    exponential_probabilities = (standardized_features * lineup_layernorm_stretch).astype(jnp.bfloat16)
    inner_width = HEADS * HEAD_DIM
    score_scale = HEAD_DIM ** (-0.5)
    output_as_float = closing_linear_kernel.astype(jnp.float32)

    def solitary_alignee(group_members):
        row_entry, row_present_mask, alignment_row = group_members
        projected = rounded(jnp.dot(row_entry, asker_lookup_sigmoid_kernel, preferred_element_type=jnp.float32))
        queries = projected[:, :inner_width].reshape(R, HEADS, HEAD_DIM)
        keys_all = projected[:, inner_width:2 * inner_width].reshape(R, HEADS, HEAD_DIM)
        values_all = projected[:, 2 * inner_width:3 * inner_width].reshape(R, HEADS, HEAD_DIM)
        gate_pre = projected[:, 3 * inner_width:]
        scores = jnp.einsum('qhd,khd->hqk', queries, keys_all) * score_scale + pair_bias + 1000000000.0 * (row_present_mask[None, None, :] - 1.0)
        highest = lax.optimization_barrier(jnp.max(scores, axis=-1, keepdims=True))
        exponent = jnp.exp(scores - highest)
        weights = rounded(exponent / lax.optimization_barrier(jnp.sum(exponent, axis=-1, keepdims=True)))
        mixed_rows = jnp.einsum('hqk,khd->qhd', weights, values_all).reshape(R, inner_width)
        gated_row_output = rounded(mixed_rows * jax.nn.sigmoid(gate_pre))
        return (alignment_row.astype(jnp.float32) + jnp.einsum('lg,gf->lf', gated_row_output, output_as_float)).astype(jnp.bfloat16)
    refreshed_family_embedding = lax.map(solitary_alignee, (exponential_probabilities, availability_real, aligned_family_embedding))
    return (refreshed_family_embedding, duo_after_averaging)
```

```python
import jax
import jax.numpy as jnp
from jax import lax
from jax.experimental import pallas as pl
from jax.experimental.pallas import tpu as pltpu
from jax.sharding import PartitionSpec as P

EPSILON = 1e-05
CONTRACT_FIRST = (((0,), (0,)), ((), ()))
LAST_LAST = (((1,), (1,)), ((), ()))
HEAD_DIM = 32


def laid_out(pieces, dim):
    lengths = list(pieces.shape[1:])
    lengths[dim] *= pieces.shape[0]
    return jnp.moveaxis(pieces, 0, dim).reshape(lengths)


def one_gather(arrays, axis, dims):
    line = jnp.concatenate([a.reshape(-1) for a in arrays])
    lines, at, outs = (lax.all_gather(line, axis), 0, [])
    for a, dim in zip(arrays, dims):
        pieces = lines[:, at : at + a.size].reshape(-1, *a.shape)
        outs.append(laid_out(pieces, dim))
        at += a.size
    return tuple(outs)


def in_one_piece(arrays, axis, dim, along):
    ends, at = ([], 0)
    for a in arrays[:-1]:
        at += a.shape[along]
        ends.append(at)
    both = jnp.concatenate(arrays, axis=along)
    return tuple(jnp.split(lax.all_gather(both, axis, axis=dim, tiled=True), ends, axis=along))


def sent_to_all(x, axis):
    copies = jnp.broadcast_to(x, (lax.axis_size(axis), *x.shape))
    return lax.all_to_all(copies, axis, split_axis=0, concat_axis=0, tiled=True)


def gather_directly(x, axis, dim):
    return laid_out(sent_to_all(x, axis), dim)


def sent_together(arrays, axis, split_dim, concat_dim, along):
    columns = [a.reshape(*a.shape[:along], -1) for a in arrays]
    both = jnp.concatenate(columns, axis=along)
    whole, at, outs = (
        lax.all_to_all(both, axis, split_axis=split_dim, concat_axis=concat_dim, tiled=True),
        0,
        [],
    )
    for a, column in zip(arrays, columns):
        section = whole[..., at : at + column.shape[along]]
        outs.append(section.reshape(*section.shape[:along], *a.shape[along:]))
        at += column.shape[along]
    return tuple(outs)


def standardize_features(values):
    average = jnp.mean(values, axis=-1, keepdims=True)
    centred = values - average
    variance = jnp.mean(centred * centred, axis=-1, keepdims=True)
    return centred * lax.rsqrt(variance + EPSILON)


def project_rows(inputs, weight, availability_real):
    projected = jnp.einsum("src,ca->sra", inputs, weight, preferred_element_type=jnp.float32)
    return (projected * availability_real[:, :, None]).astype(jnp.bfloat16)


LOG2E = 1.4426950408889634


def attn_kernel(x_ref, mb_ref, hm_ref, bias_ref, wq_ref, wk_ref, wv_ref, wg_ref, o_ref, q_s, kt_s, v_s, bf_s, acc_s):
    blk = pl.program_id(0)
    seqs = x_ref.shape[0]
    rows = o_ref.shape[1]
    heads = bias_ref.shape[0]
    scale = float(HEAD_DIM) ** -0.5

    @pl.when(blk == 0)
    def _():
        def project(b, carry):
            x = x_ref[b]
            q_s[b] = jnp.dot(x, wq_ref[...], preferred_element_type=jnp.float32).astype(jnp.bfloat16)
            v_s[b] = jnp.dot(x, wv_ref[...], preferred_element_type=jnp.float32).astype(jnp.bfloat16)
            kt_s[b] = lax.dot_general(
                wk_ref[...], x, LAST_LAST, preferred_element_type=jnp.float32
            ).astype(jnp.bfloat16)
            return carry

        lax.fori_loop(0, seqs, project, 0)

    at = pl.multiple_of(blk * rows, rows)

    def one_head(h, carry):
        bf_s[...] = bias_ref[h].astype(jnp.float32) * (1.0 / scale)
        own = hm_ref[h]
        own_f = own.astype(jnp.float32)
        other = (1.0 - own_f).astype(jnp.bfloat16)

        def one_seq(b, carry):
            q = q_s[b, pl.ds(at, rows), :] * own
            s = jnp.dot(q, kt_s[b], preferred_element_type=jnp.float32) + bf_s[...] + mb_ref[b]
            top = jnp.max(s, axis=1, keepdims=True)
            p = jnp.exp2(((s - top) * (scale * LOG2E)).astype(jnp.bfloat16))
            r = jnp.dot(p, v_s[b] * own + other, preferred_element_type=jnp.float32)
            mixed = r / pltpu.roll(r, HEAD_DIM, 1)
            acc_s[b] = jnp.where(own_f > 0.0, mixed, acc_s[b])
            return carry

        return lax.fori_loop(0, seqs, one_seq, carry)

    lax.fori_loop(0, heads, one_head, 0)

    def gate(b, carry):
        g = jnp.dot(x_ref[b, pl.ds(at, rows), :], wg_ref[...], preferred_element_type=jnp.float32)
        g = g.astype(jnp.bfloat16).astype(jnp.float32)
        o_ref[b] = (acc_s[b] * jax.nn.sigmoid(g)).astype(jnp.bfloat16)
        return carry

    lax.fori_loop(0, seqs, gate, 0)


def attention(x, mask, bias, w):
    seqs, length, channels = x.shape
    heads = bias.shape[0]
    lanes = heads * HEAD_DIM
    rows = 256
    scale = float(HEAD_DIM) ** -0.5
    mb = (1e9 / scale) * (mask.astype(jnp.float32) - 1.0)[:, None, :]
    hm = (jnp.arange(lanes)[None, None, :] // HEAD_DIM == jnp.arange(heads)[:, None, None]).astype(jnp.bfloat16)
    wq, wk, wv, wg = w
    whole = lambda a: pl.BlockSpec(a.shape, lambda i: (0,) * a.ndim)
    wk = wk.T
    return pl.pallas_call(
        attn_kernel,
        grid=(length // rows,),
        out_shape=jax.ShapeDtypeStruct((seqs, length, lanes), jnp.bfloat16),
        in_specs=[
            whole(x), whole(mb), whole(hm),
            pl.BlockSpec((heads, rows, length), lambda i: (0, i, 0)),
            whole(wq), whole(wk), whole(wv), whole(wg),
        ],
        out_specs=pl.BlockSpec((seqs, rows, lanes), lambda i: (0, i, 0)),
        scratch_shapes=[
            pltpu.VMEM((seqs, length, lanes), jnp.bfloat16),
            pltpu.VMEM((seqs, lanes, length), jnp.bfloat16),
            pltpu.VMEM((seqs, length, lanes), jnp.bfloat16),
            pltpu.VMEM((rows, length), jnp.float32),
            pltpu.VMEM((seqs, rows, lanes), jnp.float32),
        ],
        compiler_params=pltpu.CompilerParams(vmem_limit_bytes=48 << 20),
        name="attn",
    )(x, mb, hm, bias, wq, wk, wv, wg)


def opm_kernel(left_ref, right_ref, lmask_ref, rmask_ref, rrow_ref, rcol_ref, pair_ref, gain_ref, w_ref, wd_ref,
               out_ref, bias_ref, rt_s, wb_s, m_s):
    step = pl.program_id(0)
    opm = w_ref.shape[0]
    cols = pair_ref.shape[1]
    group = out_ref.shape[0] // 4
    chunk = 4 * cols

    @pl.when(step == 0)
    def _():
        wb_s[...] = jnp.zeros_like(wb_s)

        def fill(b, carry):
            for i in range(4):
                wb_s[pl.ds(pl.multiple_of(b * 128 + i * 32, 32), 32), i * 128 : (i + 1) * 128] = w_ref[b]
            return carry

        lax.fori_loop(0, opm, fill, 0)

        def flip(n, carry):
            at = pl.multiple_of(n * chunk, chunk)
            rt_s[pl.ds(at, chunk), :] = right_ref[:, pl.ds(at, chunk)].T
            return carry

        lax.fori_loop(0, opm // 4, flip, 0)

    def outer(n, carry):
        at = pl.multiple_of(n * chunk, chunk)
        m = jnp.dot(rt_s[pl.ds(at, chunk), :], left_ref[...], preferred_element_type=jnp.float32)
        m = m.astype(jnp.bfloat16)
        for bb in range(4):
            for g in range(group):
                m_s[g * cols : (g + 1) * cols, pl.ds(pl.multiple_of((n * 4 + bb) * 128, 128), 128)] = m[
                    bb * cols : (bb + 1) * cols, g * 128 : (g + 1) * 128
                ]
        return carry

    lax.fori_loop(0, opm // 4, outer, 0)
    counts = lax.dot_general(rmask_ref[...], lmask_ref[0], CONTRACT_FIRST, preferred_element_type=jnp.float32)
    factor = rcol_ref[...] * rrow_ref[0] / (counts + 0.001)
    update = jnp.dot(m_s[...], wb_s[...], preferred_element_type=jnp.float32)
    for g in range(group):
        for ii in range(4):
            i = 4 * g + ii
            u = update[g * cols : (g + 1) * cols, ii * 128 : (ii + 1) * 128]
            x = pair_ref[i] + u * factor[:, i : i + 1]
            out_ref[i] = x
            x = (standardize_features(x) * gain_ref[...]).astype(jnp.bfloat16)
            bias_ref[:, i, :] = lax.dot_general(wd_ref[...], x, LAST_LAST, preferred_element_type=jnp.float32)


def opm(left, right, lmask, rmask, rrow, rcol, pair, gain, kron, logit):
    rows, cols, channels = pair.shape
    seqs = left.shape[0]
    width = left.shape[1] // rows
    heads = logit.shape[1]
    per = 16
    steps = rows // per
    lm = lmask.reshape(seqs, steps, per).transpose(1, 0, 2)
    rr = rrow.reshape(steps, 1, per)
    rc = rcol.reshape(cols, 1)
    w = kron.reshape(width, width, channels).transpose(1, 0, 2)
    gain = gain.reshape(1, channels)
    wd = logit.T
    whole = lambda a: pl.BlockSpec(a.shape, lambda i: (0,) * a.ndim)
    return pl.pallas_call(
        opm_kernel,
        grid=(steps,),
        out_shape=(
            jax.ShapeDtypeStruct(pair.shape, jnp.float32),
            jax.ShapeDtypeStruct((heads, rows, cols), jnp.float32),
        ),
        in_specs=[
            pl.BlockSpec((seqs, per * width), lambda i: (0, i)),
            whole(right),
            pl.BlockSpec((1, seqs, per), lambda i: (i, 0, 0)),
            whole(rmask),
            pl.BlockSpec((1, 1, per), lambda i: (i, 0, 0)),
            whole(rc),
            pl.BlockSpec((per, cols, channels), lambda i: (i, 0, 0)),
            whole(gain), whole(w), whole(wd),
        ],
        out_specs=(
            pl.BlockSpec((per, cols, channels), lambda i: (i, 0, 0)),
            pl.BlockSpec((heads, per, cols), lambda i: (0, i, 0)),
        ),
        scratch_shapes=[
            pltpu.VMEM((cols * width, seqs), jnp.bfloat16),
            pltpu.VMEM((128 * width, 4 * channels), jnp.bfloat16),
            pltpu.VMEM((per // 4 * cols, 128 * width), jnp.bfloat16),
        ],
        compiler_params=pltpu.CompilerParams(vmem_limit_bytes=52 << 20),
        name="opm",
    )(left, right, lm, rmask, rr, rc, pair, gain, w, wd)


def shards(
    aligned_family_embedding,
    aligned_slot_available,
    chain_site_available,
    duo_embedding,
    averaging_layernorm_stretch,
    lineup_layernorm_stretch,
    duo_layernorm_stretch,
    lefthand_linear_kernel,
    righthand_linear_kernel,
    kronecker_linear_kernel,
    duo_logit_kernel,
    asker_lookup_sigmoid_kernel,
    closing_linear_kernel,
):
    homolog_number, amino_position_number, discarded_carry = aligned_family_embedding.shape
    res_rows = duo_embedding.shape[0]
    opm_width = lefthand_linear_kernel.shape[1]
    head_count = duo_logit_kernel.shape[1]
    inner_width = closing_linear_kernel.shape[0]
    row_index = lax.axis_index("row")
    col_index = lax.axis_index("col")
    standardized_features = standardize_features(aligned_family_embedding.astype(jnp.float32))
    availability_real = aligned_slot_available.astype(jnp.float32)
    shrunk_availability = aligned_slot_available.astype(jnp.bfloat16)
    opm_input = (standardized_features * averaging_layernorm_stretch).astype(jnp.bfloat16)
    left_flat = project_rows(opm_input, lefthand_linear_kernel, availability_real).reshape(
        homolog_number, amino_position_number * opm_width
    )
    right_flat = jnp.einsum(
        "src,ca->sar", opm_input, righthand_linear_kernel, preferred_element_type=jnp.float32
    )
    right_flat = (right_flat * availability_real[:, None, :]).astype(jnp.bfloat16)
    right_flat = right_flat.reshape(homolog_number, amino_position_number * opm_width)
    left_wide, mask_wide = one_gather((left_flat, shrunk_availability), "col", (1, 1))
    left_block, left_mask = (
        lax.all_to_all(left_wide, "row", split_axis=1, concat_axis=0, tiled=True),
        lax.all_to_all(mask_wide, "row", split_axis=1, concat_axis=0, tiled=True),
    )
    right_all, mask_all = in_one_piece((right_flat, shrunk_availability), "row", 0, 1)
    residue_float = chain_site_available.astype(jnp.float32)
    residue_rows = lax.dynamic_slice_in_dim(residue_float, row_index * res_rows, res_rows)
    residue_cols = lax.dynamic_slice_in_dim(
        residue_float, col_index * amino_position_number, amino_position_number
    )
    duo_after_averaging, bias_tile = opm(
        left_block, right_all, left_mask, mask_all, residue_rows, residue_cols, duo_embedding,
        duo_layernorm_stretch, kronecker_linear_kernel, duo_logit_kernel,
    )
    bias_tile = bias_tile.astype(jnp.bfloat16)
    bias_cols = gather_directly(bias_tile, "col", 2)
    exponential_probabilities = (standardized_features * lineup_layernorm_stretch).astype(
        jnp.bfloat16
    )
    rows_input, rows_mask = sent_together(
        (exponential_probabilities, shrunk_availability), "col", 0, 1, 2
    )
    bias_whole = lax.all_gather(bias_cols, "row", axis=1, tiled=True)
    half = inner_width // 2
    parts = []
    for k in range(2):
        w = [
            asker_lookup_sigmoid_kernel[:, n * inner_width + k * half : n * inner_width + (k + 1) * half]
            for n in range(4)
        ]
        parts.append(attention(rows_input, rows_mask, bias_whole[k * (head_count // 2) : (k + 1) * (head_count // 2)], w))
    gated_whole = jnp.concatenate(parts, axis=2)
    gated_local = lax.all_to_all(gated_whole, "col", split_axis=1, concat_axis=0, tiled=True)
    summed_increment = jnp.einsum(
        "sqd,dc->sqc", gated_local, closing_linear_kernel, preferred_element_type=jnp.float32
    )
    refreshed_family_embedding = (
        aligned_family_embedding.astype(jnp.float32) + summed_increment
    ).astype(jnp.bfloat16)
    return (refreshed_family_embedding, duo_after_averaging)


def solution(mesh):
    placed = (
        P("row", "col", None),
        P("row", "col"),
        P(),
        P("row", "col", None),
        P(),
        P(),
        P(),
        P(),
        P(),
        P(),
        P(),
        P(),
        P(),
    )
    return jax.shard_map(
        shards,
        mesh=mesh,
        in_specs=placed,
        out_specs=(P("row", "col", None), P("row", "col", None)),
        check_vma=False,
    )
```

```python
import jax
import jax.numpy as jnp
from jax import lax
from jax.experimental import pallas as pl
from jax.experimental.pallas import tpu as pltpu
from jax.sharding import PartitionSpec as P

EPSILON = 1e-05
CONTRACT_FIRST = (((0,), (0,)), ((), ()))
LAST_LAST = (((1,), (1,)), ((), ()))
HEAD_DIM = 32


def standardize_features(values):
    average = jnp.mean(values, axis=-1, keepdims=True)
    centred = values - average
    variance = jnp.mean(centred * centred, axis=-1, keepdims=True)
    return centred * lax.rsqrt(variance + EPSILON)


MESH = pl.DeviceIdType.MESH


def place():
    r, c = lax.axis_index("row"), lax.axis_index("col")
    return r, c


def row_of(y, zh, core):
    return y * 4 + zh * 2 + core


def remote(src, dst, send, recv, device):
    return pltpu.make_async_remote_copy(
        src_ref=src, dst_ref=dst, send_sem=send, recv_sem=recv, device_id=device, device_id_type=MESH
    )


def signal(barrier, device):
    pl.semaphore_signal(barrier, inc=1, device_id=device, device_id_type=MESH)


def spread_kernel(left_ref, right_ref, left_out, right_out, lsend, lrecv, rsend, rrecv, fsend, frecv):
    r, c = place()
    chip, core = r // 2, r % 2
    seqs = right_ref.shape[0]
    here = pl.ds(pl.multiple_of(r * seqs, seqs), seqs)
    partner = (chip * 2 + 1 - core, c)
    mine = chip == c
    barrier = pltpu.get_barrier_semaphore()
    for d in range(1, 8):
        signal(barrier, ((r + 2 * d) % 16, c))
    signal(barrier, partner)
    for n in range(16):

        @pl.when(jnp.logical_not(jnp.logical_and(mine, r == n)))
        def _():
            signal(barrier, (n, chip))

    pl.semaphore_wait(barrier, 24 - mine.astype(jnp.int32))

    rights = [None]
    for d in range(1, 8):
        cp = remote(right_ref, right_out.at[here], rsend.at[d], rrecv.at[d], ((r + 2 * d) % 16, c))
        cp.start()
        rights.append(cp)
    own = pltpu.make_async_copy(right_ref, right_out.at[here], rrecv.at[0])
    own.start()
    forwards = [remote(right_ref, right_out.at[here], fsend.at[0], frecv.at[0], partner)]
    forwards[0].start()
    lefts = []
    for j in range(8):
        for h in range(2):
            cd = (c + j) % 8
            cp = remote(left_ref.at[h], left_out.at[here], lsend.at[2 * j + h], lrecv.at[r], (2 * c + h, cd))
            lefts.append((cp, h, j))
            if j == 0:
                own_left = jnp.logical_and(mine, core == h)

                @pl.when(jnp.logical_not(own_left))
                def _():
                    cp.start()

                @pl.when(own_left)
                def _():
                    pltpu.make_async_copy(left_ref.at[h], left_out.at[here], lrecv.at[r]).start()
            else:
                cp.start()
    for d in range(1, 8):
        rights[d].wait_recv()
        block = pl.ds(pl.multiple_of(((r + 16 - 2 * d) % 16) * seqs, seqs), seqs)
        fw = remote(right_out.at[block], right_out.at[block], fsend.at[d], frecv.at[d], partner)
        fw.start()
        forwards.append(fw)
    own.wait()
    for n in range(16):
        pltpu.make_async_copy(left_ref.at[0], left_out.at[pl.ds(n * seqs, seqs)], lrecv.at[n]).wait()
    for d in range(8):
        forwards[d].wait()
    for d in range(1, 8):
        rights[d].wait_send()
    for cp, h, j in lefts:
        if j == 0:

            @pl.when(jnp.logical_not(jnp.logical_and(mine, core == h)))
            def _():
                cp.wait_send()
        else:
            cp.wait_send()


def spread(left, right):
    seqs = right.shape[0]
    vmem = pl.BlockSpec(memory_space=pltpu.VMEM)
    hbm = pl.BlockSpec(memory_space=pl.ANY)
    dma = pltpu.SemaphoreType.DMA
    return pl.pallas_call(
        spread_kernel,
        out_shape=(
            jax.ShapeDtypeStruct((16 * seqs, left.shape[2]), jnp.bfloat16),
            jax.ShapeDtypeStruct((16 * seqs, right.shape[1]), jnp.bfloat16),
        ),
        in_specs=[vmem, vmem],
        out_specs=(hbm, hbm),
        scratch_shapes=[dma((16,)), dma((16,)), dma((8,)), dma((8,)), dma((8,)), dma((8,))],
        compiler_params=pltpu.CompilerParams(collective_id=1, has_side_effects=True),
        name="spread",
    )(left, right)


def share_kernel(tile_ref, x_ref, m_ref, a_out, b_out, c_out, x_out, m_out, block,
                 csend, crecv, csem, s1, r1, l1, s2, r2, s3, r3):
    r, c = place()
    spot = {"x": c // 2, "y": r // 4, "z": ((r // 2) % 2) * 2 + c % 2}
    core = r % 2

    def peer(dim, d):
        to = dict(spot)
        to[dim] = (spot[dim] + d) % 4
        return (row_of(to["y"], to["z"] // 2, core), to["x"] * 2 + to["z"] % 2)

    partner = ((r // 2) * 2 + 1 - core, c)
    barrier = pltpu.get_barrier_semaphore()
    signal(barrier, partner)
    for dim in "xyz":
        for d in range(1, 4):
            signal(barrier, peer(dim, d))
    pl.semaphore_wait(barrier, 10)

    rows, lanes = tile_ref.shape[0], tile_ref.shape[1] // 2
    here = pl.ds(pl.multiple_of(core * rows, rows), rows)
    give = tile_ref.at[:, pl.ds(pl.multiple_of((1 - core) * lanes, lanes), lanes)]
    keep = tile_ref.at[:, pl.ds(pl.multiple_of(core * lanes, lanes), lanes)]
    swap = remote(give, block.at[here], csend.at[0], crecv.at[0], partner)
    swap.start()
    own = pltpu.make_async_copy(keep, block.at[here], csem.at[0])
    own.start()
    xs = remote(x_ref, x_out, csend.at[1], crecv.at[1], partner)
    ms = remote(m_ref, m_out, csend.at[2], crecv.at[2], partner)
    own.wait()
    swap.wait_recv()

    orders = ((a_out, "xzy"), (b_out, "yxz"), (c_out, "zyx"))
    part = block.shape[0] // 3
    sent = []
    first = []
    for o, (out, dims) in enumerate(orders):
        d1, d2, d3 = dims
        slot = out.at[spot[d3], spot[d2], spot[d1]]
        piece = block.at[pl.ds(o * part, part)]
        mine = pltpu.make_async_copy(piece, slot, l1.at[o])
        mine.start()
        cps = []
        for d in range(1, 4):
            cp = remote(piece, slot, s1.at[o * 4 + d], r1.at[o * 4 + d], peer(d1, d))
            cp.start()
            cps.append(cp)
        first.append((mine, cps))
        sent += cps
    xs.start()
    ms.start()
    second = []
    for o, (out, dims) in enumerate(orders):
        d1, d2, d3 = dims
        mine, cps = first[o]
        mine.wait()
        for cp in cps:
            cp.wait_recv()
        slot = out.at[spot[d3], spot[d2]]
        cps = []
        for d in range(1, 4):
            cp = remote(slot, slot, s2.at[o * 4 + d], r2.at[o * 4 + d], peer(d2, d))
            cp.start()
            cps.append(cp)
        second.append(cps)
        sent += cps
        for d in range(1, 4):
            cp = remote(slot, slot, s3.at[o * 16 + d], r3.at[o * 16 + d], peer(d3, d))
            cp.start()
            sent.append(cp)
    for e in range(1, 4):
        for o, (out, dims) in enumerate(orders):
            d1, d2, d3 = dims
            second[o][e - 1].wait_recv()
            slot = out.at[spot[d3], (spot[d2] + 4 - e) % 4]
            for d in range(1, 4):
                cp = remote(slot, slot, s3.at[o * 16 + e * 4 + d], r3.at[o * 16 + e * 4 + d], peer(d3, d))
                cp.start()
                sent.append(cp)
    for o, (out, dims) in enumerate(orders):
        d1, d2, d3 = dims
        for e in range(4):
            for d in range(1, 4):
                slot = out.at[(spot[d3] + 4 - d) % 4, (spot[d2] + 4 - e) % 4]
                remote(slot, slot, s3.at[o * 16 + e * 4 + d], r3.at[o * 16 + e * 4 + d], peer(d3, d)).wait_recv()
    for cp in sent:
        cp.wait_send()
    swap.wait_send()
    xs.wait()
    ms.wait()


def share(tile, x, m):
    vmem = pl.BlockSpec(memory_space=pltpu.VMEM)
    hbm = pl.BlockSpec(memory_space=pl.ANY)
    dma = pltpu.SemaphoreType.DMA
    rows, lanes = 2 * tile.shape[0], tile.shape[1] // 2
    table = jax.ShapeDtypeStruct((4, 4, 4, rows // 3, lanes), jnp.bfloat16)
    return pl.pallas_call(
        share_kernel,
        out_shape=(
            table, table, table,
            jax.ShapeDtypeStruct(x.shape, x.dtype),
            jax.ShapeDtypeStruct(m.shape, m.dtype),
        ),
        in_specs=[vmem, hbm, vmem],
        out_specs=(hbm,) * 5,
        scratch_shapes=[
            pltpu.VMEM((rows, lanes), jnp.bfloat16),
            dma((3,)), dma((3,)), dma((1,)),
            dma((12,)), dma((12,)), dma((3,)),
            dma((12,)), dma((12,)),
            dma((48,)), dma((48,)),
        ],
        compiler_params=pltpu.CompilerParams(collective_id=3, has_side_effects=True),
        name="share",
    )(tile, x, m)


LOG2E = 1.4426950408889634


def attn_kernel(x0_ref, x1_ref, mb_ref, hm_ref, ta_ref, tb_ref, tc_ref, wq_ref, wk_ref, wv_ref, wg_ref, o_ref,
                q_s, kt_s, v_s, bf_s, acc_s, out_s, send, recv):
    blk = pl.program_id(0)
    r, c = place()
    chip, core = r // 2, r % 2
    half = x0_ref.shape[0]
    seqs, rows = acc_s.shape[0], acc_s.shape[1]
    heads = hm_ref.shape[0]
    cols = o_ref.shape[2]
    scale = float(HEAD_DIM) ** -0.5

    @pl.when(blk == 0)
    def _():
        barrier = pltpu.get_barrier_semaphore()
        for j in range(8):
            for k in range(2):
                if j == 0:

                    @pl.when(core != k)
                    def _():
                        signal(barrier, (chip * 2 + k, c))
                else:
                    signal(barrier, (chip * 2 + k, (c + j) % 8))
        pl.semaphore_wait(barrier, 15)
        for n, x_ref in enumerate((x0_ref, x1_ref)):

            def project(b, carry):
                x = x_ref[b]
                at = n * half + b
                q_s[at] = jnp.dot(x, wq_ref[...], preferred_element_type=jnp.float32).astype(jnp.bfloat16)
                v_s[at] = jnp.dot(x, wv_ref[...], preferred_element_type=jnp.float32).astype(jnp.bfloat16)
                kt_s[at] = lax.dot_general(
                    wk_ref[...], x, LAST_LAST, preferred_element_type=jnp.float32
                ).astype(jnp.bfloat16)
                return carry

            lax.fori_loop(0, half, project, 0)

    at = pl.multiple_of(blk * rows, rows)

    def assemble(n, carry):
        y = blk * 2 + n // 2
        zh = n % 2
        for o in range(3):
            pieces = []
            for cc in range(8):
                x, z = cc // 2, zh * 2 + cc % 2
                if o == 0:
                    piece = ta_ref[y, z, x]
                elif o == 1:
                    piece = tb_ref[z, x, y]
                else:
                    piece = tc_ref[x, y, z]
                pieces.append(piece.astype(jnp.float32) * (1.0 / scale))
            for h in range(heads):
                bf_s[h, pl.ds(pl.multiple_of(n * cols + o * 32, 32), 32), :] = jnp.concatenate(
                    [p[:, h * cols : (h + 1) * cols] for p in pieces], axis=1
                )
        return carry

    lax.fori_loop(0, rows // cols, assemble, 0)

    def one_head(h, carry):
        own = hm_ref[h]
        own_f = own.astype(jnp.float32)
        other = (1.0 - own_f).astype(jnp.bfloat16)

        def one_seq(b, carry):
            q = q_s[b, pl.ds(at, rows), :] * own
            s = jnp.dot(q, kt_s[b], preferred_element_type=jnp.float32) + bf_s[h] + mb_ref[b]
            top = jnp.max(s, axis=1, keepdims=True)
            p = jnp.exp2(((s - top) * (scale * LOG2E)).astype(jnp.bfloat16))
            w = jnp.dot(p, v_s[b] * own + other, preferred_element_type=jnp.float32)
            mixed = w / pltpu.roll(w, HEAD_DIM, 1)
            acc_s[b] = jnp.where(own_f > 0.0, mixed, acc_s[b])
            return carry

        return lax.fori_loop(0, seqs, one_seq, carry, unroll=4)

    lax.fori_loop(0, heads, one_head, 0)

    for n, x_ref in enumerate((x0_ref, x1_ref)):

        def gate(b, carry):
            g = jnp.dot(x_ref[b, pl.ds(at, rows), :], wg_ref[...], preferred_element_type=jnp.float32)
            g = g.astype(jnp.bfloat16).astype(jnp.float32)
            gated = (acc_s[n * half + b] * jax.nn.sigmoid(g)).astype(jnp.bfloat16)
            for t in range(rows // cols):
                out_s[blk, t, n * half + b] = gated[t * cols : (t + 1) * cols]
            return carry

        lax.fori_loop(0, half, gate, 0)

    def message(n, k, t):
        cd = blk * (rows // cols) + t
        dst = o_ref.at[core, pl.ds(pl.multiple_of(c * half, half), half)]
        src = out_s.at[blk, t, pl.ds(n * half, half)]
        cp = remote(src, dst, send.at[(cd * 2 + n)], recv.at[c * 2 + core], (chip * 2 + k, cd))
        return cp, src, dst, cd

    for t in range(rows // cols):
        for n in range(2):
            k = core if n == 0 else 1 - core
            cp, src, dst, cd = message(n, k, t)
            if n == 0:

                @pl.when(cd != c)
                def _():
                    cp.start()

                @pl.when(cd == c)
                def _():
                    pltpu.make_async_copy(src, dst, recv.at[c * 2 + core]).start()
            else:
                cp.start()

    @pl.when(blk == pl.num_programs(0) - 1)
    def _():
        for cs in range(8):
            for k in range(2):
                pltpu.make_async_copy(
                    out_s.at[0, 0, pl.ds(0, half)], o_ref.at[k, pl.ds(cs * half, half)], recv.at[cs * 2 + k]
                ).wait()
        for cd in range(8):
            for n in range(2):
                k = core if n == 0 else 1 - core
                cp = remote(
                    out_s.at[0, 0, pl.ds(0, half)], o_ref.at[core, pl.ds(0, half)],
                    send.at[cd * 2 + n], recv.at[0], (chip * 2 + 1 - core, cd),
                )
                if n == 0:

                    @pl.when(cd != c)
                    def _():
                        cp.wait_send()
                else:
                    cp.wait_send()


def attention(x0, x1, mask, tables, w, cols, home):
    half, length, channels = x0.shape
    seqs = 2 * half
    lanes = w[0].shape[1]
    heads = lanes // HEAD_DIM
    rows = length // 2
    scale = float(HEAD_DIM) ** -0.5
    mb = (1e9 / scale) * (mask.astype(jnp.float32) - 1.0)[:, None, :]
    hm = (jnp.arange(lanes)[None, None, :] // HEAD_DIM == jnp.arange(heads)[:, None, None]).astype(jnp.bfloat16)
    wq, wk, wv, wg = w
    whole = lambda a: pl.BlockSpec(a.shape, lambda i: (0,) * a.ndim, pipeline_mode=pl.Buffered(1))
    operands = (x0, x1, mb, hm, *tables, wq, wk.T, wv, wg)
    dma = pltpu.SemaphoreType.DMA
    return pl.pallas_call(
        attn_kernel,
        grid=(length // rows,),
        out_shape=jax.ShapeDtypeStruct((2, home, cols, lanes), jnp.bfloat16),
        in_specs=[whole(a) for a in operands],
        out_specs=pl.BlockSpec(memory_space=pl.ANY),
        scratch_shapes=[
            pltpu.VMEM((seqs, length, lanes), jnp.bfloat16),
            pltpu.VMEM((seqs, lanes, length), jnp.bfloat16),
            pltpu.VMEM((seqs, length, lanes), jnp.bfloat16),
            pltpu.VMEM((heads, rows, length), jnp.float32),
            pltpu.VMEM((seqs, rows, lanes), jnp.float32),
            pltpu.VMEM((2, rows // cols, seqs, cols, lanes), jnp.bfloat16),
            dma((16,)), dma((16,)),
        ],
        compiler_params=pltpu.CompilerParams(
            vmem_limit_bytes=56 << 20, collective_id=4, has_side_effects=True
        ),
        name="attn",
    )(*operands)


def opm_kernel(left_ref, lmask_ref, right_ref, rrow_ref, rcol_ref, pair_ref, gain_ref, w_ref, wd_ref, x_ref, mk_ref,
               out_ref, bias_ref, x_out, m_out, rt_s, wb_s, m_s, f_s, b_s, xsend, xrecv, msend, mrecv):
    step = pl.program_id(0)
    r, c = place()
    opm = w_ref.shape[0]
    per, cols = out_ref.shape[0], out_ref.shape[1]
    steps = f_s.shape[0]
    heads = wd_ref.shape[0]
    group = per // 4
    chunk = 4 * cols
    half = x_out.shape[0]
    width = cols * opm
    here = pl.ds(pl.multiple_of(c * cols, cols), cols)

    def moves(d):
        to = (r, (c + d) % 8)
        block = pl.ds(pl.multiple_of(to[1] * half, half), half)
        return (
            remote(x_ref.at[block], x_out.at[:, here], xsend.at[d], xrecv.at[d], to),
            remote(mk_ref.at[to[1]], m_out.at[c], msend.at[d], mrecv.at[d], to),
        )

    def kept():
        return (
            pltpu.make_async_copy(
                x_ref.at[pl.ds(pl.multiple_of(c * half, half), half)], x_out.at[:, here], xrecv.at[0]
            ),
            pltpu.make_async_copy(mk_ref.at[c], m_out.at[c], mrecv.at[0]),
        )

    @pl.when(step == 0)
    def _():
        barrier = pltpu.get_barrier_semaphore()
        for d in range(1, 8):
            signal(barrier, (r, (c + d) % 8))
        pl.semaphore_wait(barrier, 7)
        for d in range(1, 8):
            for cp in moves(d):
                cp.start()
        for cp in kept():
            cp.start()
        wb_s[...] = jnp.zeros_like(wb_s)

        def fill(b, carry):
            for i in range(4):
                wb_s[pl.ds(pl.multiple_of(b * 128 + i * 32, 32), 32), i * 128 : (i + 1) * 128] = w_ref[b]
            return carry

        lax.fori_loop(0, opm, fill, 0)

        def flip(n, carry):
            at = pl.multiple_of(n * chunk, chunk)
            rt_s[pl.ds(at, chunk), :] = right_ref[:, pl.ds(at, chunk)].T
            return carry

        lax.fori_loop(0, opm // 4, flip, 0)
        counts = lax.dot_general(
            right_ref[:, width:], lmask_ref[...], CONTRACT_FIRST, preferred_element_type=jnp.float32
        )[:cols, : steps * per]
        factor = rcol_ref[...] * rrow_ref[...] / (counts + 0.001)
        for n in range(steps):
            f_s[n] = factor[:, n * per : (n + 1) * per]

    def outer(n, carry):
        at = pl.multiple_of(n * chunk, chunk)
        m = jnp.dot(rt_s[pl.ds(at, chunk), :], left_ref[...], preferred_element_type=jnp.float32)
        m = m.astype(jnp.bfloat16)
        for bb in range(4):
            for g in range(group):
                m_s[g * cols : (g + 1) * cols, pl.ds(pl.multiple_of((n * 4 + bb) * 128, 128), 128)] = m[
                    bb * cols : (bb + 1) * cols, g * 128 : (g + 1) * 128
                ]
        return carry

    lax.fori_loop(0, opm // 4, outer, 0)
    factor = f_s[step]
    update = jnp.dot(m_s[...], wb_s[...], preferred_element_type=jnp.float32)
    for g in range(group):
        for ii in range(4):
            i = 4 * g + ii
            u = update[g * cols : (g + 1) * cols, ii * 128 : (ii + 1) * 128]
            x = pair_ref[i] + u * factor[:, i : i + 1]
            out_ref[i] = x
            x = (standardize_features(x) * gain_ref[...]).astype(jnp.bfloat16)
            b_s[:, i, :] = lax.dot_general(wd_ref[...], x, LAST_LAST, preferred_element_type=jnp.float32)
    bias_ref[...] = jnp.concatenate([b_s[h] for h in range(heads)], axis=1).astype(jnp.bfloat16)

    @pl.when(step == steps - 1)
    def _():
        for d in range(1, 8):
            for cp in moves(d):
                cp.wait()
        for cp in kept():
            cp.wait()


def opm(left, right, rrow, rcol, pair, gain, kron, logit, x, mk):
    rows, cols, channels = pair.shape
    seqs = left.shape[0]
    heads = logit.shape[1]
    per = 16
    steps = rows // per
    width = kron.shape[0] // 32
    rr = rrow.reshape(1, rows)
    rc = rcol.reshape(cols, 1)
    w = kron.reshape(width, width, channels).transpose(1, 0, 2)
    gain = gain.reshape(1, channels)
    wd = logit.T
    whole = lambda a: pl.BlockSpec(a.shape, lambda i: (0,) * a.ndim, pipeline_mode=pl.Buffered(1))
    hbm = pl.BlockSpec(memory_space=pl.ANY)
    dma = pltpu.SemaphoreType.DMA
    return pl.pallas_call(
        opm_kernel,
        grid=(steps,),
        out_shape=(
            jax.ShapeDtypeStruct(pair.shape, jnp.float32),
            jax.ShapeDtypeStruct((rows, heads * cols), jnp.bfloat16),
            jax.ShapeDtypeStruct((x.shape[0] // 8, 8 * cols, x.shape[2]), jnp.bfloat16),
            jax.ShapeDtypeStruct(mk.shape, mk.dtype),
        ),
        in_specs=[
            pl.BlockSpec((seqs, per * width), lambda i: (0, i)),
            pl.BlockSpec((seqs, 128), lambda i: (0, rows * width // 128)),
            whole(right), whole(rr), whole(rc),
            pl.BlockSpec((per, cols, channels), lambda i: (i, 0, 0)),
            whole(gain), whole(w), whole(wd), whole(x), whole(mk),
        ],
        out_specs=(
            pl.BlockSpec((per, cols, channels), lambda i: (i, 0, 0)),
            pl.BlockSpec((per, heads * cols), lambda i: (i, 0)),
            hbm, hbm,
        ),
        scratch_shapes=[
            pltpu.VMEM((cols * width, seqs), jnp.bfloat16),
            pltpu.VMEM((128 * width, 4 * channels), jnp.bfloat16),
            pltpu.VMEM((per // 4 * cols, 128 * width), jnp.bfloat16),
            pltpu.VMEM((steps, cols, per), jnp.float32),
            pltpu.VMEM((heads, per, cols), jnp.float32),
            dma((8,)), dma((8,)), dma((8,)), dma((8,)),
        ],
        compiler_params=pltpu.CompilerParams(
            vmem_limit_bytes=52 << 20, collective_id=2, has_side_effects=True
        ),
        name="opm",
    )(left, left, right, rr, rc, pair, gain, w, wd, x, mk)


def shards(
    aligned_family_embedding,
    aligned_slot_available,
    chain_site_available,
    duo_embedding,
    averaging_layernorm_stretch,
    lineup_layernorm_stretch,
    duo_layernorm_stretch,
    lefthand_linear_kernel,
    righthand_linear_kernel,
    kronecker_linear_kernel,
    duo_logit_kernel,
    asker_lookup_sigmoid_kernel,
    closing_linear_kernel,
):
    homolog_number, amino_position_number, discarded_carry = aligned_family_embedding.shape
    res_rows = duo_embedding.shape[0]
    opm_width = lefthand_linear_kernel.shape[1]
    head_count = duo_logit_kernel.shape[1]
    inner_width = closing_linear_kernel.shape[0]
    row_index = lax.axis_index("row")
    col_index = lax.axis_index("col")
    standardized_features = standardize_features(aligned_family_embedding.astype(jnp.float32))
    availability_real = aligned_slot_available.astype(jnp.float32)
    half_rows = res_rows
    opm_input = (standardized_features * averaging_layernorm_stretch).astype(jnp.bfloat16)
    left = jnp.einsum("src,ca->sra", opm_input, lefthand_linear_kernel, preferred_element_type=jnp.float32)
    left = (left * availability_real[:, :, None]).astype(jnp.bfloat16)
    left = left.reshape(homolog_number, 2, half_rows * opm_width).transpose(1, 0, 2)
    left_mask = availability_real.reshape(homolog_number, 2, half_rows).transpose(1, 0, 2)
    left_mask = jnp.pad(left_mask, ((0, 0), (0, 0), (0, 128 - half_rows))).astype(jnp.bfloat16)
    left = jnp.concatenate([left, left_mask], axis=2)
    right = jnp.einsum("src,ca->sar", opm_input, righthand_linear_kernel, preferred_element_type=jnp.float32)
    right = (right * availability_real[:, None, :]).astype(jnp.bfloat16)
    right_mask = jnp.pad(availability_real, ((0, 0), (0, 128 - amino_position_number))).astype(jnp.bfloat16)
    right = jnp.concatenate([right.reshape(homolog_number, -1), right_mask], axis=1)
    exponential_probabilities = (standardized_features * lineup_layernorm_stretch).astype(jnp.bfloat16)
    mask_out = jnp.pad(
        availability_real.reshape(8, homolog_number // 8, amino_position_number),
        ((0, 0), (0, 8 - homolog_number // 8), (0, 128 - amino_position_number)),
    )
    left_all, right_all = spread(left, right)
    residue_float = chain_site_available.astype(jnp.float32)
    residue_rows = lax.dynamic_slice_in_dim(residue_float, row_index * res_rows, res_rows)
    residue_cols = lax.dynamic_slice_in_dim(
        residue_float, col_index * amino_position_number, amino_position_number
    )
    duo_after_averaging, bias_tile, own_rows, own_mask = opm(
        left_all, right_all, residue_rows, residue_cols, duo_embedding,
        duo_layernorm_stretch, kronecker_linear_kernel, duo_logit_kernel, exponential_probabilities, mask_out,
    )
    *tables, other_rows, other_mask = share(bias_tile, own_rows, own_mask)
    masks = jnp.concatenate([own_mask, other_mask], axis=1).reshape(8, 2, 8, 128)
    masks = masks[:, :, : homolog_number // 8, :amino_position_number].transpose(1, 2, 0, 3)
    masks = masks.reshape(homolog_number // 4, 8 * amino_position_number)
    lanes = inner_width // 2
    by_half = asker_lookup_sigmoid_kernel.reshape(-1, 4, 2, lanes)
    mine = lax.dynamic_index_in_dim(by_half, row_index % 2, 2, keepdims=False)
    gated = attention(
        own_rows, other_rows, masks, tables, [mine[:, n] for n in range(4)], amino_position_number, homolog_number
    )
    closing = closing_linear_kernel.reshape(2, lanes, -1)
    summed_increment = jnp.einsum("hsqd,hdc->sqc", gated, closing, preferred_element_type=jnp.float32)
    refreshed_family_embedding = (
        aligned_family_embedding.astype(jnp.float32) + summed_increment
    ).astype(jnp.bfloat16)
    return (refreshed_family_embedding, duo_after_averaging)


def solution(mesh):
    placed = (
        P("row", "col", None),
        P("row", "col"),
        P(),
        P("row", "col", None),
        P(),
        P(),
        P(),
        P(),
        P(),
        P(),
        P(),
        P(),
        P(),
    )
    return jax.shard_map(
        shards,
        mesh=mesh,
        in_specs=placed,
        out_specs=(P("row", "col", None), P("row", "col", None)),
        check_vma=False,
    )
```

```python
import jax
import jax.numpy as jnp
from jax import lax
from jax.experimental import pallas as pl
from jax.experimental.pallas import tpu as pltpu
from jax.sharding import PartitionSpec as P

EPSILON = 1e-05
CONTRACT_FIRST = (((0,), (0,)), ((), ()))
LAST_LAST = (((1,), (1,)), ((), ()))
HEAD_DIM = 32


def standardize_features(values):
    average = jnp.mean(values, axis=-1, keepdims=True)
    centred = values - average
    variance = jnp.mean(centred * centred, axis=-1, keepdims=True)
    return centred * lax.rsqrt(variance + EPSILON)


MESH = pl.DeviceIdType.MESH


def place():
    r, c = lax.axis_index("row"), lax.axis_index("col")
    return r, c


def row_of(y, zh, core):
    return y * 4 + zh * 2 + core


def remote(src, dst, send, recv, device):
    return pltpu.make_async_remote_copy(
        src_ref=src, dst_ref=dst, send_sem=send, recv_sem=recv, device_id=device, device_id_type=MESH
    )


def signal(barrier, device):
    pl.semaphore_signal(barrier, inc=1, device_id=device, device_id_type=MESH)


def spread_kernel(left_ref, right_ref, left_out, right_out, lsend, lrecv, rsend, rrecv, fsend, frecv):
    r, c = place()
    chip, core = r // 2, r % 2
    seqs = right_ref.shape[0]
    here = pl.ds(pl.multiple_of(r * seqs, seqs), seqs)
    partner = (chip * 2 + 1 - core, c)
    mine = chip == c
    barrier = pltpu.get_barrier_semaphore()
    for d in range(1, 8):
        signal(barrier, ((r + 2 * d) % 16, c))
    signal(barrier, partner)
    for n in range(16):

        @pl.when(jnp.logical_not(jnp.logical_and(mine, r == n)))
        def _():
            signal(barrier, (n, chip))

    pl.semaphore_wait(barrier, 24 - mine.astype(jnp.int32))

    rights = [None]
    for d in range(1, 8):
        cp = remote(right_ref, right_out.at[here], rsend.at[d], rrecv.at[d], ((r + 2 * d) % 16, c))
        cp.start()
        rights.append(cp)
    own = pltpu.make_async_copy(right_ref, right_out.at[here], rrecv.at[0])
    own.start()
    forwards = [remote(right_ref, right_out.at[here], fsend.at[0], frecv.at[0], partner)]
    forwards[0].start()
    lefts = []
    for j in range(8):
        for h in range(2):
            cd = (c + j) % 8
            cp = remote(left_ref.at[h], left_out.at[here], lsend.at[2 * j + h], lrecv.at[r], (2 * c + h, cd))
            lefts.append((cp, h, j))
            if j == 0:
                own_left = jnp.logical_and(mine, core == h)

                @pl.when(jnp.logical_not(own_left))
                def _():
                    cp.start()

                @pl.when(own_left)
                def _():
                    pltpu.make_async_copy(left_ref.at[h], left_out.at[here], lrecv.at[r]).start()
            else:
                cp.start()
    for d in range(1, 8):
        rights[d].wait_recv()
        block = pl.ds(pl.multiple_of(((r + 16 - 2 * d) % 16) * seqs, seqs), seqs)
        fw = remote(right_out.at[block], right_out.at[block], fsend.at[d], frecv.at[d], partner)
        fw.start()
        forwards.append(fw)
    own.wait()
    for n in range(16):
        pltpu.make_async_copy(left_ref.at[0], left_out.at[pl.ds(n * seqs, seqs)], lrecv.at[n]).wait()
    for d in range(8):
        forwards[d].wait()
    for d in range(1, 8):
        rights[d].wait_send()
    for cp, h, j in lefts:
        if j == 0:

            @pl.when(jnp.logical_not(jnp.logical_and(mine, core == h)))
            def _():
                cp.wait_send()
        else:
            cp.wait_send()


def spread(left, right):
    seqs = right.shape[0]
    vmem = pl.BlockSpec(memory_space=pltpu.VMEM)
    hbm = pl.BlockSpec(memory_space=pl.ANY)
    dma = pltpu.SemaphoreType.DMA
    return pl.pallas_call(
        spread_kernel,
        out_shape=(
            jax.ShapeDtypeStruct((16 * seqs, left.shape[2]), jnp.bfloat16),
            jax.ShapeDtypeStruct((16 * seqs, right.shape[1]), jnp.bfloat16),
        ),
        in_specs=[vmem, vmem],
        out_specs=(hbm, hbm),
        scratch_shapes=[dma((16,)), dma((16,)), dma((8,)), dma((8,)), dma((8,)), dma((8,))],
        compiler_params=pltpu.CompilerParams(collective_id=1, has_side_effects=True),
        name="spread",
    )(left, right)


LOG2E = 1.4426950408889634


def attn_kernel(tile_ref, xin_ref, mask_ref, hm_ref, wq_ref, wk_ref, wv_ref, wg_ref, o_ref,
                block, ta, tb, tc, x_s, m_s, mb_s, q_s, kt_s, v_s, g_s, bf_s, acc_s, out_s,
                csem, csend, crecv, l1, s1, r1, s2, r2, s3, r3, send, recv):
    r, c = place()
    chip, core = r // 2, r % 2
    spot = {"x": c // 2, "y": r // 4, "z": (chip % 2) * 2 + c % 2}
    half, length = x_s.shape[1], x_s.shape[2]
    heads, rows = bf_s.shape[0], bf_s.shape[1]
    cols = length // 8
    sub = cols // 6
    scale = float(HEAD_DIM) ** -0.5
    partner = (chip * 2 + 1 - core, c)
    orders = ((ta, "xzy"), (tb, "yxz"), (tc, "zyx"))

    def peer(dim, d):
        to = dict(spot)
        to[dim] = (spot[dim] + d) % 4
        return (row_of(to["y"], to["z"] // 2, core), to["x"] * 2 + to["z"] % 2)

    barrier = pltpu.get_barrier_semaphore()
    signal(barrier, partner)
    for dim in "xyz":
        for d in range(1, 4):
            signal(barrier, peer(dim, d))
    for j in range(8):
        if j > 0:
            signal(barrier, (r, (c + j) % 8))
        signal(barrier, (partner[0], (c + j) % 8))

    trows, lanes = tile_ref.shape[0], tile_ref.shape[1] // 2
    here = pl.ds(pl.multiple_of(core * trows, trows), trows)
    give = tile_ref.at[:, pl.ds(pl.multiple_of((1 - core) * lanes, lanes), lanes)]
    keep = tile_ref.at[:, pl.ds(pl.multiple_of(core * lanes, lanes), lanes)]
    own = pltpu.make_async_copy(keep, block.at[here], csem.at[0])
    own.start()
    xl = pltpu.make_async_copy(xin_ref, x_s.at[0], csem.at[1])
    xl.start()
    ml = pltpu.make_async_copy(mask_ref, m_s.at[0], csem.at[2])
    ml.start()
    pl.semaphore_wait(barrier, 25)
    swap = remote(give, block.at[here], csend.at[0], crecv.at[0], partner)
    swap.start()
    xs = remote(xin_ref, x_s.at[1], csend.at[1], crecv.at[1], partner)
    ms = remote(mask_ref, m_s.at[1], csend.at[2], crecv.at[2], partner)
    own.wait()
    swap.wait_recv()

    def one(hf, o, d):
        out, dims = orders[o]
        slot = out.at[hf, spot[dims[2]], spot[dims[1]], spot[dims[0]]]
        piece = block.at[pl.ds(o * 2 * sub + hf * sub, sub)]
        if d == 0:
            return pltpu.make_async_copy(piece, slot, l1.at[hf * 3 + o])
        at = (hf * 3 + o) * 4 + d
        return remote(piece, slot, s1.at[at], r1.at[at], peer(dims[0], d))

    def two(hf, o, d):
        out, dims = orders[o]
        slot = out.at[hf, spot[dims[2]], spot[dims[1]]]
        at = (hf * 3 + o) * 4 + d
        return remote(slot, slot, s2.at[at], r2.at[at], peer(dims[1], d))

    def three(hf, o, e, d):
        out, dims = orders[o]
        slot = out.at[hf, spot[dims[2]], (spot[dims[1]] + 4 - e) % 4]
        at = (hf * 3 + o) * 16 + e * 4 + d
        return remote(slot, slot, s3.at[at], r3.at[at], peer(dims[2], d))

    def middle(hf):
        for o in range(3):
            for d in range(4):
                if d == 0:
                    one(hf, o, d).wait()
                else:
                    one(hf, o, d).wait_recv()
            for d in range(1, 4):
                two(hf, o, d).start()
            for d in range(1, 4):
                three(hf, o, 0, d).start()

    def last(hf):
        for e in range(1, 4):
            for o in range(3):
                two(hf, o, e).wait_recv()
                for d in range(1, 4):
                    three(hf, o, e, d).start()

    for hf in range(2):
        for o in range(3):
            for d in range(4):
                one(hf, o, d).start()
    xs.start()
    ms.start()

    def project(n):
        def body(b, carry):
            x = x_s[n, b]
            at = n * half + b
            p = jnp.dot(x, wq_ref[...], preferred_element_type=jnp.float32).astype(jnp.bfloat16)
            g = jnp.dot(x, wg_ref[...], preferred_element_type=jnp.float32).astype(jnp.bfloat16)
            for hf in range(2):
                q_s[at, hf] = jnp.concatenate(
                    [p[(2 * i + hf) * sub : (2 * i + hf + 1) * sub] for i in range(rows // sub)], axis=0
                )
                g_s[at, hf] = jnp.concatenate(
                    [g[(2 * i + hf) * sub : (2 * i + hf + 1) * sub] for i in range(rows // sub)], axis=0
                )
            v_s[at] = jnp.dot(x, wv_ref[...], preferred_element_type=jnp.float32).astype(jnp.bfloat16)
            kt_s[at] = lax.dot_general(
                wk_ref[...], x, LAST_LAST, preferred_element_type=jnp.float32
            ).astype(jnp.bfloat16)
            return carry

        lax.fori_loop(0, half, body, 0)
        for b in range(half):
            line = jnp.concatenate([m_s[n, cc, b : b + 1, :cols] for cc in range(8)], axis=1)
            mb_s[n * half + b] = (1e9 / scale) * (line - 1.0)

    middle(0)
    xl.wait()
    ml.wait()
    project(0)
    last(0)
    middle(1)
    xs.wait_recv()
    ms.wait_recv()
    project(1)

    def block_of_rows(hf, carry):
        for o in range(3):
            for e in range(4):
                for d in range(1, 4):
                    out, dims = orders[o]
                    at = (hf * 3 + o) * 16 + e * 4 + d
                    slot = out.at[hf, (spot[dims[2]] + 4 - d) % 4, (spot[dims[1]] + 4 - e) % 4]
                    remote(slot, slot, s3.at[at], r3.at[at], peer(dims[2], d)).wait_recv()

        def assemble(p, carry):
            y, zh = p // 2, p % 2
            for o in range(3):
                pieces = []
                for cc in range(8):
                    x, z = cc // 2, zh * 2 + cc % 2
                    if o == 0:
                        piece = ta[hf, y, z, x]
                    elif o == 1:
                        piece = tb[hf, z, x, y]
                    else:
                        piece = tc[hf, x, y, z]
                    pieces.append(piece.astype(jnp.float32) * (1.0 / scale))
                for h in range(heads):
                    bf_s[h, pl.ds(pl.multiple_of(p * 3 * sub + o * sub, sub), sub), :] = jnp.concatenate(
                        [piece[:, h * cols : (h + 1) * cols] for piece in pieces], axis=1
                    )
            return carry

        lax.fori_loop(0, 8, assemble, 0)

        def group(n, carry):
            def one_head(h, carry):
                @pl.when(jnp.logical_and(hf == 0, jnp.logical_and(n == 0, h == 1)))
                def _():
                    last(1)

                mine = hm_ref[h]
                mine_f = mine.astype(jnp.float32)
                other = (1.0 - mine_f).astype(jnp.bfloat16)
                for b in range(half):
                    at = n * half + b
                    q = q_s[at, hf] * mine
                    s = jnp.dot(q, kt_s[at], preferred_element_type=jnp.float32) + bf_s[h] + mb_s[at]
                    top = jnp.max(s, axis=1, keepdims=True)
                    p = jnp.exp2(((s - top) * (scale * LOG2E)).astype(jnp.bfloat16))
                    w = jnp.dot(p, v_s[at] * mine + other, preferred_element_type=jnp.float32)
                    mixed = w / pltpu.roll(w, HEAD_DIM, 1)
                    acc_s[b] = jnp.where(mine_f > 0.0, mixed, acc_s[b])
                return carry

            lax.fori_loop(0, heads, one_head, 0)

            def gate(b, carry):
                g = g_s[n * half + b, hf].astype(jnp.float32)
                gated = (acc_s[b] * jax.nn.sigmoid(g)).astype(jnp.bfloat16)
                for p in range(8):
                    for o in range(3):
                        at = (p * 3 + o) * sub
                        out_s[hf, n, p, b, o] = gated[at : at + sub]
                return carry

            lax.fori_loop(0, half, gate, 0)
            for j in range(8):
                p = (c + j) % 8
                src = out_s.at[hf, n, p]
                dst = o_ref.at[core, pl.ds(pl.multiple_of(c * half, half), half), :, hf]
                arrived = recv.at[hf * 16 + c * 2 + core]
                row = jnp.where(n == 0, r, partner[0])
                cp = remote(src, dst, send.at[(hf * 2 + n) * 8 + p], arrived, (row, p))
                if j == 0:

                    @pl.when(n > 0)
                    def _():
                        cp.start()

                    @pl.when(n == 0)
                    def _():
                        pltpu.make_async_copy(src, dst, arrived).start()
                else:
                    cp.start()
            return carry

        return lax.fori_loop(0, 2, group, carry)

    lax.fori_loop(0, 2, block_of_rows, 0)

    for hf in range(2):
        for cs in range(8):
            for k in range(2):
                pltpu.make_async_copy(
                    out_s.at[0, 0, 0], o_ref.at[k, pl.ds(cs * half, half), :, hf], recv.at[hf * 16 + cs * 2 + k]
                ).wait()
        for n in range(2):
            for j in range(8):
                p = (c + j) % 8
                if n == 0 and j == 0:
                    continue
                row = r if n == 0 else partner[0]
                remote(
                    out_s.at[hf, n, p], o_ref.at[core, pl.ds(pl.multiple_of(c * half, half), half), :, hf],
                    send.at[(hf * 2 + n) * 8 + p], recv.at[0], (row, p),
                ).wait_send()
        for o in range(3):
            for d in range(1, 4):
                one(hf, o, d).wait_send()
                two(hf, o, d).wait_send()
                for e in range(4):
                    three(hf, o, e, d).wait_send()
    swap.wait_send()
    xs.wait_send()
    ms.wait_send()


def attention(tile, x, mask, w, cols, home):
    half, length, channels = x.shape
    seqs = 2 * half
    lanes = w[0].shape[1]
    heads = lanes // HEAD_DIM
    rows = length // 2
    sub = cols // 6
    hm = (jnp.arange(lanes)[None, None, :] // HEAD_DIM == jnp.arange(heads)[:, None, None]).astype(jnp.bfloat16)
    wq, wk, wv, wg = w
    vmem = pl.BlockSpec(memory_space=pltpu.VMEM)
    hbm = pl.BlockSpec(memory_space=pl.ANY)
    dma = pltpu.SemaphoreType.DMA
    table = pltpu.VMEM((2, 4, 4, 4, sub, tile.shape[1] // 2), jnp.bfloat16)
    out = pl.pallas_call(
        attn_kernel,
        out_shape=jax.ShapeDtypeStruct((2, home, 3, 2, sub, lanes), jnp.bfloat16),
        in_specs=[vmem, hbm, vmem] + [vmem] * 5,
        out_specs=hbm,
        scratch_shapes=[
            pltpu.VMEM((2 * tile.shape[0], tile.shape[1] // 2), jnp.bfloat16),
            table, table, table,
            pltpu.VMEM((2,) + x.shape, jnp.bfloat16),
            pltpu.VMEM((2,) + mask.shape, jnp.float32),
            pltpu.VMEM((seqs, 1, length), jnp.float32),
            pltpu.VMEM((seqs, 2, rows, lanes), jnp.bfloat16),
            pltpu.VMEM((seqs, lanes, length), jnp.bfloat16),
            pltpu.VMEM((seqs, length, lanes), jnp.bfloat16),
            pltpu.VMEM((seqs, 2, rows, lanes), jnp.bfloat16),
            pltpu.VMEM((heads, rows, length), jnp.float32),
            pltpu.VMEM((half, rows, lanes), jnp.float32),
            pltpu.VMEM((2, 2, 8, half, 3, sub, lanes), jnp.bfloat16),
            dma((3,)), dma((3,)), dma((3,)), dma((6,)),
            dma((24,)), dma((24,)), dma((24,)), dma((24,)), dma((96,)), dma((96,)),
            dma((32,)), dma((32,)),
        ],
        compiler_params=pltpu.CompilerParams(
            vmem_limit_bytes=56 << 20, collective_id=3, has_side_effects=True
        ),
        name="attn",
    )(tile, x, mask, hm, wq, wk.T, wv, wg)
    return out.reshape(2, home, cols, lanes)


def opm_kernel(left_ref, lmask_ref, right_ref, rrow_ref, rcol_ref, pair_ref, gain_ref, w_ref, wd_ref, x_ref, mk_ref,
               out_ref, bias_ref, x_out, m_out, rt_s, wb_s, m_s, f_s, b_s, xsend, xrecv, msend, mrecv):
    step = pl.program_id(0)
    r, c = place()
    opm = w_ref.shape[0]
    per, cols = out_ref.shape[0], out_ref.shape[1]
    steps = f_s.shape[0]
    heads = wd_ref.shape[0]
    group = per // 4
    chunk = 4 * cols
    half = x_out.shape[0]
    width = cols * opm
    here = pl.ds(pl.multiple_of(c * cols, cols), cols)

    def moves(d):
        to = (r, (c + d) % 8)
        block = pl.ds(pl.multiple_of(to[1] * half, half), half)
        return (
            remote(x_ref.at[block], x_out.at[:, here], xsend.at[d], xrecv.at[d], to),
            remote(mk_ref.at[to[1]], m_out.at[c], msend.at[d], mrecv.at[d], to),
        )

    def kept():
        return (
            pltpu.make_async_copy(
                x_ref.at[pl.ds(pl.multiple_of(c * half, half), half)], x_out.at[:, here], xrecv.at[0]
            ),
            pltpu.make_async_copy(mk_ref.at[c], m_out.at[c], mrecv.at[0]),
        )

    @pl.when(step == 0)
    def _():
        barrier = pltpu.get_barrier_semaphore()
        for d in range(1, 8):
            signal(barrier, (r, (c + d) % 8))
        pl.semaphore_wait(barrier, 7)
        for d in range(1, 8):
            for cp in moves(d):
                cp.start()
        for cp in kept():
            cp.start()
        wb_s[...] = jnp.zeros_like(wb_s)

        def fill(b, carry):
            for i in range(4):
                wb_s[pl.ds(pl.multiple_of(b * 128 + i * 32, 32), 32), i * 128 : (i + 1) * 128] = w_ref[b]
            return carry

        lax.fori_loop(0, opm, fill, 0)

        def flip(n, carry):
            at = pl.multiple_of(n * chunk, chunk)
            rt_s[pl.ds(at, chunk), :] = right_ref[:, pl.ds(at, chunk)].T
            return carry

        lax.fori_loop(0, opm // 4, flip, 0)
        counts = lax.dot_general(
            right_ref[:, width:], lmask_ref[...], CONTRACT_FIRST, preferred_element_type=jnp.float32
        )[:cols, : steps * per]
        factor = rcol_ref[...] * rrow_ref[...] / (counts + 0.001)
        for n in range(steps):
            f_s[n] = factor[:, n * per : (n + 1) * per]

    def outer(n, carry):
        at = pl.multiple_of(n * chunk, chunk)
        m = jnp.dot(rt_s[pl.ds(at, chunk), :], left_ref[...], preferred_element_type=jnp.float32)
        m = m.astype(jnp.bfloat16)
        for bb in range(4):
            for g in range(group):
                m_s[g * cols : (g + 1) * cols, pl.ds(pl.multiple_of((n * 4 + bb) * 128, 128), 128)] = m[
                    bb * cols : (bb + 1) * cols, g * 128 : (g + 1) * 128
                ]
        return carry

    lax.fori_loop(0, opm // 4, outer, 0)
    factor = f_s[step]
    update = jnp.dot(m_s[...], wb_s[...], preferred_element_type=jnp.float32)
    for g in range(group):
        for ii in range(4):
            i = 4 * g + ii
            u = update[g * cols : (g + 1) * cols, ii * 128 : (ii + 1) * 128]
            x = pair_ref[i] + u * factor[:, i : i + 1]
            out_ref[i] = x
            x = (standardize_features(x) * gain_ref[...]).astype(jnp.bfloat16)
            b_s[:, i, :] = lax.dot_general(wd_ref[...], x, LAST_LAST, preferred_element_type=jnp.float32)
    bias_ref[...] = jnp.concatenate([b_s[h] for h in range(heads)], axis=1).astype(jnp.bfloat16)

    @pl.when(step == steps - 1)
    def _():
        for d in range(1, 8):
            for cp in moves(d):
                cp.wait()
        for cp in kept():
            cp.wait()


def opm(left, right, rrow, rcol, pair, gain, kron, logit, x, mk):
    rows, cols, channels = pair.shape
    seqs = left.shape[0]
    heads = logit.shape[1]
    per = 16
    steps = rows // per
    width = kron.shape[0] // 32
    rr = rrow.reshape(1, rows)
    rc = rcol.reshape(cols, 1)
    w = kron.reshape(width, width, channels).transpose(1, 0, 2)
    gain = gain.reshape(1, channels)
    wd = logit.T
    whole = lambda a: pl.BlockSpec(a.shape, lambda i: (0,) * a.ndim, pipeline_mode=pl.Buffered(1))
    hbm = pl.BlockSpec(memory_space=pl.ANY)
    dma = pltpu.SemaphoreType.DMA
    return pl.pallas_call(
        opm_kernel,
        grid=(steps,),
        out_shape=(
            jax.ShapeDtypeStruct(pair.shape, jnp.float32),
            jax.ShapeDtypeStruct((rows, heads * cols), jnp.bfloat16),
            jax.ShapeDtypeStruct((x.shape[0] // 8, 8 * cols, x.shape[2]), jnp.bfloat16),
            jax.ShapeDtypeStruct(mk.shape, mk.dtype),
        ),
        in_specs=[
            pl.BlockSpec((seqs, per * width), lambda i: (0, i)),
            pl.BlockSpec((seqs, 128), lambda i: (0, rows * width // 128)),
            whole(right), whole(rr), whole(rc),
            pl.BlockSpec((per, cols, channels), lambda i: (i, 0, 0)),
            whole(gain), whole(w), whole(wd), whole(x), whole(mk),
        ],
        out_specs=(
            pl.BlockSpec((per, cols, channels), lambda i: (i, 0, 0)),
            pl.BlockSpec((per, heads * cols), lambda i: (i, 0)),
            hbm, hbm,
        ),
        scratch_shapes=[
            pltpu.VMEM((cols * width, seqs), jnp.bfloat16),
            pltpu.VMEM((128 * width, 4 * channels), jnp.bfloat16),
            pltpu.VMEM((per // 4 * cols, 128 * width), jnp.bfloat16),
            pltpu.VMEM((steps, cols, per), jnp.float32),
            pltpu.VMEM((heads, per, cols), jnp.float32),
            dma((8,)), dma((8,)), dma((8,)), dma((8,)),
        ],
        compiler_params=pltpu.CompilerParams(
            vmem_limit_bytes=52 << 20, collective_id=2, has_side_effects=True
        ),
        name="opm",
    )(left, left, right, rr, rc, pair, gain, w, wd, x, mk)


def shards(
    aligned_family_embedding,
    aligned_slot_available,
    chain_site_available,
    duo_embedding,
    averaging_layernorm_stretch,
    lineup_layernorm_stretch,
    duo_layernorm_stretch,
    lefthand_linear_kernel,
    righthand_linear_kernel,
    kronecker_linear_kernel,
    duo_logit_kernel,
    asker_lookup_sigmoid_kernel,
    closing_linear_kernel,
):
    homolog_number, amino_position_number, discarded_carry = aligned_family_embedding.shape
    res_rows = duo_embedding.shape[0]
    opm_width = lefthand_linear_kernel.shape[1]
    head_count = duo_logit_kernel.shape[1]
    inner_width = closing_linear_kernel.shape[0]
    row_index = lax.axis_index("row")
    col_index = lax.axis_index("col")
    standardized_features = standardize_features(aligned_family_embedding.astype(jnp.float32))
    availability_real = aligned_slot_available.astype(jnp.float32)
    half_rows = res_rows
    opm_input = (standardized_features * averaging_layernorm_stretch).astype(jnp.bfloat16)
    left = jnp.einsum("src,ca->sra", opm_input, lefthand_linear_kernel, preferred_element_type=jnp.float32)
    left = (left * availability_real[:, :, None]).astype(jnp.bfloat16)
    left = left.reshape(homolog_number, 2, half_rows * opm_width).transpose(1, 0, 2)
    left_mask = availability_real.reshape(homolog_number, 2, half_rows).transpose(1, 0, 2)
    left_mask = jnp.pad(left_mask, ((0, 0), (0, 0), (0, 128 - half_rows))).astype(jnp.bfloat16)
    left = jnp.concatenate([left, left_mask], axis=2)
    right = jnp.einsum("src,ca->sar", opm_input, righthand_linear_kernel, preferred_element_type=jnp.float32)
    right = (right * availability_real[:, None, :]).astype(jnp.bfloat16)
    right_mask = jnp.pad(availability_real, ((0, 0), (0, 128 - amino_position_number))).astype(jnp.bfloat16)
    right = jnp.concatenate([right.reshape(homolog_number, -1), right_mask], axis=1)
    exponential_probabilities = (standardized_features * lineup_layernorm_stretch).astype(jnp.bfloat16)
    mask_out = jnp.pad(
        availability_real.reshape(8, homolog_number // 8, amino_position_number),
        ((0, 0), (0, 8 - homolog_number // 8), (0, 128 - amino_position_number)),
    )
    left_all, right_all = spread(left, right)
    residue_float = chain_site_available.astype(jnp.float32)
    residue_rows = lax.dynamic_slice_in_dim(residue_float, row_index * res_rows, res_rows)
    residue_cols = lax.dynamic_slice_in_dim(
        residue_float, col_index * amino_position_number, amino_position_number
    )
    duo_after_averaging, bias_tile, own_rows, own_mask = opm(
        left_all, right_all, residue_rows, residue_cols, duo_embedding,
        duo_layernorm_stretch, kronecker_linear_kernel, duo_logit_kernel, exponential_probabilities, mask_out,
    )
    lanes = inner_width // 2
    by_half = asker_lookup_sigmoid_kernel.reshape(-1, 4, 2, lanes)
    mine = lax.dynamic_index_in_dim(by_half, row_index % 2, 2, keepdims=False)
    gated = attention(
        bias_tile, own_rows, own_mask, [mine[:, n] for n in range(4)], amino_position_number, homolog_number
    )
    closing = closing_linear_kernel.reshape(2, lanes, -1)
    summed_increment = jnp.einsum("hsqd,hdc->sqc", gated, closing, preferred_element_type=jnp.float32)
    refreshed_family_embedding = (
        aligned_family_embedding.astype(jnp.float32) + summed_increment
    ).astype(jnp.bfloat16)
    return (refreshed_family_embedding, duo_after_averaging)


def solution(mesh):
    placed = (
        P("row", "col", None),
        P("row", "col"),
        P(),
        P("row", "col", None),
        P(),
        P(),
        P(),
        P(),
        P(),
        P(),
        P(),
        P(),
        P(),
    )
    return jax.shard_map(
        shards,
        mesh=mesh,
        in_specs=placed,
        out_specs=(P("row", "col", None), P("row", "col", None)),
        check_vma=False,
    )
```

```python
import jax
import jax.numpy as jnp
from jax import lax
from jax.experimental import pallas as pl
from jax.experimental.pallas import tpu as pltpu
from jax.sharding import PartitionSpec as P

EPSILON = 1e-05
CONTRACT_FIRST = (((0,), (0,)), ((), ()))
LAST_LAST = (((1,), (1,)), ((), ()))
HEAD_DIM = 32


def standardize_features(values):
    average = jnp.mean(values, axis=-1, keepdims=True)
    centred = values - average
    variance = jnp.mean(centred * centred, axis=-1, keepdims=True)
    return centred * lax.rsqrt(variance + EPSILON)


MESH = pl.DeviceIdType.MESH


def place():
    r, c = lax.axis_index("row"), lax.axis_index("col")
    return r, c


def row_of(y, zh, core):
    return y * 4 + zh * 2 + core


def remote(src, dst, send, recv, device):
    return pltpu.make_async_remote_copy(
        src_ref=src, dst_ref=dst, send_sem=send, recv_sem=recv, device_id=device, device_id_type=MESH
    )


def signal(barrier, device):
    pl.semaphore_signal(barrier, inc=1, device_id=device, device_id_type=MESH)


def spread_kernel(left_ref, right_ref, left_out, right_out, lsend, lrecv, gsend, zsend, zrecv, ysend, yrecv, fsend,
                  frecv, own_sem):
    r, c = place()
    chip, core = r // 2, r % 2
    y, zh, x, zl = r // 4, chip % 2, c // 2, c % 2
    seqs = right_ref.shape[0]

    def rows(n):
        return pl.ds(pl.multiple_of(n * seqs, seqs), seqs)

    here = rows(r)
    partner = (chip * 2 + 1 - core, c)
    across = (row_of(y, 1 - zh, core), c)
    aside = (r, x * 2 + 1 - zl)
    mine = jnp.logical_and(chip == c, zh == zl)

    def own_left(h, j):
        return jnp.logical_and(mine, core == h) if j == 0 else False

    def unless(cond, f):
        if cond is False:
            f()
        else:
            pl.when(jnp.logical_not(cond))(f)

    barrier = pltpu.get_barrier_semaphore()
    signal(barrier, partner)
    signal(barrier, across)
    signal(barrier, aside)
    for d in range(1, 4):
        signal(barrier, (row_of((y + d) % 4, zh, core), c))
    for ys in range(4):
        for k in range(2):
            source = row_of(ys, zl, k)
            unless(jnp.logical_and(mine, r == source), lambda: signal(barrier, (source, chip)))
    pl.semaphore_wait(barrier, 14 - mine.astype(jnp.int32))

    over = remote(right_ref, right_out.at[here], zsend.at[0], zrecv.at[0], across)
    over.start()
    sends = [over]
    lefts = []
    for j in range(4):
        for h in range(2):
            to = (2 * c + h, ((x + j) % 4) * 2 + zh)
            cp = remote(left_ref.at[h], left_out.at[here], lsend.at[2 * j + h], lrecv.at[r], to)
            lefts.append((cp, h, j))
            unless(own_left(h, j), cp.start)
            if j == 0:

                @pl.when(own_left(h, j))
                def _():
                    pltpu.make_async_copy(left_ref.at[h], left_out.at[here], lrecv.at[r]).start()

    def along(n, d):
        block = rows(row_of(y, (zh + n) % 2, core))
        src = right_ref if n == 0 else right_out.at[block]
        return remote(src, right_out.at[block], ysend.at[n * 4 + d], yrecv.at[n * 4 + d], (row_of((y + d) % 4, zh, core), c))

    def forward(n, d):
        block = rows(row_of((y + 4 - d) % 4, (zh + n) % 2, core))
        src = right_ref if n == 0 and d == 0 else right_out.at[block]
        return remote(src, right_out.at[block], fsend.at[n * 4 + d], frecv.at[n * 4 + d], partner)

    for d in (1, 3, 2):
        along(0, d).start()
    own = pltpu.make_async_copy(right_ref, right_out.at[here], own_sem.at[0])
    own.start()
    forward(0, 0).start()
    over.wait_recv()
    for d in (1, 3, 2):
        along(1, d).start()
    forward(1, 0).start()

    def relay(d, k):
        source = row_of((y + 4 - d) % 4, zl, k)
        block = left_out.at[rows(source)]
        return block, source, remote(block, block, gsend.at[d * 2 + k], lrecv.at[source], aside)

    for d in (0, 1, 3, 2):
        for k in range(2):
            block, source, cp = relay(d, k)
            pltpu.make_async_copy(left_ref.at[0], block, lrecv.at[source]).wait()
            cp.start()
        if d > 0:
            along(0, d).wait_recv()
            forward(0, d).start()
    for d in (1, 3, 2):
        along(1, d).wait_recv()
        forward(1, d).start()
    for ys in range(4):
        for k in range(2):
            source = row_of(ys, 1 - zl, k)
            pltpu.make_async_copy(left_ref.at[0], left_out.at[rows(source)], lrecv.at[source]).wait()
    own.wait()
    for n in range(2):
        for d in range(4):
            forward(n, d).wait()
            if d > 0:
                along(n, d).wait_send()
    over.wait_send()
    for cp, h, j in lefts:
        unless(own_left(h, j), cp.wait_send)
    for d in range(4):
        for k in range(2):
            relay(d, k)[2].wait_send()


def spread(left, right):
    seqs = right.shape[0]
    vmem = pl.BlockSpec(memory_space=pltpu.VMEM)
    hbm = pl.BlockSpec(memory_space=pl.ANY)
    dma = pltpu.SemaphoreType.DMA
    return pl.pallas_call(
        spread_kernel,
        out_shape=(
            jax.ShapeDtypeStruct((16 * seqs, left.shape[2]), jnp.bfloat16),
            jax.ShapeDtypeStruct((16 * seqs, right.shape[1]), jnp.bfloat16),
        ),
        in_specs=[vmem, vmem],
        out_specs=(hbm, hbm),
        scratch_shapes=[
            dma((8,)), dma((16,)), dma((8,)), dma((1,)), dma((1,)), dma((8,)), dma((8,)), dma((8,)), dma((8,)), dma((1,))
        ],
        compiler_params=pltpu.CompilerParams(collective_id=1, has_side_effects=True),
        name="spread",
    )(left, right)


LOG2E = 1.4426950408889634


def attn_kernel(tile_ref, xin_ref, mask_ref, gain_ref, w_ref, o_ref, w_s, block, ta, tb, tc, x_s, m_s, mb_s, q_s, kt_s, v_s, g_s, bf_s, acc_s, out_s,
                csem, csend, crecv, l1, s1, r1, s2, r2, s3, r3, send, recv):
    r, c = place()
    chip, core = r // 2, r % 2
    spot = {"x": c // 2, "y": r // 4, "z": (chip % 2) * 2 + c % 2}
    half, length = x_s.shape[1], x_s.shape[2]
    heads, rows = bf_s.shape[0], bf_s.shape[1]
    cols = length // 8
    sub = cols // 6
    scale = float(HEAD_DIM) ** -0.5
    partner = (chip * 2 + 1 - core, c)
    orders = ((ta, "xzy"), (tb, "yxz"), (tc, "zyx"))

    def peer(dim, d):
        to = dict(spot)
        to[dim] = (spot[dim] + d) % 4
        return (row_of(to["y"], to["z"] // 2, core), to["x"] * 2 + to["z"] % 2)

    barrier = pltpu.get_barrier_semaphore()
    signal(barrier, partner)
    for dim in "xyz":
        for d in range(1, 4):
            signal(barrier, peer(dim, d))
    for j in range(8):
        if j > 0:
            signal(barrier, (r, (c + j) % 8))
        signal(barrier, (partner[0], (c + j) % 8))

    trows, lanes = tile_ref.shape[0], tile_ref.shape[1] // 2
    here = pl.ds(pl.multiple_of(core * trows, trows), trows)
    give = tile_ref.at[:, pl.ds(pl.multiple_of((1 - core) * lanes, lanes), lanes)]
    keep = tile_ref.at[:, pl.ds(pl.multiple_of(core * lanes, lanes), lanes)]
    own = pltpu.make_async_copy(keep, block.at[here], csem.at[0])
    own.start()
    xl = pltpu.make_async_copy(xin_ref, x_s.at[0], csem.at[1])
    xl.start()
    ml = pltpu.make_async_copy(mask_ref, m_s.at[0], csem.at[2])
    ml.start()
    pl.semaphore_wait(barrier, 25)
    swap = remote(give, block.at[here], csend.at[0], crecv.at[0], partner)
    swap.start()
    xs = remote(xin_ref, x_s.at[1], csend.at[1], crecv.at[1], partner)
    ms = remote(mask_ref, m_s.at[1], csend.at[2], crecv.at[2], partner)
    own.wait()
    swap.wait_recv()

    def one(hf, o, d):
        out, dims = orders[o]
        slot = out.at[hf, spot[dims[2]], spot[dims[1]], spot[dims[0]]]
        piece = block.at[pl.ds(o * 2 * sub + hf * sub, sub)]
        if d == 0:
            return pltpu.make_async_copy(piece, slot, l1.at[hf * 3 + o])
        at = (hf * 3 + o) * 4 + d
        return remote(piece, slot, s1.at[at], r1.at[at], peer(dims[0], d))

    def two(hf, o, d):
        out, dims = orders[o]
        slot = out.at[hf, spot[dims[2]], spot[dims[1]]]
        at = (hf * 3 + o) * 4 + d
        return remote(slot, slot, s2.at[at], r2.at[at], peer(dims[1], d))

    def three(hf, o, e, d):
        out, dims = orders[o]
        slot = out.at[hf, spot[dims[2]], (spot[dims[1]] + 4 - e) % 4]
        at = (hf * 3 + o) * 16 + e * 4 + d
        return remote(slot, slot, s3.at[at], r3.at[at], peer(dims[2], d))

    def middle(hf):
        for o in range(3):
            for d in range(4):
                if d == 0:
                    one(hf, o, d).wait()
                else:
                    one(hf, o, d).wait_recv()
            for d in range(1, 4):
                two(hf, o, d).start()
            for d in range(1, 4):
                three(hf, o, 0, d).start()

    def last(hf):
        for e in range(1, 4):
            for o in range(3):
                two(hf, o, e).wait_recv()
                for d in range(1, 4):
                    three(hf, o, e, d).start()

    for hf in range(2):
        for o in range(3):
            for d in range(4):
                one(hf, o, d).start()
    xs.start()
    ms.start()

    width = w_ref.shape[1] // 4
    part = w_s.shape[1] // 4
    for n in range(4):
        w_s[:, n * part : (n + 1) * part] = w_ref[:, pl.ds(pl.multiple_of(n * width + core * part, part), part)]

    def project(n):
        def body(b, carry):
            x = standardize_features(x_s[n, b].astype(jnp.float32))
            x = (x * gain_ref[...]).astype(jnp.bfloat16)
            at = n * half + b
            both = jnp.dot(x, w_s[...], preferred_element_type=jnp.float32).astype(jnp.bfloat16)
            p, k, v, g = [both[:, i * part : (i + 1) * part] for i in range(4)]
            for hf in range(2):
                q_s[at, hf] = jnp.concatenate(
                    [p[(2 * i + hf) * sub : (2 * i + hf + 1) * sub] for i in range(rows // sub)], axis=0
                )
                g_s[at, hf] = jnp.concatenate(
                    [g[(2 * i + hf) * sub : (2 * i + hf + 1) * sub] for i in range(rows // sub)], axis=0
                )
            v_s[at] = v
            kt_s[at] = k.T
            return carry

        lax.fori_loop(0, half, body, 0)
        for b in range(half):
            line = jnp.concatenate([m_s[n, cc, b : b + 1, :cols] for cc in range(8)], axis=1)
            mb_s[n * half + b] = (1e9 / scale) * (line - 1.0)

    middle(0)
    xl.wait()
    ml.wait()
    project(0)
    last(0)
    middle(1)
    xs.wait_recv()
    ms.wait_recv()
    project(1)

    def block_of_rows(hf, carry):
        for o in range(3):
            for e in range(4):
                for d in range(1, 4):
                    out, dims = orders[o]
                    at = (hf * 3 + o) * 16 + e * 4 + d
                    slot = out.at[hf, (spot[dims[2]] + 4 - d) % 4, (spot[dims[1]] + 4 - e) % 4]
                    remote(slot, slot, s3.at[at], r3.at[at], peer(dims[2], d)).wait_recv()

        def assemble(p, carry):
            y, zh = p // 2, p % 2
            for o in range(3):
                pieces = []
                for cc in range(8):
                    x, z = cc // 2, zh * 2 + cc % 2
                    if o == 0:
                        piece = ta[hf, y, z, x]
                    elif o == 1:
                        piece = tb[hf, z, x, y]
                    else:
                        piece = tc[hf, x, y, z]
                    pieces.append(piece)
                for h in range(heads):
                    line = jnp.concatenate([piece[:, h * cols : (h + 1) * cols] for piece in pieces], axis=1)
                    bf_s[h, pl.ds(pl.multiple_of(p * 3 * sub + o * sub, sub), sub), :] = line.astype(jnp.float32) * (
                        1.0 / scale
                    )
            return carry

        lax.fori_loop(0, 8, assemble, 0)

        def group(n, carry):
            def one_head(h, carry):
                @pl.when(jnp.logical_and(hf == 0, jnp.logical_and(n == 0, h == 1)))
                def _():
                    last(1)

                head = lax.broadcasted_iota(jnp.int32, (1, part), 1) // HEAD_DIM
                mine_f = jnp.where(head == h, 1.0, 0.0)
                mine = mine_f.astype(jnp.bfloat16)
                other = (1.0 - mine_f).astype(jnp.bfloat16)
                for b in range(half):
                    at = n * half + b
                    q = q_s[at, hf] * mine
                    s = jnp.dot(q, kt_s[at], preferred_element_type=jnp.float32) + bf_s[h] + mb_s[at]
                    top = jnp.max(s, axis=1, keepdims=True)
                    p = jnp.exp2(((s - top) * (scale * LOG2E)).astype(jnp.bfloat16))
                    w = jnp.dot(p, v_s[at] * mine + other, preferred_element_type=jnp.float32)
                    mixed = w / pltpu.roll(w, HEAD_DIM, 1)
                    acc_s[b] = jnp.where(mine_f > 0.0, mixed, acc_s[b])
                return carry

            lax.fori_loop(0, heads, one_head, 0)

            def gate(b, carry):
                g = g_s[n * half + b, hf].astype(jnp.float32)
                gated = (acc_s[b] * jax.nn.sigmoid(g)).astype(jnp.bfloat16)
                for p in range(8):
                    for o in range(3):
                        at = (p * 3 + o) * sub
                        out_s[hf, n, p, b, o] = gated[at : at + sub]
                return carry

            lax.fori_loop(0, half, gate, 0)
            for j in range(8):
                p = (c + j) % 8
                src = out_s.at[hf, n, p]
                dst = o_ref.at[core, pl.ds(pl.multiple_of(c * half, half), half), :, hf]
                arrived = recv.at[hf * 16 + c * 2 + core]
                row = jnp.where(n == 0, r, partner[0])
                cp = remote(src, dst, send.at[(hf * 2 + n) * 8 + p], arrived, (row, p))
                if j == 0:

                    @pl.when(n > 0)
                    def _():
                        cp.start()

                    @pl.when(n == 0)
                    def _():
                        pltpu.make_async_copy(src, dst, arrived).start()
                else:
                    cp.start()
            return carry

        return lax.fori_loop(0, 2, group, carry)

    lax.fori_loop(0, 2, block_of_rows, 0)

    for hf in range(2):
        for cs in range(8):
            for k in range(2):
                pltpu.make_async_copy(
                    out_s.at[0, 0, 0], o_ref.at[k, pl.ds(cs * half, half), :, hf], recv.at[hf * 16 + cs * 2 + k]
                ).wait()
        for n in range(2):
            for j in range(8):
                p = (c + j) % 8
                if n == 0 and j == 0:
                    continue
                row = r if n == 0 else partner[0]
                remote(
                    out_s.at[hf, n, p], o_ref.at[core, pl.ds(pl.multiple_of(c * half, half), half), :, hf],
                    send.at[(hf * 2 + n) * 8 + p], recv.at[0], (row, p),
                ).wait_send()
        for o in range(3):
            for d in range(1, 4):
                one(hf, o, d).wait_send()
                two(hf, o, d).wait_send()
                for e in range(4):
                    three(hf, o, e, d).wait_send()
    swap.wait_send()
    xs.wait_send()
    ms.wait_send()


def attention(tile, x, mask, gain, w, cols, home):
    half, length, channels = x.shape
    seqs = 2 * half
    lanes = w.shape[1] // 8
    heads = lanes // HEAD_DIM
    rows = length // 2
    sub = cols // 6
    vmem = pl.BlockSpec(memory_space=pltpu.VMEM)
    hbm = pl.BlockSpec(memory_space=pl.ANY)
    dma = pltpu.SemaphoreType.DMA
    table = pltpu.VMEM((2, 4, 4, 4, sub, tile.shape[1] // 2), jnp.bfloat16)
    out = pl.pallas_call(
        attn_kernel,
        out_shape=jax.ShapeDtypeStruct((2, home, 3, 2, sub, lanes), jnp.bfloat16),
        in_specs=[vmem, hbm, vmem, vmem, vmem],
        out_specs=hbm,
        scratch_shapes=[
            pltpu.VMEM((channels, 4 * lanes), jnp.bfloat16),
            pltpu.VMEM((2 * tile.shape[0], tile.shape[1] // 2), jnp.bfloat16),
            table, table, table,
            pltpu.VMEM((2,) + x.shape, jnp.bfloat16),
            pltpu.VMEM((2,) + mask.shape, jnp.float32),
            pltpu.VMEM((seqs, 1, length), jnp.float32),
            pltpu.VMEM((seqs, 2, rows, lanes), jnp.bfloat16),
            pltpu.VMEM((seqs, lanes, length), jnp.bfloat16),
            pltpu.VMEM((seqs, length, lanes), jnp.bfloat16),
            pltpu.VMEM((seqs, 2, rows, lanes), jnp.bfloat16),
            pltpu.VMEM((heads, rows, length), jnp.float32),
            pltpu.VMEM((half, rows, lanes), jnp.float32),
            pltpu.VMEM((2, 2, 8, half, 3, sub, lanes), jnp.bfloat16),
            dma((3,)), dma((3,)), dma((3,)), dma((6,)),
            dma((24,)), dma((24,)), dma((24,)), dma((24,)), dma((96,)), dma((96,)),
            dma((32,)), dma((32,)),
        ],
        compiler_params=pltpu.CompilerParams(
            vmem_limit_bytes=56 << 20, collective_id=3, has_side_effects=True
        ),
        name="attn",
    )(tile, x, mask, gain.reshape(1, channels), w)
    return out.reshape(2, home, cols, lanes)


def opm_kernel(left_ref, lmask_ref, right_ref, rrow_ref, rcol_ref, pair_ref, gain_ref, w_ref, wd_ref, x_ref, mk_ref,
               out_ref, bias_ref, x_out, m_out, rt_s, wb_s, m_s, f_s, b_s, xsend, xrecv, msend, mrecv):
    step = pl.program_id(0)
    r, c = place()
    opm = w_ref.shape[0]
    per, cols = out_ref.shape[0], out_ref.shape[1]
    steps = f_s.shape[0]
    heads = wd_ref.shape[0]
    group = per // 4
    chunk = 4 * cols
    half = x_out.shape[0]
    width = cols * opm
    here = pl.ds(pl.multiple_of(c * cols, cols), cols)

    def moves(d):
        to = (r, (c + d) % 8)
        block = pl.ds(pl.multiple_of(to[1] * half, half), half)
        return (
            remote(x_ref.at[block], x_out.at[:, here], xsend.at[d], xrecv.at[d], to),
            remote(mk_ref.at[to[1]], m_out.at[c], msend.at[d], mrecv.at[d], to),
        )

    def kept():
        return (
            pltpu.make_async_copy(
                x_ref.at[pl.ds(pl.multiple_of(c * half, half), half)], x_out.at[:, here], xrecv.at[0]
            ),
            pltpu.make_async_copy(mk_ref.at[c], m_out.at[c], mrecv.at[0]),
        )

    @pl.when(step == 0)
    def _():
        barrier = pltpu.get_barrier_semaphore()
        for d in range(1, 8):
            signal(barrier, (r, (c + d) % 8))
        pl.semaphore_wait(barrier, 7)
        for d in range(1, 8):
            for cp in moves(d):
                cp.start()
        for cp in kept():
            cp.start()
        wb_s[...] = jnp.zeros_like(wb_s)

        def fill(b, carry):
            for i in range(2):
                wb_s[pl.ds(pl.multiple_of(b * 64 + i * 32, 32), 32), i * 128 : (i + 1) * 128] = w_ref[b]
            return carry

        lax.fori_loop(0, opm, fill, 0)

        def flip(n, carry):
            at = pl.multiple_of(n * chunk, chunk)
            rt_s[pl.ds(at, chunk), :] = right_ref[:, pl.ds(at, chunk)].T
            return carry

        lax.fori_loop(0, opm // 4, flip, 0)
        counts = lax.dot_general(
            right_ref[:, width:], lmask_ref[...], CONTRACT_FIRST, preferred_element_type=jnp.float32
        )[:cols, : steps * per]
        factor = rcol_ref[...] * rrow_ref[...] / (counts + 0.001)
        for n in range(steps):
            f_s[n] = factor[:, n * per : (n + 1) * per]

    def outer(n, carry):
        at = pl.multiple_of(n * chunk, chunk)
        m = jnp.dot(rt_s[pl.ds(at, chunk), :], left_ref[...], preferred_element_type=jnp.float32)
        low = lax.broadcasted_iota(jnp.int32, (1, 128), 1) < 64
        for bb in range(2):
            lanes = pl.ds(pl.multiple_of((n * 2 + bb) * 128, 128), 128)
            for g in range(group):
                m0, m1 = [
                    m[(2 * bb + k) * cols : (2 * bb + k + 1) * cols, g * 128 : (g + 1) * 128] for k in range(2)
                ]
                one = jnp.where(low, m0, pltpu.roll(m1, 64, 1)).astype(jnp.bfloat16)
                two = jnp.where(low, pltpu.roll(m0, 64, 1), m1).astype(jnp.bfloat16)
                m_s[(2 * g) * cols : (2 * g + 1) * cols, lanes] = one
                m_s[(2 * g + 1) * cols : (2 * g + 2) * cols, lanes] = two
        return carry

    lax.fori_loop(0, opm // 4, outer, 0)
    factor = f_s[step]
    update = jnp.dot(m_s[...], wb_s[...], preferred_element_type=jnp.float32)
    for g in range(2 * group):
        for ii in range(2):
            i = 2 * g + ii
            u = update[g * cols : (g + 1) * cols, ii * 128 : (ii + 1) * 128]
            x = pair_ref[i] + u * factor[:, i : i + 1]
            out_ref[i] = x
            x = (standardize_features(x) * gain_ref[...]).astype(jnp.bfloat16)
            b_s[:, i, :] = lax.dot_general(wd_ref[...], x, LAST_LAST, preferred_element_type=jnp.float32)
    bias_ref[...] = jnp.concatenate([b_s[h] for h in range(heads)], axis=1).astype(jnp.bfloat16)

    @pl.when(step == steps - 1)
    def _():
        for d in range(1, 8):
            for cp in moves(d):
                cp.wait()
        for cp in kept():
            cp.wait()


def opm(left, right, rrow, rcol, pair, gain, kron, logit, x, mk):
    rows, cols, channels = pair.shape
    seqs = left.shape[0]
    heads = logit.shape[1]
    per = 16
    steps = rows // per
    width = kron.shape[0] // 32
    rr = rrow.reshape(1, rows)
    rc = rcol.reshape(cols, 1)
    w = kron.reshape(width, width, channels).transpose(1, 0, 2)
    gain = gain.reshape(1, channels)
    wd = logit.T
    whole = lambda a: pl.BlockSpec(a.shape, lambda i: (0,) * a.ndim, pipeline_mode=pl.Buffered(1))
    hbm = pl.BlockSpec(memory_space=pl.ANY)
    dma = pltpu.SemaphoreType.DMA
    return pl.pallas_call(
        opm_kernel,
        grid=(steps,),
        out_shape=(
            jax.ShapeDtypeStruct(pair.shape, jnp.float32),
            jax.ShapeDtypeStruct((rows, heads * cols), jnp.bfloat16),
            jax.ShapeDtypeStruct((x.shape[0] // 8, 8 * cols, x.shape[2]), jnp.bfloat16),
            jax.ShapeDtypeStruct(mk.shape, mk.dtype),
        ),
        in_specs=[
            pl.BlockSpec((seqs, per * width), lambda i: (0, i)),
            pl.BlockSpec((seqs, 128), lambda i: (0, rows * width // 128)),
            whole(right), whole(rr), whole(rc),
            pl.BlockSpec((per, cols, channels), lambda i: (i, 0, 0)),
            whole(gain), whole(w), whole(wd), whole(x), whole(mk),
        ],
        out_specs=(
            pl.BlockSpec((per, cols, channels), lambda i: (i, 0, 0)),
            pl.BlockSpec((per, heads * cols), lambda i: (i, 0)),
            hbm, hbm,
        ),
        scratch_shapes=[
            pltpu.VMEM((cols * width, seqs), jnp.bfloat16),
            pltpu.VMEM((64 * width, 2 * channels), jnp.bfloat16),
            pltpu.VMEM((per // 2 * cols, 64 * width), jnp.bfloat16),
            pltpu.VMEM((steps, cols, per), jnp.float32),
            pltpu.VMEM((heads, per, cols), jnp.float32),
            dma((8,)), dma((8,)), dma((8,)), dma((8,)),
        ],
        compiler_params=pltpu.CompilerParams(
            vmem_limit_bytes=52 << 20, collective_id=2, has_side_effects=True
        ),
        name="opm",
    )(left, left, right, rr, rc, pair, gain, w, wd, x, mk)


def shards(
    aligned_family_embedding,
    aligned_slot_available,
    chain_site_available,
    duo_embedding,
    averaging_layernorm_stretch,
    lineup_layernorm_stretch,
    duo_layernorm_stretch,
    lefthand_linear_kernel,
    righthand_linear_kernel,
    kronecker_linear_kernel,
    duo_logit_kernel,
    asker_lookup_sigmoid_kernel,
    closing_linear_kernel,
):
    homolog_number, amino_position_number, discarded_carry = aligned_family_embedding.shape
    res_rows = duo_embedding.shape[0]
    opm_width = lefthand_linear_kernel.shape[1]
    head_count = duo_logit_kernel.shape[1]
    inner_width = closing_linear_kernel.shape[0]
    row_index = lax.axis_index("row")
    col_index = lax.axis_index("col")
    standardized_features = standardize_features(aligned_family_embedding.astype(jnp.float32))
    availability_real = aligned_slot_available.astype(jnp.float32)
    half_rows = res_rows
    opm_input = (standardized_features * averaging_layernorm_stretch).astype(jnp.bfloat16)
    left = jnp.einsum("src,ca->sra", opm_input, lefthand_linear_kernel, preferred_element_type=jnp.float32)
    left = (left * availability_real[:, :, None]).astype(jnp.bfloat16)
    left = left.reshape(homolog_number, 2, half_rows * opm_width).transpose(1, 0, 2)
    left_mask = availability_real.reshape(homolog_number, 2, half_rows).transpose(1, 0, 2)
    left_mask = jnp.pad(left_mask, ((0, 0), (0, 0), (0, 128 - half_rows))).astype(jnp.bfloat16)
    left = jnp.concatenate([left, left_mask], axis=2)
    right = jnp.einsum("src,ca->sar", opm_input, righthand_linear_kernel, preferred_element_type=jnp.float32)
    right = (right * availability_real[:, None, :]).astype(jnp.bfloat16)
    right_mask = jnp.pad(availability_real, ((0, 0), (0, 128 - amino_position_number))).astype(jnp.bfloat16)
    right = jnp.concatenate([right.reshape(homolog_number, -1), right_mask], axis=1)
    mask_out = jnp.pad(
        availability_real.reshape(8, homolog_number // 8, amino_position_number),
        ((0, 0), (0, 8 - homolog_number // 8), (0, 128 - amino_position_number)),
    )
    left_all, right_all = spread(left, right)
    residue_float = chain_site_available.astype(jnp.float32)
    residue_rows = lax.dynamic_slice_in_dim(residue_float, row_index * res_rows, res_rows)
    residue_cols = lax.dynamic_slice_in_dim(
        residue_float, col_index * amino_position_number, amino_position_number
    )
    duo_after_averaging, bias_tile, own_rows, own_mask = opm(
        left_all, right_all, residue_rows, residue_cols, duo_embedding,
        duo_layernorm_stretch, kronecker_linear_kernel, duo_logit_kernel, aligned_family_embedding, mask_out,
    )
    lanes = inner_width // 2
    gated = attention(
        bias_tile, own_rows, own_mask, lineup_layernorm_stretch, asker_lookup_sigmoid_kernel,
        amino_position_number, homolog_number,
    )
    closing = closing_linear_kernel.reshape(2, lanes, -1)
    summed_increment = jnp.einsum("hsqd,hdc->sqc", gated, closing, preferred_element_type=jnp.float32)
    refreshed_family_embedding = (
        aligned_family_embedding.astype(jnp.float32) + summed_increment
    ).astype(jnp.bfloat16)
    return (refreshed_family_embedding, duo_after_averaging)


def solution(mesh):
    placed = (
        P("row", "col", None),
        P("row", "col"),
        P(),
        P("row", "col", None),
        P(),
        P(),
        P(),
        P(),
        P(),
        P(),
        P(),
        P(),
        P(),
    )
    return jax.shard_map(
        shards,
        mesh=mesh,
        in_specs=placed,
        out_specs=(P("row", "col", None), P("row", "col", None)),
        check_vma=False,
    )
```

```python
import jax
import jax.numpy as jnp
from jax import lax
from jax.experimental import pallas as pl
from jax.experimental.pallas import tpu as pltpu
from jax.sharding import PartitionSpec as P

EPSILON = 1e-05
CONTRACT_FIRST = (((0,), (0,)), ((), ()))
LAST_LAST = (((1,), (1,)), ((), ()))
HEAD_DIM = 32


def standardize_features(values):
    average = jnp.mean(values, axis=-1, keepdims=True)
    centred = values - average
    variance = jnp.mean(centred * centred, axis=-1, keepdims=True)
    return centred * lax.rsqrt(variance + EPSILON)


MESH = pl.DeviceIdType.MESH


def place():
    r, c = lax.axis_index("row"), lax.axis_index("col")
    return r, c


def row_of(y, zh, core):
    return y * 4 + zh * 2 + core


def remote(src, dst, send, recv, device):
    return pltpu.make_async_remote_copy(
        src_ref=src, dst_ref=dst, send_sem=send, recv_sem=recv, device_id=device, device_id_type=MESH
    )


def signal(barrier, device):
    pl.semaphore_signal(barrier, inc=1, device_id=device, device_id_type=MESH)


LOG2E = 1.4426950408889634


def whole_kernel(left_ref, right_ref, rrow_ref, rcol_ref, pair_ref, gain_ref, kron_ref, wd_ref, emb_ref, mask_ref,
                 again_ref, w_ref, out_ref, o_ref,
                 left_s, right_s, pair_s, rt_s, wb_s, mm_s, f_s, b_s, tile_s, w_s, block, ta, tb, tc, x_s, m_s, mb_s,
                 q_s, kt_s, v_s, g_s, bf_s, acc_s, out_s,
                 lsend, lrecv, gsend, zsend, zrecv, ysend, yrecv, fsend, frecv, own_sem, pin, pout,
                 asend, arecv, msend, mrecv, csem, csend, crecv, xsend, xrecv, l1, s1, r1, s2, r2, s3, r3, send, recv):
    r, c = place()
    chip, core = r // 2, r % 2
    y, zh, x, zl = r // 4, chip % 2, c // 2, c % 2
    seqs = right_ref.shape[0]
    opm = kron_ref.shape[0]
    parts, per = tile_s.shape[0], tile_s.shape[1]
    cols = pair_ref.shape[1]
    width = cols * opm
    half, length = x_s.shape[1], x_s.shape[2]
    heads, rows = bf_s.shape[0], bf_s.shape[1]
    spot = {"x": x, "y": y, "z": zh * 2 + zl}
    scale = float(HEAD_DIM) ** -0.5
    orders = ((ta, "xzy"), (tb, "yxz"), (tc, "zyx"))

    def rows_of(n):
        return pl.ds(pl.multiple_of(n * seqs, seqs), seqs)

    here = rows_of(r)
    partner = (chip * 2 + 1 - core, c)
    across = (row_of(y, 1 - zh, core), c)
    aside = (r, x * 2 + 1 - zl)
    mine = jnp.logical_and(chip == c, zh == zl)

    def own_left(h, j):
        return jnp.logical_and(mine, core == h) if j == 0 else False

    def unless(cond, f):
        if cond is False:
            f()
        else:
            pl.when(jnp.logical_not(cond))(f)

    def peer(dim, d):
        to = dict(spot)
        to[dim] = (spot[dim] + d) % 4
        return (row_of(to["y"], to["z"] // 2, core), to["x"] * 2 + to["z"] % 2)

    barrier = pltpu.get_barrier_semaphore()
    signal(barrier, across)
    for dim in "xyz":
        for d in range(1, 4):
            signal(barrier, peer(dim, d))
    for j in range(8):
        if j > 0:
            signal(barrier, (r, (c + j) % 8))
        signal(barrier, (partner[0], (c + j) % 8))
    for ys in range(4):
        for k in range(2):
            source = row_of(ys, zl, k)
            unless(jnp.logical_and(mine, r == source), lambda: signal(barrier, (source, chip)))
    pair_in = pltpu.make_async_copy(pair_ref, pair_s, pin.at[0])
    pair_in.start()
    pl.semaphore_wait(barrier, 33 - mine.astype(jnp.int32))

    over = remote(right_ref, right_s.at[here], zsend.at[0], zrecv.at[0], across)
    over.start()
    lefts = []
    for j in range(4):
        for h in range(2):
            to = (2 * c + h, ((x + j) % 4) * 2 + zh)
            cp = remote(left_ref.at[h], left_s.at[here], lsend.at[2 * j + h], lrecv.at[r], to)
            lefts.append((cp, h, j))
            unless(own_left(h, j), cp.start)
            if j == 0:

                @pl.when(own_left(h, j))
                def _():
                    pltpu.make_async_copy(left_ref.at[h], left_s.at[here], lrecv.at[r]).start()

    def along(n, d):
        blk = rows_of(row_of(y, (zh + n) % 2, core))
        src = right_ref if n == 0 else right_s.at[blk]
        return remote(src, right_s.at[blk], ysend.at[n * 4 + d], yrecv.at[n * 4 + d], (row_of((y + d) % 4, zh, core), c))

    def forward(n, d):
        blk = rows_of(row_of((y + 4 - d) % 4, (zh + n) % 2, core))
        src = right_ref if n == 0 and d == 0 else right_s.at[blk]
        return remote(src, right_s.at[blk], fsend.at[n * 4 + d], frecv.at[n * 4 + d], partner)

    def relay(d, k):
        source = row_of((y + 4 - d) % 4, zl, k)
        blk = left_s.at[rows_of(source)]
        return blk, source, remote(blk, blk, gsend.at[d * 2 + k], lrecv.at[source], aside)

    res = pl.ds(pl.multiple_of(c * cols, cols), cols)

    def moves(d):
        to = (r, (c + d) % 8)
        take = pl.ds(pl.multiple_of(to[1] * half, half), half)
        return (
            remote(emb_ref.at[take], x_s.at[0, :, res], asend.at[d], arecv.at[d], to),
            remote(mask_ref.at[to[1]], m_s.at[0, c], msend.at[d], mrecv.at[d], to),
        )

    def kept():
        return (
            pltpu.make_async_copy(
                emb_ref.at[pl.ds(pl.multiple_of(c * half, half), half)], x_s.at[0, :, res], arecv.at[0]
            ),
            pltpu.make_async_copy(mask_ref.at[c], m_s.at[0, c], mrecv.at[0]),
        )

    for d in (1, 3, 2):
        along(0, d).start()
    own = pltpu.make_async_copy(right_ref, right_s.at[here], own_sem.at[0])
    own.start()
    forward(0, 0).start()
    for d in (2, 4, 6):
        for cp in moves(d):
            cp.start()
    for cp in kept():
        cp.start()
    over.wait_recv()
    for d in (1, 3, 2):
        along(1, d).start()
    forward(1, 0).start()

    wb_s[...] = jnp.zeros_like(wb_s)

    def fill(b, carry):
        for i in range(2):
            wb_s[pl.ds(pl.multiple_of(b * 64 + i * 32, 32), 32), i * 128 : (i + 1) * 128] = kron_ref[b]
        return carry

    lax.fori_loop(0, opm, fill, 0)
    wide = w_ref.shape[1] // 4
    part = w_s.shape[1] // 4
    for n in range(4):
        w_s[:, n * part : (n + 1) * part] = w_ref[:, pl.ds(pl.multiple_of(n * wide + core * part, part), part)]

    for d in (0, 1, 3, 2):
        for k in range(2):
            blk, source, cp = relay(d, k)
            pltpu.make_async_copy(left_ref.at[0], blk, lrecv.at[source]).wait()
            cp.start()
        if d > 0:
            along(0, d).wait_recv()
            forward(0, d).start()
    for d in (1, 3, 2):
        along(1, d).wait_recv()
        forward(1, d).start()
    for d in (1, 3, 5, 7):
        for cp in moves(d):
            cp.start()

    chunk = 4 * cols
    for d in (0, 1, 3, 2):
        if d == 0:
            own.wait()
        for n in range(2):
            forward(n, d).wait_recv()
        ys = (y + 4 - d) % 4
        near = pl.ds(pl.multiple_of(ys * 4 * seqs, 4 * seqs), 4 * seqs)

        def flip(n, carry):
            at = pl.ds(pl.multiple_of(n * chunk, chunk), chunk)
            rt_s[at, near] = right_s[near, at].T
            return carry

        lax.fori_loop(0, opm // 4, flip, 0)
    for ys in range(4):
        for k in range(2):
            source = row_of(ys, 1 - zl, k)
            pltpu.make_async_copy(left_ref.at[0], left_s.at[rows_of(source)], lrecv.at[source]).wait()
    counts = lax.dot_general(
        right_s[:, width:], left_s[:, parts * per * 32 :], CONTRACT_FIRST, preferred_element_type=jnp.float32
    )[:cols, : parts * per]
    f_s[...] = rcol_ref[...] * rrow_ref[...] / (counts + 0.001)
    pair_in.wait()

    lanes = tile_s.shape[2] // 2

    def swap(st):
        spot_rows = pl.ds(pl.multiple_of(core * per, per), per)
        give = tile_s.at[st, :, pl.ds(pl.multiple_of((1 - core) * lanes, lanes), lanes)]
        keep = tile_s.at[st, :, pl.ds(pl.multiple_of(core * lanes, lanes), lanes)]
        return (
            pltpu.make_async_copy(keep, block.at[st, spot_rows], csem.at[st]),
            remote(give, block.at[st, spot_rows], csend.at[st], crecv.at[st], partner),
        )

    def one(st, o, d):
        out, dims = orders[o]
        slot = out.at[st, spot[dims[2]], spot[dims[1]], spot[dims[0]]]
        piece = block.at[st, :, pl.ds(o * 128, 128)]
        if d == 0:
            return pltpu.make_async_copy(piece, slot, l1.at[st * 3 + o])
        at = (st * 3 + o) * 4 + d
        return remote(piece, slot, s1.at[at], r1.at[at], peer(dims[0], d))

    def two(st, o, d):
        out, dims = orders[o]
        slot = out.at[st, spot[dims[2]], spot[dims[1]]]
        at = (st * 3 + o) * 4 + d
        return remote(slot, slot, s2.at[at], r2.at[at], peer(dims[1], d))

    def three(st, o, e, d):
        out, dims = orders[o]
        slot = out.at[st, spot[dims[2]], (spot[dims[1]] + 4 - e) % 4]
        at = (st * 3 + o) * 16 + e * 4 + d
        return remote(slot, slot, s3.at[at], r3.at[at], peer(dims[2], d))

    def begin(st):
        for cp in swap(st):
            cp.start()

    def first(st):
        cps = swap(st)
        cps[0].wait()
        cps[1].wait_recv()
        for o in range(3):
            for d in range(4):
                one(st, o, d).start()

    def middle(st):
        for o in range(3):
            for d in range(4):
                if d == 0:
                    one(st, o, d).wait()
                else:
                    one(st, o, d).wait_recv()
            for d in range(1, 4):
                two(st, o, d).start()
            for d in range(1, 4):
                three(st, o, 0, d).start()

    def last(st):
        for e in range(1, 4):
            for o in range(3):
                two(st, o, e).wait_recv()
                for d in range(1, 4):
                    three(st, o, e, d).start()

    group = per // 4

    def outer(st):
        def body(n, carry):
            at = pl.multiple_of(n * chunk, chunk)
            m = jnp.dot(
                rt_s[pl.ds(at, chunk), :], left_s[:, st * per * 32 : (st + 1) * per * 32],
                preferred_element_type=jnp.float32,
            )
            low = lax.broadcasted_iota(jnp.int32, (1, 128), 1) < 64
            for bb in range(2):
                to = pl.ds(pl.multiple_of((n * 2 + bb) * 128, 128), 128)
                for g in range(group):
                    m0, m1 = [
                        m[(2 * bb + k) * cols : (2 * bb + k + 1) * cols, g * 128 : (g + 1) * 128] for k in range(2)
                    ]
                    lo = jnp.where(low, m0, pltpu.roll(m1, 64, 1)).astype(jnp.bfloat16)
                    hi = jnp.where(low, pltpu.roll(m0, 64, 1), m1).astype(jnp.bfloat16)
                    mm_s[(2 * g) * cols : (2 * g + 1) * cols, to] = lo
                    mm_s[(2 * g + 1) * cols : (2 * g + 2) * cols, to] = hi
            return carry

        lax.fori_loop(0, opm // 4, body, 0)

    def mix(st):
        update = jnp.dot(mm_s[...], wb_s[...], preferred_element_type=jnp.float32)
        for g in range(2 * group):
            for ii in range(2):
                i = 2 * g + ii
                at = st * per + i
                u = update[g * cols : (g + 1) * cols, ii * 128 : (ii + 1) * 128]
                v = pair_s[at] + u * f_s[:, at : at + 1]
                pair_s[at] = v
                v = (standardize_features(v) * gain_ref[...]).astype(jnp.bfloat16)
                b_s[:, i, :] = lax.dot_general(wd_ref[...], v, LAST_LAST, preferred_element_type=jnp.float32)
        tile_s[st] = jnp.concatenate([b_s[h] for h in range(2 * heads)], axis=1).astype(jnp.bfloat16)

    def pair_back(st):
        at = pl.ds(st * per, per)
        return pltpu.make_async_copy(pair_s.at[at], out_ref.at[at], pout.at[st])

    outer(0)
    mix(0)
    begin(0)
    pair_back(0).start()
    outer(1)
    first(0)
    mix(1)
    middle(0)
    begin(1)
    pair_back(1).start()
    outer(2)
    last(0)
    first(1)
    mix(2)
    middle(1)
    begin(2)
    pair_back(2).start()

    for d in range(1, 8):
        for cp in moves(d):
            cp.wait_recv()
    for cp in kept():
        cp.wait()
    xs = remote(x_s.at[0], x_s.at[1], xsend.at[0], xrecv.at[0], partner)
    ms = remote(m_s.at[0], m_s.at[1], xsend.at[1], xrecv.at[1], partner)
    xs.start()
    ms.start()

    def project(n):
        def body(b, carry):
            v = standardize_features(x_s[n, b].astype(jnp.float32))
            v = (v * again_ref[...]).astype(jnp.bfloat16)
            at = n * half + b
            both = jnp.dot(v, w_s[...], preferred_element_type=jnp.float32).astype(jnp.bfloat16)
            q, k, v, g = [both[:, i * part : (i + 1) * part] for i in range(4)]
            for st in range(parts):
                pick = [slice((i * parts + st) * per, (i * parts + st + 1) * per) for i in range(rows // per)]
                q_s[at, st] = jnp.concatenate([q[p] for p in pick], axis=0)
                g_s[at, st] = jnp.concatenate([g[p] for p in pick], axis=0)
            v_s[at] = v
            kt_s[at] = k.T
            return carry

        lax.fori_loop(0, half, body, 0)
        for b in range(half):
            line = jnp.concatenate([m_s[n, cc, b : b + 1, :cols] for cc in range(8)], axis=1)
            mb_s[n * half + b] = (1e9 / scale) * (line - 1.0)

    first(2)
    last(1)
    project(0)
    middle(2)
    xs.wait_recv()
    ms.wait_recv()
    project(1)

    def attend(st, carry):
        for o in range(3):
            for e in range(4):
                for d in range(1, 4):
                    out, dims = orders[o]
                    at = (st * 3 + o) * 16 + e * 4 + d
                    slot = out.at[st, (spot[dims[2]] + 4 - d) % 4, (spot[dims[1]] + 4 - e) % 4]
                    remote(slot, slot, s3.at[at], r3.at[at], peer(dims[2], d)).wait_recv()

        def assemble(p, carry):
            yy, zz = p // 2, p % 2
            pieces = []
            for cc in range(8):
                xx, z = cc // 2, zz * 2 + cc % 2
                pieces.append(
                    jnp.concatenate([ta[st, yy, z, xx], tb[st, z, xx, yy], tc[st, xx, yy, z]], axis=1)
                )
            for h in range(heads):
                line = jnp.concatenate([piece[:, h * cols : (h + 1) * cols] for piece in pieces], axis=1)
                bf_s[h, pl.ds(pl.multiple_of(p * 2 * per, 2 * per), 2 * per), :] = line.astype(jnp.float32) * (
                    1.0 / scale
                )
            return carry

        lax.fori_loop(0, 8, assemble, 0)

        def batch(n, carry):
            def one_head(h, carry):
                @pl.when(jnp.logical_and(st == 0, jnp.logical_and(n == 0, h == 1)))
                def _():
                    last(2)

                head = lax.broadcasted_iota(jnp.int32, (1, part), 1) // HEAD_DIM
                mine_f = jnp.where(head == h, 1.0, 0.0)
                its = mine_f.astype(jnp.bfloat16)
                other = (1.0 - mine_f).astype(jnp.bfloat16)
                for b in range(half):
                    at = n * half + b
                    q = q_s[at, st] * its
                    s = jnp.dot(q, kt_s[at], preferred_element_type=jnp.float32) + bf_s[h] + mb_s[at]
                    top = jnp.max(s, axis=1, keepdims=True)
                    p = jnp.exp2(((s - top) * (scale * LOG2E)).astype(jnp.bfloat16))
                    w = jnp.dot(p, v_s[at] * its + other, preferred_element_type=jnp.float32)
                    mixed = w / pltpu.roll(w, HEAD_DIM, 1)
                    acc_s[b] = jnp.where(mine_f > 0.0, mixed, acc_s[b])
                return carry

            lax.fori_loop(0, heads, one_head, 0)

            def gate(b, carry):
                g = g_s[n * half + b, st].astype(jnp.float32)
                gated = (acc_s[b] * jax.nn.sigmoid(g)).astype(jnp.bfloat16)
                for p in range(8):
                    for k in range(2):
                        at = (p * 2 + k) * per
                        out_s[st, n, p, b, k] = gated[at : at + per]
                return carry

            lax.fori_loop(0, half, gate, 0)
            for j in range(8):
                p = (c + j) % 8
                src = out_s.at[st, n, p]
                dst = o_ref.at[core, pl.ds(pl.multiple_of(c * half, half), half), :, st]
                arrived = recv.at[st * 16 + c * 2 + core]
                row = jnp.where(n == 0, r, partner[0])
                cp = remote(src, dst, send.at[(st * 2 + n) * 8 + p], arrived, (row, p))
                if j == 0:

                    @pl.when(n > 0)
                    def _():
                        cp.start()

                    @pl.when(n == 0)
                    def _():
                        pltpu.make_async_copy(src, dst, arrived).start()
                else:
                    cp.start()
            return carry

        return lax.fori_loop(0, 2, batch, carry)

    lax.fori_loop(0, parts, attend, 0)

    over.wait_send()
    for cp, h, j in lefts:
        unless(own_left(h, j), cp.wait_send)
    for d in range(4):
        for k in range(2):
            relay(d, k)[2].wait_send()
    for n in range(2):
        for d in range(4):
            forward(n, d).wait_send()
            if d > 0:
                along(n, d).wait_send()
    for d in range(1, 8):
        for cp in moves(d):
            cp.wait_send()
    xs.wait_send()
    ms.wait_send()

    def close(st, carry):
        swap(st)[1].wait_send()
        pair_back(st).wait()
        for cs in range(8):
            for k in range(2):
                pltpu.make_async_copy(
                    out_s.at[0, 0, 0], o_ref.at[k, pl.ds(cs * half, half), :, st], recv.at[st * 16 + cs * 2 + k]
                ).wait()
        for n in range(2):
            for j in range(8):
                p = (c + j) % 8
                if n == 0 and j == 0:
                    continue
                row = r if n == 0 else partner[0]
                remote(
                    out_s.at[st, n, p], o_ref.at[core, pl.ds(pl.multiple_of(c * half, half), half), :, st],
                    send.at[(st * 2 + n) * 8 + p], recv.at[0], (row, p),
                ).wait_send()
        for o in range(3):
            for d in range(1, 4):
                one(st, o, d).wait_send()
                two(st, o, d).wait_send()
                for e in range(4):
                    three(st, o, e, d).wait_send()
        return carry

    for st in range(parts):
        close(st, 0)


def whole(left, right, rrow, rcol, pair, gain, kron, logit, emb, mask, again, w):
    rows, cols, channels = pair.shape
    home, _, depth = emb.shape
    seqs = home // 4
    half = seqs // 2
    total = 16 * home
    heads = logit.shape[1] // 2
    lanes = heads * HEAD_DIM
    length = 8 * cols
    width = kron.shape[0] // 32
    per = 16
    parts = rows // per
    block = length // parts
    kr = kron.reshape(width, width, channels).transpose(1, 0, 2)
    vmem = pl.BlockSpec(memory_space=pltpu.VMEM)
    hbm = pl.BlockSpec(memory_space=pl.ANY)
    dma = pltpu.SemaphoreType.DMA
    bf = lambda *s: pltpu.VMEM(s, jnp.bfloat16)
    fl = lambda *s: pltpu.VMEM(s, jnp.float32)
    pair_out, out = pl.pallas_call(
        whole_kernel,
        out_shape=(
            jax.ShapeDtypeStruct(pair.shape, jnp.float32),
            jax.ShapeDtypeStruct((2, home, 2, parts, per, lanes), jnp.bfloat16),
        ),
        in_specs=[vmem, vmem, vmem, vmem, hbm, vmem, vmem, vmem, hbm, vmem, vmem, vmem],
        out_specs=(hbm, hbm),
        scratch_shapes=[
            bf(total, left.shape[2]), bf(total, right.shape[1]), fl(*pair.shape),
            bf(cols * width, total), bf(64 * width, 2 * channels), bf(per // 2 * cols, 64 * width),
            fl(cols, rows), fl(2 * heads, per, cols), bf(parts, per, 2 * heads * cols),
            bf(depth, 4 * lanes), bf(parts, 2 * per, heads * cols),
            bf(parts, 4, 4, 4, 2 * per, 128), bf(parts, 4, 4, 4, 2 * per, 128), bf(parts, 4, 4, 4, 2 * per, 128),
            bf(2, half, length, depth), pltpu.VMEM((2,) + mask.shape, jnp.float32), fl(seqs, 1, length),
            bf(seqs, parts, block, lanes), bf(seqs, lanes, length), bf(seqs, length, lanes),
            bf(seqs, parts, block, lanes), fl(heads, block, length), fl(half, block, lanes),
            bf(parts, 2, 8, half, 2, per, lanes),
            dma((8,)), dma((16,)), dma((8,)), dma((1,)), dma((1,)), dma((8,)), dma((8,)), dma((8,)), dma((8,)),
            dma((1,)), dma((1,)), dma((3,)),
            dma((8,)), dma((8,)), dma((8,)), dma((8,)), dma((3,)), dma((3,)), dma((3,)), dma((2,)), dma((2,)),
            dma((9,)), dma((36,)), dma((36,)), dma((36,)), dma((36,)), dma((144,)), dma((144,)),
            dma((48,)), dma((48,)),
        ],
        compiler_params=pltpu.CompilerParams(
            vmem_limit_bytes=60 << 20, collective_id=1, has_side_effects=True
        ),
        name="whole",
    )(left, right, rrow.reshape(1, rows), rcol.reshape(cols, 1), pair, gain.reshape(1, channels), kr, logit.T, emb, mask,
      again.reshape(1, depth), w)
    return pair_out, out.reshape(2, home, cols, lanes)


def shards(
    aligned_family_embedding,
    aligned_slot_available,
    chain_site_available,
    duo_embedding,
    averaging_layernorm_stretch,
    lineup_layernorm_stretch,
    duo_layernorm_stretch,
    lefthand_linear_kernel,
    righthand_linear_kernel,
    kronecker_linear_kernel,
    duo_logit_kernel,
    asker_lookup_sigmoid_kernel,
    closing_linear_kernel,
):
    homolog_number, amino_position_number, discarded_carry = aligned_family_embedding.shape
    res_rows = duo_embedding.shape[0]
    opm_width = lefthand_linear_kernel.shape[1]
    head_count = duo_logit_kernel.shape[1]
    inner_width = closing_linear_kernel.shape[0]
    row_index = lax.axis_index("row")
    col_index = lax.axis_index("col")
    standardized_features = standardize_features(aligned_family_embedding.astype(jnp.float32))
    availability_real = aligned_slot_available.astype(jnp.float32)
    half_rows = res_rows
    opm_input = (standardized_features * averaging_layernorm_stretch).astype(jnp.bfloat16)
    left = jnp.einsum("src,ca->sra", opm_input, lefthand_linear_kernel, preferred_element_type=jnp.float32)
    left = (left * availability_real[:, :, None]).astype(jnp.bfloat16)
    left = left.reshape(homolog_number, 2, half_rows * opm_width).transpose(1, 0, 2)
    left_mask = availability_real.reshape(homolog_number, 2, half_rows).transpose(1, 0, 2)
    left_mask = jnp.pad(left_mask, ((0, 0), (0, 0), (0, 128 - half_rows))).astype(jnp.bfloat16)
    left = jnp.concatenate([left, left_mask], axis=2)
    right = jnp.einsum("src,ca->sar", opm_input, righthand_linear_kernel, preferred_element_type=jnp.float32)
    right = (right * availability_real[:, None, :]).astype(jnp.bfloat16)
    right_mask = jnp.pad(availability_real, ((0, 0), (0, 128 - amino_position_number))).astype(jnp.bfloat16)
    right = jnp.concatenate([right.reshape(homolog_number, -1), right_mask], axis=1)
    mask_out = jnp.pad(
        availability_real.reshape(8, homolog_number // 8, amino_position_number),
        ((0, 0), (0, 8 - homolog_number // 8), (0, 128 - amino_position_number)),
    )
    residue_float = chain_site_available.astype(jnp.float32)
    residue_rows = lax.dynamic_slice_in_dim(residue_float, row_index * res_rows, res_rows)
    residue_cols = lax.dynamic_slice_in_dim(
        residue_float, col_index * amino_position_number, amino_position_number
    )
    lanes = inner_width // 2
    duo_after_averaging, gated = whole(
        left, right, residue_rows, residue_cols, duo_embedding, duo_layernorm_stretch, kronecker_linear_kernel,
        duo_logit_kernel, aligned_family_embedding, mask_out, lineup_layernorm_stretch, asker_lookup_sigmoid_kernel,
    )
    closing = closing_linear_kernel.reshape(2, lanes, -1)
    summed_increment = jnp.einsum("hsqd,hdc->sqc", gated, closing, preferred_element_type=jnp.float32)
    refreshed_family_embedding = (
        aligned_family_embedding.astype(jnp.float32) + summed_increment
    ).astype(jnp.bfloat16)
    return (refreshed_family_embedding, duo_after_averaging)


def solution(mesh):
    placed = (
        P("row", "col", None),
        P("row", "col"),
        P(),
        P("row", "col", None),
        P(),
        P(),
        P(),
        P(),
        P(),
        P(),
        P(),
        P(),
        P(),
    )
    return jax.shard_map(
        shards,
        mesh=mesh,
        in_specs=placed,
        out_specs=(P("row", "col", None), P("row", "col", None)),
        check_vma=False,
    )
```

```python
import jax
import jax.numpy as jnp
from jax import lax
from jax.experimental import pallas as pl
from jax.experimental.pallas import tpu as pltpu
from jax.sharding import PartitionSpec as P

EPSILON = 1e-05
CONTRACT_FIRST = (((0,), (0,)), ((), ()))
LAST_LAST = (((1,), (1,)), ((), ()))
HEAD_DIM = 32


def standardize_features(values):
    average = jnp.mean(values, axis=-1, keepdims=True)
    centred = values - average
    variance = jnp.mean(centred * centred, axis=-1, keepdims=True)
    return centred * lax.rsqrt(variance + EPSILON)


MESH = pl.DeviceIdType.MESH


def place():
    r, c = lax.axis_index("row"), lax.axis_index("col")
    return r, c


def row_of(y, zh, core):
    return y * 4 + zh * 2 + core


def remote(src, dst, send, recv, device):
    return pltpu.make_async_remote_copy(
        src_ref=src, dst_ref=dst, send_sem=send, recv_sem=recv, device_id=device, device_id_type=MESH
    )


def signal(barrier, device):
    pl.semaphore_signal(barrier, inc=1, device_id=device, device_id_type=MESH)


def spread_kernel(left_ref, right_ref, emb_ref, left_out, right_out, x_out, xsend, xrecv, lsend, lrecv, gsend, zsend, zrecv, ysend, yrecv, fsend,
                  frecv, own_sem):
    r, c = place()
    chip, core = r // 2, r % 2
    y, zh, x, zl = r // 4, chip % 2, c // 2, c % 2
    seqs = right_ref.shape[0]

    def rows(n):
        return pl.ds(pl.multiple_of(n * seqs, seqs), seqs)

    here = rows(r)
    partner = (chip * 2 + 1 - core, c)
    across = (row_of(y, 1 - zh, core), c)
    aside = (r, x * 2 + 1 - zl)
    mine = jnp.logical_and(chip == c, zh == zl)

    def own_left(h, j):
        return jnp.logical_and(mine, core == h) if j == 0 else False

    def unless(cond, f):
        if cond is False:
            f()
        else:
            pl.when(jnp.logical_not(cond))(f)

    barrier = pltpu.get_barrier_semaphore()
    signal(barrier, partner)
    signal(barrier, across)
    signal(barrier, aside)
    for d in range(1, 4):
        signal(barrier, (row_of((y + d) % 4, zh, core), c))
    for ys in range(4):
        for k in range(2):
            source = row_of(ys, zl, k)
            unless(jnp.logical_and(mine, r == source), lambda: signal(barrier, (source, chip)))
    for d in range(1, 4):
        signal(barrier, (r, ((x + d) % 4) * 2 + zl))
    pl.semaphore_wait(barrier, 17 - mine.astype(jnp.int32))
    half = x_out.shape[1]

    def move(d):
        xd = (x + d) % 4
        take = pl.ds(pl.multiple_of((xd * 2 + zl) * half, half), half)
        return remote(emb_ref.at[take], x_out.at[x], xsend.at[d], xrecv.at[d], (r, xd * 2 + zl))


    over = remote(right_ref, right_out.at[here], zsend.at[0], zrecv.at[0], across)
    over.start()
    sends = [over]
    lefts = []
    for j in range(4):
        for h in range(2):
            to = (2 * c + h, ((x + j) % 4) * 2 + zh)
            cp = remote(left_ref.at[h], left_out.at[here], lsend.at[2 * j + h], lrecv.at[r], to)
            lefts.append((cp, h, j))
            unless(own_left(h, j), cp.start)
            if j == 0:

                @pl.when(own_left(h, j))
                def _():
                    pltpu.make_async_copy(left_ref.at[h], left_out.at[here], lrecv.at[r]).start()

    def along(n, d):
        block = rows(row_of(y, (zh + n) % 2, core))
        src = right_ref if n == 0 else right_out.at[block]
        return remote(src, right_out.at[block], ysend.at[n * 4 + d], yrecv.at[n * 4 + d], (row_of((y + d) % 4, zh, core), c))

    def forward(n, d):
        block = rows(row_of((y + 4 - d) % 4, (zh + n) % 2, core))
        src = right_ref if n == 0 and d == 0 else right_out.at[block]
        return remote(src, right_out.at[block], fsend.at[n * 4 + d], frecv.at[n * 4 + d], partner)

    for d in (1, 3, 2):
        along(0, d).start()
    own = pltpu.make_async_copy(right_ref, right_out.at[here], own_sem.at[0])
    own.start()
    forward(0, 0).start()
    for d in (1, 3, 2):
        move(d).start()
    over.wait_recv()
    for d in (1, 3, 2):
        along(1, d).start()
    forward(1, 0).start()

    def relay(d, k):
        source = row_of((y + 4 - d) % 4, zl, k)
        block = left_out.at[rows(source)]
        return block, source, remote(block, block, gsend.at[d * 2 + k], lrecv.at[source], aside)

    for d in (0, 1, 3, 2):
        for k in range(2):
            block, source, cp = relay(d, k)
            pltpu.make_async_copy(left_ref.at[0], block, lrecv.at[source]).wait()
            cp.start()
        if d > 0:
            along(0, d).wait_recv()
            forward(0, d).start()
    for d in (1, 3, 2):
        along(1, d).wait_recv()
        forward(1, d).start()
    for ys in range(4):
        for k in range(2):
            source = row_of(ys, 1 - zl, k)
            pltpu.make_async_copy(left_ref.at[0], left_out.at[rows(source)], lrecv.at[source]).wait()
    own.wait()
    for n in range(2):
        for d in range(4):
            forward(n, d).wait()
            if d > 0:
                along(n, d).wait_send()
    over.wait_send()
    for d in range(1, 4):
        move(d).wait()
    for cp, h, j in lefts:
        unless(own_left(h, j), cp.wait_send)
    for d in range(4):
        for k in range(2):
            relay(d, k)[2].wait_send()


def spread(left, right, emb):
    seqs = right.shape[0]
    vmem = pl.BlockSpec(memory_space=pltpu.VMEM)
    hbm = pl.BlockSpec(memory_space=pl.ANY)
    dma = pltpu.SemaphoreType.DMA
    return pl.pallas_call(
        spread_kernel,
        out_shape=(
            jax.ShapeDtypeStruct((16 * seqs, left.shape[2]), jnp.bfloat16),
            jax.ShapeDtypeStruct((16 * seqs, right.shape[1]), jnp.bfloat16),
            jax.ShapeDtypeStruct((4, seqs // 8) + emb.shape[1:], jnp.bfloat16),
        ),
        in_specs=[vmem, vmem, hbm],
        out_specs=(hbm, hbm, hbm),
        scratch_shapes=[
            dma((4,)), dma((4,)),
            dma((8,)), dma((16,)), dma((8,)), dma((1,)), dma((1,)), dma((8,)), dma((8,)), dma((8,)), dma((8,)), dma((1,))
        ],
        compiler_params=pltpu.CompilerParams(collective_id=1, has_side_effects=True),
        name="spread",
    )(left, right, emb)


LOG2E = 1.4426950408889634


def attn_kernel(tile_ref, emb_ref, near_ref, far_ref, mask_ref, gain_ref, w_ref, o_ref, w_s, block, ta, tb, tc, x_s, m_s, mb_s, q_s, kt_s, v_s, g_s, bf_s, acc_s, out_s,
                lsem, csem, csend, crecv, l1, s1, r1, s2, r2, s3, r3, send, recv):
    r, c = place()
    chip, core = r // 2, r % 2
    spot = {"x": c // 2, "y": r // 4, "z": (chip % 2) * 2 + c % 2}
    half, length = x_s.shape[1], x_s.shape[2]
    heads, rows = bf_s.shape[0], bf_s.shape[1]
    cols = length // 8
    sub = cols // 6
    scale = float(HEAD_DIM) ** -0.5
    partner = (chip * 2 + 1 - core, c)
    orders = ((ta, "xzy"), (tb, "yxz"), (tc, "zyx"))

    def peer(dim, d):
        to = dict(spot)
        to[dim] = (spot[dim] + d) % 4
        return (row_of(to["y"], to["z"] // 2, core), to["x"] * 2 + to["z"] % 2)

    barrier = pltpu.get_barrier_semaphore()
    signal(barrier, partner)
    for dim in "xyz":
        for d in range(1, 4):
            signal(barrier, peer(dim, d))
    for j in range(8):
        if j > 0:
            signal(barrier, (r, (c + j) % 8))
        signal(barrier, (partner[0], (c + j) % 8))

    trows, lanes = tile_ref.shape[0], tile_ref.shape[1] // 2
    here = pl.ds(pl.multiple_of(core * trows, trows), trows)
    give = tile_ref.at[:, pl.ds(pl.multiple_of((1 - core) * lanes, lanes), lanes)]
    keep = tile_ref.at[:, pl.ds(pl.multiple_of(core * lanes, lanes), lanes)]
    own = pltpu.make_async_copy(keep, block.at[here], csem.at[0])
    own.start()
    locals_ = []
    for d in range(8):
        xd, zd = (c // 2 + d // 2) % 4, (c + d) % 2
        if d == 0:
            src = emb_ref.at[pl.ds(pl.multiple_of(c * half, half), half)]
        else:
            src = (far_ref if d % 2 else near_ref).at[xd]
        spot_cols = pl.ds(pl.multiple_of((xd * 2 + zd) * cols, cols), cols)
        locals_.append(pltpu.make_async_copy(src, x_s.at[0, :, spot_cols], lsem.at[d]))
        locals_[d].start()
    ml = pltpu.make_async_copy(mask_ref, m_s.at[0], csem.at[2])
    ml.start()
    pl.semaphore_wait(barrier, 25)
    swap = remote(give, block.at[here], csend.at[0], crecv.at[0], partner)
    swap.start()
    xs = remote(x_s.at[0], x_s.at[1], csend.at[1], crecv.at[1], partner)
    ms = remote(mask_ref, m_s.at[1], csend.at[2], crecv.at[2], partner)
    own.wait()
    swap.wait_recv()

    def one(hf, o, d):
        out, dims = orders[o]
        slot = out.at[hf, spot[dims[2]], spot[dims[1]], spot[dims[0]]]
        piece = block.at[pl.ds(o * 2 * sub + hf * sub, sub)]
        if d == 0:
            return pltpu.make_async_copy(piece, slot, l1.at[hf * 3 + o])
        at = (hf * 3 + o) * 4 + d
        return remote(piece, slot, s1.at[at], r1.at[at], peer(dims[0], d))

    def two(hf, o, d):
        out, dims = orders[o]
        slot = out.at[hf, spot[dims[2]], spot[dims[1]]]
        at = (hf * 3 + o) * 4 + d
        return remote(slot, slot, s2.at[at], r2.at[at], peer(dims[1], d))

    def three(hf, o, e, d):
        out, dims = orders[o]
        slot = out.at[hf, spot[dims[2]], (spot[dims[1]] + 4 - e) % 4]
        at = (hf * 3 + o) * 16 + e * 4 + d
        return remote(slot, slot, s3.at[at], r3.at[at], peer(dims[2], d))

    def middle(hf):
        for o in range(3):
            for d in range(4):
                if d == 0:
                    one(hf, o, d).wait()
                else:
                    one(hf, o, d).wait_recv()
            for d in range(1, 4):
                two(hf, o, d).start()
            for d in range(1, 4):
                three(hf, o, 0, d).start()

    def last(hf):
        for e in range(1, 4):
            for o in range(3):
                two(hf, o, e).wait_recv()
                for d in range(1, 4):
                    three(hf, o, e, d).start()

    for hf in range(2):
        for o in range(3):
            for d in range(4):
                one(hf, o, d).start()
    for cp in locals_:
        cp.wait()
    xs.start()
    ms.start()

    width = w_ref.shape[1] // 4
    part = w_s.shape[1] // 4
    for n in range(4):
        w_s[:, n * part : (n + 1) * part] = w_ref[:, pl.ds(pl.multiple_of(n * width + core * part, part), part)]

    def project(n, lo, hi):
        def body(b, carry):
            x = standardize_features(x_s[n, b].astype(jnp.float32))
            x = (x * gain_ref[...]).astype(jnp.bfloat16)
            at = n * half + b
            both = jnp.dot(x, w_s[...], preferred_element_type=jnp.float32).astype(jnp.bfloat16)
            p, k, v, g = [both[:, i * part : (i + 1) * part] for i in range(4)]
            for hf in range(2):
                q_s[at, hf] = jnp.concatenate(
                    [p[(2 * i + hf) * sub : (2 * i + hf + 1) * sub] for i in range(rows // sub)], axis=0
                )
                g_s[at, hf] = jnp.concatenate(
                    [g[(2 * i + hf) * sub : (2 * i + hf + 1) * sub] for i in range(rows // sub)], axis=0
                )
            v_s[at] = v
            kt_s[at] = k.T
            return carry

        lax.fori_loop(lo, hi, body, 0, unroll=2)

    def mask_lines(n):
        for b in range(half):
            line = jnp.concatenate([m_s[n, cc, b : b + 1, :cols] for cc in range(8)], axis=1)
            mb_s[n * half + b] = (1e9 / scale) * (line - 1.0)

    project(0, 0, 2)
    middle(0)
    project(0, 2, half)
    last(0)
    middle(1)
    ml.wait()
    mask_lines(0)
    xs.wait_recv()
    ms.wait_recv()
    mask_lines(1)
    project(1, 0, half)

    def block_of_rows(hf, carry):
        for o in range(3):
            for e in range(4):
                for d in range(1, 4):
                    out, dims = orders[o]
                    at = (hf * 3 + o) * 16 + e * 4 + d
                    slot = out.at[hf, (spot[dims[2]] + 4 - d) % 4, (spot[dims[1]] + 4 - e) % 4]
                    remote(slot, slot, s3.at[at], r3.at[at], peer(dims[2], d)).wait_recv()

        def assemble(p, carry):
            y, zh = p // 2, p % 2
            for o in range(3):
                pieces = []
                for cc in range(8):
                    x, z = cc // 2, zh * 2 + cc % 2
                    if o == 0:
                        piece = ta[hf, y, z, x]
                    elif o == 1:
                        piece = tb[hf, z, x, y]
                    else:
                        piece = tc[hf, x, y, z]
                    pieces.append(piece)
                for h in range(heads):
                    line = jnp.concatenate([piece[:, h * cols : (h + 1) * cols] for piece in pieces], axis=1)
                    bf_s[h, pl.ds(pl.multiple_of(p * 3 * sub + o * sub, sub), sub), :] = line.astype(jnp.float32) * (
                        1.0 / scale
                    )
            return carry

        lax.fori_loop(0, 8, assemble, 0)

        def group(n, carry):
            def one_head(h, carry):
                @pl.when(jnp.logical_and(hf == 0, jnp.logical_and(n == 0, h == 1)))
                def _():
                    last(1)

                head = lax.broadcasted_iota(jnp.int32, (1, part), 1) // HEAD_DIM
                mine_f = jnp.where(head == h, 1.0, 0.0)
                mine = mine_f.astype(jnp.bfloat16)
                other = (1.0 - mine_f).astype(jnp.bfloat16)
                for b in range(half):
                    at = n * half + b
                    q = q_s[at, hf] * mine
                    s = jnp.dot(q, kt_s[at], preferred_element_type=jnp.float32) + bf_s[h] + mb_s[at]
                    top = jnp.max(s, axis=1, keepdims=True)
                    p = jnp.exp2(((s - top) * (scale * LOG2E)).astype(jnp.bfloat16))
                    w = jnp.dot(p, v_s[at] * mine + other, preferred_element_type=jnp.float32)
                    mixed = w / pltpu.roll(w, HEAD_DIM, 1)
                    acc_s[b] = jnp.where(mine_f > 0.0, mixed, acc_s[b])
                return carry

            lax.fori_loop(0, heads, one_head, 0)

            def gate(b, carry):
                g = g_s[n * half + b, hf].astype(jnp.float32)
                gated = (acc_s[b] * jax.nn.sigmoid(g)).astype(jnp.bfloat16)
                for p in range(8):
                    for o in range(3):
                        at = (p * 3 + o) * sub
                        out_s[hf, n, p, b, o] = gated[at : at + sub]
                return carry

            lax.fori_loop(0, half, gate, 0)
            for j in range(8):
                p = (c + j) % 8
                src = out_s.at[hf, n, p]
                dst = o_ref.at[core, pl.ds(pl.multiple_of(c * half, half), half), :, hf]
                arrived = recv.at[hf * 16 + c * 2 + core]
                row = jnp.where(n == 0, r, partner[0])
                cp = remote(src, dst, send.at[(hf * 2 + n) * 8 + p], arrived, (row, p))
                if j == 0:

                    @pl.when(n > 0)
                    def _():
                        cp.start()

                    @pl.when(n == 0)
                    def _():
                        pltpu.make_async_copy(src, dst, arrived).start()
                else:
                    cp.start()
            return carry

        return lax.fori_loop(0, 2, group, carry)

    lax.fori_loop(0, 2, block_of_rows, 0)

    for hf in range(2):
        for cs in range(8):
            for k in range(2):
                pltpu.make_async_copy(
                    out_s.at[0, 0, 0], o_ref.at[k, pl.ds(cs * half, half), :, hf], recv.at[hf * 16 + cs * 2 + k]
                ).wait()
        for n in range(2):
            for j in range(8):
                p = (c + j) % 8
                if n == 0 and j == 0:
                    continue
                row = r if n == 0 else partner[0]
                remote(
                    out_s.at[hf, n, p], o_ref.at[core, pl.ds(pl.multiple_of(c * half, half), half), :, hf],
                    send.at[(hf * 2 + n) * 8 + p], recv.at[0], (row, p),
                ).wait_send()
        for o in range(3):
            for d in range(1, 4):
                one(hf, o, d).wait_send()
                two(hf, o, d).wait_send()
                for e in range(4):
                    three(hf, o, e, d).wait_send()
    swap.wait_send()
    xs.wait_send()
    ms.wait_send()


def attention(tile, emb, near, far, mask, gain, w):
    home, cols, channels = emb.shape
    half, length = home // 8, 8 * cols
    seqs = 2 * half
    lanes = w.shape[1] // 8
    heads = lanes // HEAD_DIM
    rows = length // 2
    sub = cols // 6
    vmem = pl.BlockSpec(memory_space=pltpu.VMEM)
    hbm = pl.BlockSpec(memory_space=pl.ANY)
    dma = pltpu.SemaphoreType.DMA
    table = pltpu.VMEM((2, 4, 4, 4, sub, tile.shape[1] // 2), jnp.bfloat16)
    out = pl.pallas_call(
        attn_kernel,
        out_shape=jax.ShapeDtypeStruct((2, home, 3, 2, sub, lanes), jnp.bfloat16),
        in_specs=[vmem, hbm, hbm, hbm, vmem, vmem, vmem],
        out_specs=hbm,
        scratch_shapes=[
            pltpu.VMEM((channels, 4 * lanes), jnp.bfloat16),
            pltpu.VMEM((2 * tile.shape[0], tile.shape[1] // 2), jnp.bfloat16),
            table, table, table,
            pltpu.VMEM((2, half, length, channels), jnp.bfloat16),
            pltpu.VMEM((2,) + mask.shape, jnp.float32),
            pltpu.VMEM((seqs, 1, length), jnp.float32),
            pltpu.VMEM((seqs, 2, rows, lanes), jnp.bfloat16),
            pltpu.VMEM((seqs, lanes, length), jnp.bfloat16),
            pltpu.VMEM((seqs, length, lanes), jnp.bfloat16),
            pltpu.VMEM((seqs, 2, rows, lanes), jnp.bfloat16),
            pltpu.VMEM((heads, rows, length), jnp.float32),
            pltpu.VMEM((half, rows, lanes), jnp.float32),
            pltpu.VMEM((2, 2, 8, half, 3, sub, lanes), jnp.bfloat16),
            dma((8,)), dma((3,)), dma((3,)), dma((3,)), dma((6,)),
            dma((24,)), dma((24,)), dma((24,)), dma((24,)), dma((96,)), dma((96,)),
            dma((32,)), dma((32,)),
        ],
        compiler_params=pltpu.CompilerParams(
            vmem_limit_bytes=56 << 20, collective_id=3, has_side_effects=True
        ),
        name="attn",
    )(tile, emb, near, far, mask, gain.reshape(1, channels), w)
    return out.reshape(2, home, cols, lanes)


def opm_kernel(left_ref, lmask_ref, right_ref, rrow_ref, rcol_ref, pair_ref, gain_ref, w_ref, wd_ref, x_ref, mk_ref,
               out_ref, bias_ref, x_out, m_out, rt_s, wb_s, m_s, f_s, b_s, xsend, xrecv, msend, mrecv):
    step = pl.program_id(0)
    r, c = place()
    opm = w_ref.shape[0]
    per, cols = out_ref.shape[0], out_ref.shape[1]
    steps = f_s.shape[0]
    heads = wd_ref.shape[0]
    group = per // 4
    chunk = 4 * cols
    half = x_out.shape[1]
    width = cols * opm

    def move(d):
        to = ((c // 2 + d) % 4) * 2 + 1 - c % 2
        block = pl.ds(pl.multiple_of(to * half, half), half)
        return remote(x_ref.at[block], x_out.at[c // 2], xsend.at[d], xrecv.at[d], (r, to))

    def note(d):
        to = (c + d) % 8
        return remote(mk_ref.at[to], m_out.at[c], msend.at[d], mrecv.at[d], (r, to))

    def kept():
        return pltpu.make_async_copy(mk_ref.at[c], m_out.at[c], mrecv.at[0])

    @pl.when(step == 0)
    def _():
        barrier = pltpu.get_barrier_semaphore()
        for d in range(1, 8):
            signal(barrier, (r, (c + d) % 8))
        pl.semaphore_wait(barrier, 7)
        for d in (0, 1, 3, 2):
            move(d).start()
        for d in range(1, 8):
            note(d).start()
        kept().start()
        wb_s[...] = jnp.zeros_like(wb_s)

        def fill(b, carry):
            for i in range(2):
                wb_s[pl.ds(pl.multiple_of(b * 64 + i * 32, 32), 32), i * 128 : (i + 1) * 128] = w_ref[b]
            return carry

        lax.fori_loop(0, opm, fill, 0)

        def flip(n, carry):
            at = pl.multiple_of(n * chunk, chunk)
            rt_s[pl.ds(at, chunk), :] = right_ref[:, pl.ds(at, chunk)].T
            return carry

        lax.fori_loop(0, opm // 4, flip, 0)
        counts = lax.dot_general(
            right_ref[:, width:], lmask_ref[...], CONTRACT_FIRST, preferred_element_type=jnp.float32
        )[:cols, : steps * per]
        factor = rcol_ref[...] * rrow_ref[...] / (counts + 0.001)
        for n in range(steps):
            f_s[n] = factor[:, n * per : (n + 1) * per]

    def outer(n, carry):
        at = pl.multiple_of(n * chunk, chunk)
        m = jnp.dot(rt_s[pl.ds(at, chunk), :], left_ref[...], preferred_element_type=jnp.float32)
        low = lax.broadcasted_iota(jnp.int32, (1, 128), 1) < 64
        for bb in range(2):
            lanes = pl.ds(pl.multiple_of((n * 2 + bb) * 128, 128), 128)
            for g in range(group):
                m0, m1 = [
                    m[(2 * bb + k) * cols : (2 * bb + k + 1) * cols, g * 128 : (g + 1) * 128] for k in range(2)
                ]
                one = jnp.where(low, m0, pltpu.roll(m1, 64, 1)).astype(jnp.bfloat16)
                two = jnp.where(low, pltpu.roll(m0, 64, 1), m1).astype(jnp.bfloat16)
                m_s[(2 * g) * cols : (2 * g + 1) * cols, lanes] = one
                m_s[(2 * g + 1) * cols : (2 * g + 2) * cols, lanes] = two
        return carry

    lax.fori_loop(0, opm // 4, outer, 0)
    factor = f_s[step]
    update = jnp.dot(m_s[...], wb_s[...], preferred_element_type=jnp.float32)
    for g in range(2 * group):
        for ii in range(2):
            i = 2 * g + ii
            u = update[g * cols : (g + 1) * cols, ii * 128 : (ii + 1) * 128]
            x = pair_ref[i] + u * factor[:, i : i + 1]
            out_ref[i] = x
            x = (standardize_features(x) * gain_ref[...]).astype(jnp.bfloat16)
            b_s[:, i, :] = lax.dot_general(wd_ref[...], x, LAST_LAST, preferred_element_type=jnp.float32)
    bias_ref[...] = jnp.concatenate([b_s[h] for h in range(heads)], axis=1).astype(jnp.bfloat16)

    @pl.when(step == steps - 1)
    def _():
        for d in range(4):
            move(d).wait()
        for d in range(1, 8):
            note(d).wait()
        kept().wait()


def opm(left, right, rrow, rcol, pair, gain, kron, logit, x, mk):
    rows, cols, channels = pair.shape
    seqs = left.shape[0]
    heads = logit.shape[1]
    per = 16
    steps = rows // per
    width = kron.shape[0] // 32
    rr = rrow.reshape(1, rows)
    rc = rcol.reshape(cols, 1)
    w = kron.reshape(width, width, channels).transpose(1, 0, 2)
    gain = gain.reshape(1, channels)
    wd = logit.T
    whole = lambda a: pl.BlockSpec(a.shape, lambda i: (0,) * a.ndim, pipeline_mode=pl.Buffered(1))
    hbm = pl.BlockSpec(memory_space=pl.ANY)
    dma = pltpu.SemaphoreType.DMA
    return pl.pallas_call(
        opm_kernel,
        grid=(steps,),
        out_shape=(
            jax.ShapeDtypeStruct(pair.shape, jnp.float32),
            jax.ShapeDtypeStruct((rows, heads * cols), jnp.bfloat16),
            jax.ShapeDtypeStruct((4, x.shape[0] // 8) + x.shape[1:], jnp.bfloat16),
            jax.ShapeDtypeStruct(mk.shape, mk.dtype),
        ),
        in_specs=[
            pl.BlockSpec((seqs, per * width), lambda i: (0, i)),
            pl.BlockSpec((seqs, 128), lambda i: (0, rows * width // 128)),
            whole(right), whole(rr), whole(rc),
            pl.BlockSpec((per, cols, channels), lambda i: (i, 0, 0)),
            whole(gain), whole(w), whole(wd), hbm, whole(mk),
        ],
        out_specs=(
            pl.BlockSpec((per, cols, channels), lambda i: (i, 0, 0)),
            pl.BlockSpec((per, heads * cols), lambda i: (i, 0)),
            hbm, hbm,
        ),
        scratch_shapes=[
            pltpu.VMEM((cols * width, seqs), jnp.bfloat16),
            pltpu.VMEM((64 * width, 2 * channels), jnp.bfloat16),
            pltpu.VMEM((per // 2 * cols, 64 * width), jnp.bfloat16),
            pltpu.VMEM((steps, cols, per), jnp.float32),
            pltpu.VMEM((heads, per, cols), jnp.float32),
            dma((8,)), dma((8,)), dma((8,)), dma((8,)),
        ],
        compiler_params=pltpu.CompilerParams(
            vmem_limit_bytes=52 << 20, collective_id=2, has_side_effects=True
        ),
        name="opm",
    )(left, left, right, rr, rc, pair, gain, w, wd, x, mk)


def shards(
    aligned_family_embedding,
    aligned_slot_available,
    chain_site_available,
    duo_embedding,
    averaging_layernorm_stretch,
    lineup_layernorm_stretch,
    duo_layernorm_stretch,
    lefthand_linear_kernel,
    righthand_linear_kernel,
    kronecker_linear_kernel,
    duo_logit_kernel,
    asker_lookup_sigmoid_kernel,
    closing_linear_kernel,
):
    homolog_number, amino_position_number, discarded_carry = aligned_family_embedding.shape
    res_rows = duo_embedding.shape[0]
    opm_width = lefthand_linear_kernel.shape[1]
    head_count = duo_logit_kernel.shape[1]
    inner_width = closing_linear_kernel.shape[0]
    row_index = lax.axis_index("row")
    col_index = lax.axis_index("col")
    standardized_features = standardize_features(aligned_family_embedding.astype(jnp.float32))
    availability_real = aligned_slot_available.astype(jnp.float32)
    half_rows = res_rows
    opm_input = (standardized_features * averaging_layernorm_stretch).astype(jnp.bfloat16)
    left = jnp.einsum("src,ca->sra", opm_input, lefthand_linear_kernel, preferred_element_type=jnp.float32)
    left = (left * availability_real[:, :, None]).astype(jnp.bfloat16)
    left = left.reshape(homolog_number, 2, half_rows * opm_width).transpose(1, 0, 2)
    left_mask = availability_real.reshape(homolog_number, 2, half_rows).transpose(1, 0, 2)
    left_mask = jnp.pad(left_mask, ((0, 0), (0, 0), (0, 128 - half_rows))).astype(jnp.bfloat16)
    left = jnp.concatenate([left, left_mask], axis=2)
    right = jnp.einsum("src,ca->sar", opm_input, righthand_linear_kernel, preferred_element_type=jnp.float32)
    right = (right * availability_real[:, None, :]).astype(jnp.bfloat16)
    right_mask = jnp.pad(availability_real, ((0, 0), (0, 128 - amino_position_number))).astype(jnp.bfloat16)
    right = jnp.concatenate([right.reshape(homolog_number, -1), right_mask], axis=1)
    mask_out = jnp.pad(
        availability_real.reshape(8, homolog_number // 8, amino_position_number),
        ((0, 0), (0, 8 - homolog_number // 8), (0, 128 - amino_position_number)),
    )
    left_all, right_all, near_rows = spread(left, right, aligned_family_embedding)
    residue_float = chain_site_available.astype(jnp.float32)
    residue_rows = lax.dynamic_slice_in_dim(residue_float, row_index * res_rows, res_rows)
    residue_cols = lax.dynamic_slice_in_dim(
        residue_float, col_index * amino_position_number, amino_position_number
    )
    duo_after_averaging, bias_tile, far_rows, own_mask = opm(
        left_all, right_all, residue_rows, residue_cols, duo_embedding,
        duo_layernorm_stretch, kronecker_linear_kernel, duo_logit_kernel, aligned_family_embedding, mask_out,
    )
    lanes = inner_width // 2
    gated = attention(
        bias_tile, aligned_family_embedding, near_rows, far_rows, own_mask, lineup_layernorm_stretch,
        asker_lookup_sigmoid_kernel,
    )
    closing = closing_linear_kernel.reshape(2, lanes, -1)
    summed_increment = jnp.einsum("hsqd,hdc->sqc", gated, closing, preferred_element_type=jnp.float32)
    refreshed_family_embedding = (
        aligned_family_embedding.astype(jnp.float32) + summed_increment
    ).astype(jnp.bfloat16)
    return (refreshed_family_embedding, duo_after_averaging)


def solution(mesh):
    placed = (
        P("row", "col", None),
        P("row", "col"),
        P(),
        P("row", "col", None),
        P(),
        P(),
        P(),
        P(),
        P(),
        P(),
        P(),
        P(),
        P(),
    )
    return jax.shard_map(
        shards,
        mesh=mesh,
        in_specs=placed,
        out_specs=(P("row", "col", None), P("row", "col", None)),
        check_vma=False,
    )
```

```python
import jax
import jax.numpy as jnp
from jax import lax
from jax.experimental import pallas as pl
from jax.experimental.pallas import tpu as pltpu
from jax.sharding import PartitionSpec as P

EPSILON = 1e-05
CONTRACT_FIRST = (((0,), (0,)), ((), ()))
LAST_LAST = (((1,), (1,)), ((), ()))
HEAD_DIM = 32


def standardize_features(values):
    average = jnp.mean(values, axis=-1, keepdims=True)
    centred = values - average
    variance = jnp.mean(centred * centred, axis=-1, keepdims=True)
    return centred * lax.rsqrt(variance + EPSILON)


MESH = pl.DeviceIdType.MESH


def place():
    r, c = lax.axis_index("row"), lax.axis_index("col")
    return r, c


def row_of(y, zh, core):
    return y * 4 + zh * 2 + core


def remote(src, dst, send, recv, device):
    return pltpu.make_async_remote_copy(
        src_ref=src, dst_ref=dst, send_sem=send, recv_sem=recv, device_id=device, device_id_type=MESH
    )


def signal(barrier, device):
    pl.semaphore_signal(barrier, inc=1, device_id=device, device_id_type=MESH)


def spread_kernel(left_ref, right_ref, emb_ref, left_out, right_out, x_out, xsend, xrecv, lsend, lrecv, gsend, zsend, zrecv, ysend, yrecv, fsend,
                  frecv, own_sem):
    r, c = place()
    chip, core = r // 2, r % 2
    y, zh, x, zl = r // 4, chip % 2, c // 2, c % 2
    seqs = right_ref.shape[0]

    def rows(n):
        return pl.ds(pl.multiple_of(n * seqs, seqs), seqs)

    here = rows(r)
    partner = (chip * 2 + 1 - core, c)
    across = (row_of(y, 1 - zh, core), c)
    aside = (r, x * 2 + 1 - zl)
    mine = jnp.logical_and(chip == c, zh == zl)

    def own_left(h, j):
        return jnp.logical_and(mine, core == h) if j == 0 else False

    def unless(cond, f):
        if cond is False:
            f()
        else:
            pl.when(jnp.logical_not(cond))(f)

    barrier = pltpu.get_barrier_semaphore()
    signal(barrier, partner)
    signal(barrier, across)
    signal(barrier, aside)
    for d in range(1, 4):
        signal(barrier, (row_of((y + d) % 4, zh, core), c))
    for ys in range(4):
        for k in range(2):
            source = row_of(ys, zl, k)
            unless(jnp.logical_and(mine, r == source), lambda: signal(barrier, (source, chip)))
    for d in range(1, 4):
        signal(barrier, (r, ((x + d) % 4) * 2 + zl))
    pl.semaphore_wait(barrier, 17 - mine.astype(jnp.int32))
    half = x_out.shape[1]

    def move(d):
        xd = (x + d) % 4
        take = pl.ds(pl.multiple_of((xd * 2 + zl) * half, half), half)
        return remote(emb_ref.at[take], x_out.at[x], xsend.at[d], xrecv.at[d], (r, xd * 2 + zl))


    over = remote(right_ref, right_out.at[here], zsend.at[0], zrecv.at[0], across)
    over.start()
    sends = [over]
    lefts = []
    for j in range(4):
        for h in range(2):
            to = (2 * c + h, ((x + j) % 4) * 2 + zh)
            cp = remote(left_ref.at[h], left_out.at[here], lsend.at[2 * j + h], lrecv.at[r], to)
            lefts.append((cp, h, j))
            unless(own_left(h, j), cp.start)
            if j == 0:

                @pl.when(own_left(h, j))
                def _():
                    pltpu.make_async_copy(left_ref.at[h], left_out.at[here], lrecv.at[r]).start()

    def along(n, d):
        if d == 2:
            turn = 1 if n == 0 else 3
            block = right_out.at[rows(row_of((y + 4 - turn) % 4, (zh + n) % 2, core))]
            at = n * 4 + d
            return remote(block, block, ysend.at[at], yrecv.at[at], (row_of((y + turn) % 4, zh, core), c))
        block = rows(row_of(y, (zh + n) % 2, core))
        src = right_ref if n == 0 else right_out.at[block]
        return remote(src, right_out.at[block], ysend.at[n * 4 + d], yrecv.at[n * 4 + d], (row_of((y + d) % 4, zh, core), c))

    def forward(n, d):
        block = rows(row_of((y + 4 - d) % 4, (zh + n) % 2, core))
        src = right_ref if n == 0 and d == 0 else right_out.at[block]
        return remote(src, right_out.at[block], fsend.at[n * 4 + d], frecv.at[n * 4 + d], partner)

    for d in (1, 3):
        along(0, d).start()
    own = pltpu.make_async_copy(right_ref, right_out.at[here], own_sem.at[0])
    own.start()
    forward(0, 0).start()
    for d in (1, 3, 2):
        move(d).start()
    over.wait_recv()
    for d in (3, 1):
        along(1, d).start()
    forward(1, 0).start()

    def relay(d, k):
        source = row_of((y + 4 - d) % 4, zl, k)
        block = left_out.at[rows(source)]
        return block, source, remote(block, block, gsend.at[d * 2 + k], lrecv.at[source], aside)

    def pass_left(d):
        for k in range(2):
            block, source, cp = relay(d, k)
            pltpu.make_async_copy(left_ref.at[0], block, lrecv.at[source]).wait()
            cp.start()

    def pass_right(n, d):
        along(n, d).wait_recv()
        if (n, d) in ((0, 1), (1, 3)):
            along(n, 2).start()
        forward(n, d).start()

    pass_left(0)
    pass_right(0, 1)
    pass_left(1)
    pass_right(0, 3)
    pass_right(1, 3)
    pass_left(3)
    pass_right(1, 1)
    pass_left(2)
    pass_right(0, 2)
    pass_right(1, 2)
    for ys in range(4):
        for k in range(2):
            source = row_of(ys, 1 - zl, k)
            pltpu.make_async_copy(left_ref.at[0], left_out.at[rows(source)], lrecv.at[source]).wait()
    own.wait()
    for n in range(2):
        for d in range(4):
            forward(n, d).wait()
            if d > 0:
                along(n, d).wait_send()
    over.wait_send()
    for d in range(1, 4):
        move(d).wait()
    for cp, h, j in lefts:
        unless(own_left(h, j), cp.wait_send)
    for d in range(4):
        for k in range(2):
            relay(d, k)[2].wait_send()


def spread(left, right, emb):
    seqs = right.shape[0]
    vmem = pl.BlockSpec(memory_space=pltpu.VMEM)
    hbm = pl.BlockSpec(memory_space=pl.ANY)
    dma = pltpu.SemaphoreType.DMA
    return pl.pallas_call(
        spread_kernel,
        out_shape=(
            jax.ShapeDtypeStruct((16 * seqs, left.shape[2]), jnp.bfloat16),
            jax.ShapeDtypeStruct((16 * seqs, right.shape[1]), jnp.bfloat16),
            jax.ShapeDtypeStruct((4, seqs // 8) + emb.shape[1:], jnp.bfloat16),
        ),
        in_specs=[vmem, vmem, hbm],
        out_specs=(hbm, hbm, hbm),
        scratch_shapes=[
            dma((4,)), dma((4,)),
            dma((8,)), dma((16,)), dma((8,)), dma((1,)), dma((1,)), dma((8,)), dma((8,)), dma((8,)), dma((8,)), dma((1,))
        ],
        compiler_params=pltpu.CompilerParams(collective_id=1, has_side_effects=True),
        name="spread",
    )(left, right, emb)


LOG2E = 1.4426950408889634


def attn_kernel(tile_ref, emb_ref, near_ref, far_ref, mask_ref, gain_ref, w_ref, o_ref, w_s, block, ta, tb, tc, x_s, m_s, mb_s, q_s, kt_s, v_s, g_s, bf_s, acc_s, out_s,
                lsem, csem, csend, crecv, l1, s1, r1, s2, r2, s3, r3, send, recv):
    r, c = place()
    chip, core = r // 2, r % 2
    spot = {"x": c // 2, "y": r // 4, "z": (chip % 2) * 2 + c % 2}
    half, length = x_s.shape[1], x_s.shape[2]
    heads, rows = bf_s.shape[0], bf_s.shape[1]
    cols = length // 8
    sub = cols // 6
    scale = float(HEAD_DIM) ** -0.5
    partner = (chip * 2 + 1 - core, c)
    orders = ((ta, "xzy"), (tb, "yxz"), (tc, "zyx"))

    def peer(dim, d):
        to = dict(spot)
        to[dim] = (spot[dim] + d) % 4
        return (row_of(to["y"], to["z"] // 2, core), to["x"] * 2 + to["z"] % 2)

    barrier = pltpu.get_barrier_semaphore()
    signal(barrier, partner)
    for dim in "xyz":
        for d in range(1, 4):
            signal(barrier, peer(dim, d))
    for j in range(8):
        if j > 0:
            signal(barrier, (r, (c + j) % 8))
        signal(barrier, (partner[0], (c + j) % 8))

    trows, lanes = tile_ref.shape[0], tile_ref.shape[1] // 2
    here = pl.ds(pl.multiple_of(core * trows, trows), trows)
    give = tile_ref.at[:, pl.ds(pl.multiple_of((1 - core) * lanes, lanes), lanes)]
    keep = tile_ref.at[:, pl.ds(pl.multiple_of(core * lanes, lanes), lanes)]
    own = pltpu.make_async_copy(keep, block.at[here], csem.at[0])
    own.start()
    locals_ = []
    for d in range(8):
        xd, zd = (c // 2 + d // 2) % 4, (c + d) % 2
        if d == 0:
            src = emb_ref.at[pl.ds(pl.multiple_of(c * half, half), half)]
        else:
            src = (far_ref if d % 2 else near_ref).at[xd]
        spot_cols = pl.ds(pl.multiple_of((xd * 2 + zd) * cols, cols), cols)
        locals_.append(pltpu.make_async_copy(src, x_s.at[0, :, spot_cols], lsem.at[d]))
        locals_[d].start()
    ml = pltpu.make_async_copy(mask_ref, m_s.at[0], csem.at[2])
    ml.start()
    pl.semaphore_wait(barrier, 25)
    swap = remote(give, block.at[here], csend.at[0], crecv.at[0], partner)
    swap.start()
    xs = remote(x_s.at[0], x_s.at[1], csend.at[1], crecv.at[1], partner)
    ms = remote(mask_ref, m_s.at[1], csend.at[2], crecv.at[2], partner)
    own.wait()
    swap.wait_recv()

    def one(hf, o, d):
        out, dims = orders[o]
        slot = out.at[hf, spot[dims[2]], spot[dims[1]], spot[dims[0]]]
        piece = block.at[pl.ds(o * 2 * sub + hf * sub, sub)]
        if d == 0:
            return pltpu.make_async_copy(piece, slot, l1.at[hf * 3 + o])
        at = (hf * 3 + o) * 4 + d
        return remote(piece, slot, s1.at[at], r1.at[at], peer(dims[0], d))

    def two(hf, o, d):
        out, dims = orders[o]
        slot = out.at[hf, spot[dims[2]], spot[dims[1]]]
        at = (hf * 3 + o) * 4 + d
        return remote(slot, slot, s2.at[at], r2.at[at], peer(dims[1], d))

    def three(hf, o, e, d):
        out, dims = orders[o]
        slot = out.at[hf, spot[dims[2]], (spot[dims[1]] + 4 - e) % 4]
        at = (hf * 3 + o) * 16 + e * 4 + d
        return remote(slot, slot, s3.at[at], r3.at[at], peer(dims[2], d))

    def middle(hf):
        for o in range(3):
            for d in range(4):
                if d == 0:
                    one(hf, o, d).wait()
                else:
                    one(hf, o, d).wait_recv()
            for d in range(1, 4):
                two(hf, o, d).start()
            for d in range(1, 4):
                three(hf, o, 0, d).start()

    def last(hf):
        for e in range(1, 4):
            for o in range(3):
                two(hf, o, e).wait_recv()
                for d in range(1, 4):
                    three(hf, o, e, d).start()

    for hf in range(2):
        for o in range(3):
            for d in range(4):
                one(hf, o, d).start()
    for cp in locals_:
        cp.wait()
    xs.start()
    ms.start()

    width = w_ref.shape[1] // 4
    part = w_s.shape[1] // 4
    for n in range(4):
        w_s[:, n * part : (n + 1) * part] = w_ref[:, pl.ds(pl.multiple_of(n * width + core * part, part), part)]

    def project(n, lo, hi):
        def body(b, carry):
            x = standardize_features(x_s[n, b].astype(jnp.float32))
            x = (x * gain_ref[...]).astype(jnp.bfloat16)
            at = n * half + b
            both = jnp.dot(x, w_s[...], preferred_element_type=jnp.float32).astype(jnp.bfloat16)
            p, k, v, g = [both[:, i * part : (i + 1) * part] for i in range(4)]
            for hf in range(2):
                q_s[at, hf] = jnp.concatenate(
                    [p[(2 * i + hf) * sub : (2 * i + hf + 1) * sub] for i in range(rows // sub)], axis=0
                )
                g_s[at, hf] = jnp.concatenate(
                    [g[(2 * i + hf) * sub : (2 * i + hf + 1) * sub] for i in range(rows // sub)], axis=0
                )
            v_s[at] = v
            kt_s[at] = k.T
            return carry

        lax.fori_loop(lo, hi, body, 0, unroll=2)

    def mask_lines(n):
        for b in range(half):
            line = jnp.concatenate([m_s[n, cc, b : b + 1, :cols] for cc in range(8)], axis=1)
            mb_s[n * half + b] = (1e9 / scale) * (line - 1.0)

    project(0, 0, 2)
    middle(0)
    project(0, 2, half)
    last(0)
    middle(1)
    ml.wait()
    mask_lines(0)
    xs.wait_recv()
    ms.wait_recv()
    mask_lines(1)
    project(1, 0, half)

    def block_of_rows(hf, carry):
        for o in range(3):
            for e in range(4):
                for d in range(1, 4):
                    out, dims = orders[o]
                    at = (hf * 3 + o) * 16 + e * 4 + d
                    slot = out.at[hf, (spot[dims[2]] + 4 - d) % 4, (spot[dims[1]] + 4 - e) % 4]
                    remote(slot, slot, s3.at[at], r3.at[at], peer(dims[2], d)).wait_recv()

        def assemble(p, carry):
            y, zh = p // 2, p % 2
            for o in range(3):
                pieces = []
                for cc in range(8):
                    x, z = cc // 2, zh * 2 + cc % 2
                    if o == 0:
                        piece = ta[hf, y, z, x]
                    elif o == 1:
                        piece = tb[hf, z, x, y]
                    else:
                        piece = tc[hf, x, y, z]
                    pieces.append(piece)
                for h in range(heads):
                    line = jnp.concatenate([piece[:, h * cols : (h + 1) * cols] for piece in pieces], axis=1)
                    bf_s[h, pl.ds(pl.multiple_of(p * 3 * sub + o * sub, sub), sub), :] = line.astype(jnp.float32) * (
                        1.0 / scale
                    )
            return carry

        lax.fori_loop(0, 8, assemble, 0)

        def group(n, carry):
            def one_head(h, carry):
                @pl.when(jnp.logical_and(hf == 0, jnp.logical_and(n == 0, h == 1)))
                def _():
                    last(1)

                head = lax.broadcasted_iota(jnp.int32, (1, part), 1) // HEAD_DIM
                mine_f = jnp.where(head == h, 1.0, 0.0)
                mine = mine_f.astype(jnp.bfloat16)
                other = (1.0 - mine_f).astype(jnp.bfloat16)
                for b in range(half):
                    at = n * half + b
                    q = q_s[at, hf] * mine
                    s = jnp.dot(q, kt_s[at], preferred_element_type=jnp.float32) + bf_s[h] + mb_s[at]
                    top = jnp.max(s, axis=1, keepdims=True)
                    p = jnp.exp2(((s - top) * (scale * LOG2E)).astype(jnp.bfloat16))
                    w = jnp.dot(p, v_s[at] * mine + other, preferred_element_type=jnp.float32)
                    mixed = w / pltpu.roll(w, HEAD_DIM, 1)
                    acc_s[b] = jnp.where(mine_f > 0.0, mixed, acc_s[b])
                return carry

            lax.fori_loop(0, heads, one_head, 0)

            def gate(b, carry):
                g = g_s[n * half + b, hf].astype(jnp.float32)
                gated = (acc_s[b] * jax.nn.sigmoid(g)).astype(jnp.bfloat16)
                for p in range(8):
                    for o in range(3):
                        at = (p * 3 + o) * sub
                        out_s[hf, n, p, b, o] = gated[at : at + sub]
                return carry

            lax.fori_loop(0, half, gate, 0)
            for j in range(8):
                p = (c + j) % 8
                src = out_s.at[hf, n, p]
                dst = o_ref.at[core, pl.ds(pl.multiple_of(c * half, half), half), :, hf]
                arrived = recv.at[hf * 16 + c * 2 + core]
                row = jnp.where(n == 0, r, partner[0])
                cp = remote(src, dst, send.at[(hf * 2 + n) * 8 + p], arrived, (row, p))
                if j == 0:

                    @pl.when(n > 0)
                    def _():
                        cp.start()

                    @pl.when(n == 0)
                    def _():
                        pltpu.make_async_copy(src, dst, arrived).start()
                else:
                    cp.start()
            return carry

        return lax.fori_loop(0, 2, group, carry)

    lax.fori_loop(0, 2, block_of_rows, 0)

    for hf in range(2):
        for cs in range(8):
            for k in range(2):
                pltpu.make_async_copy(
                    out_s.at[0, 0, 0], o_ref.at[k, pl.ds(cs * half, half), :, hf], recv.at[hf * 16 + cs * 2 + k]
                ).wait()
        for n in range(2):
            for j in range(8):
                p = (c + j) % 8
                if n == 0 and j == 0:
                    continue
                row = r if n == 0 else partner[0]
                remote(
                    out_s.at[hf, n, p], o_ref.at[core, pl.ds(pl.multiple_of(c * half, half), half), :, hf],
                    send.at[(hf * 2 + n) * 8 + p], recv.at[0], (row, p),
                ).wait_send()
        for o in range(3):
            for d in range(1, 4):
                one(hf, o, d).wait_send()
                two(hf, o, d).wait_send()
                for e in range(4):
                    three(hf, o, e, d).wait_send()
    swap.wait_send()
    xs.wait_send()
    ms.wait_send()


def attention(tile, emb, near, far, mask, gain, w):
    home, cols, channels = emb.shape
    half, length = home // 8, 8 * cols
    seqs = 2 * half
    lanes = w.shape[1] // 8
    heads = lanes // HEAD_DIM
    rows = length // 2
    sub = cols // 6
    vmem = pl.BlockSpec(memory_space=pltpu.VMEM)
    hbm = pl.BlockSpec(memory_space=pl.ANY)
    dma = pltpu.SemaphoreType.DMA
    table = pltpu.VMEM((2, 4, 4, 4, sub, tile.shape[1] // 2), jnp.bfloat16)
    out = pl.pallas_call(
        attn_kernel,
        out_shape=jax.ShapeDtypeStruct((2, home, 3, 2, sub, lanes), jnp.bfloat16),
        in_specs=[hbm, hbm, hbm, hbm, hbm, vmem, vmem],
        out_specs=hbm,
        scratch_shapes=[
            pltpu.VMEM((channels, 4 * lanes), jnp.bfloat16),
            pltpu.VMEM((2 * tile.shape[0], tile.shape[1] // 2), jnp.bfloat16),
            table, table, table,
            pltpu.VMEM((2, half, length, channels), jnp.bfloat16),
            pltpu.VMEM((2,) + mask.shape, jnp.float32),
            pltpu.VMEM((seqs, 1, length), jnp.float32),
            pltpu.VMEM((seqs, 2, rows, lanes), jnp.bfloat16),
            pltpu.VMEM((seqs, lanes, length), jnp.bfloat16),
            pltpu.VMEM((seqs, length, lanes), jnp.bfloat16),
            pltpu.VMEM((seqs, 2, rows, lanes), jnp.bfloat16),
            pltpu.VMEM((heads, rows, length), jnp.float32),
            pltpu.VMEM((half, rows, lanes), jnp.float32),
            pltpu.VMEM((2, 2, 8, half, 3, sub, lanes), jnp.bfloat16),
            dma((8,)), dma((3,)), dma((3,)), dma((3,)), dma((6,)),
            dma((24,)), dma((24,)), dma((24,)), dma((24,)), dma((96,)), dma((96,)),
            dma((32,)), dma((32,)),
        ],
        compiler_params=pltpu.CompilerParams(
            vmem_limit_bytes=56 << 20, collective_id=3, has_side_effects=True
        ),
        name="attn",
    )(tile, emb, near, far, mask, gain.reshape(1, channels), w)
    return out.reshape(2, home, cols, lanes)


def opm_kernel(left_ref, lmask_ref, right_ref, rrow_ref, rcol_ref, pair_ref, gain_ref, w_ref, wd_ref, x_ref, mk_ref,
               out_ref, bias_ref, x_out, m_out, rt_s, wb_s, m_s, f_s, b_s, xsend, xrecv, msend, mrecv):
    step = pl.program_id(0)
    r, c = place()
    opm = w_ref.shape[0]
    per, cols = out_ref.shape[0], out_ref.shape[1]
    steps = f_s.shape[0]
    heads = wd_ref.shape[0]
    group = per // 4
    chunk = 4 * cols
    half = x_out.shape[1]
    width = cols * opm

    def move(d):
        to = ((c // 2 + d) % 4) * 2 + 1 - c % 2
        block = pl.ds(pl.multiple_of(to * half, half), half)
        return remote(x_ref.at[block], x_out.at[c // 2], xsend.at[d], xrecv.at[d], (r, to))

    def note(d):
        to = (c + d) % 8
        return remote(mk_ref.at[to], m_out.at[c], msend.at[d], mrecv.at[d], (r, to))

    def kept():
        return pltpu.make_async_copy(mk_ref.at[c], m_out.at[c], mrecv.at[0])

    @pl.when(step == 0)
    def _():
        barrier = pltpu.get_barrier_semaphore()
        for d in range(1, 8):
            signal(barrier, (r, (c + d) % 8))
        pl.semaphore_wait(barrier, 7)
        for d in (0, 1, 3, 2):
            move(d).start()
        for d in range(1, 8):
            note(d).start()
        kept().start()
        wb_s[...] = jnp.zeros_like(wb_s)

        def fill(b, carry):
            for i in range(2):
                wb_s[pl.ds(pl.multiple_of(b * 64 + i * 32, 32), 32), i * 128 : (i + 1) * 128] = w_ref[b]
            return carry

        lax.fori_loop(0, opm, fill, 0)

        def flip(n, carry):
            at = pl.multiple_of(n * chunk, chunk)
            rt_s[pl.ds(at, chunk), :] = right_ref[:, pl.ds(at, chunk)].T
            return carry

        lax.fori_loop(0, opm // 4, flip, 0)
        counts = lax.dot_general(
            right_ref[:, width:], lmask_ref[...], CONTRACT_FIRST, preferred_element_type=jnp.float32
        )[:cols, : steps * per]
        factor = rcol_ref[...] * rrow_ref[...] / (counts + 0.001)
        for n in range(steps):
            f_s[n] = factor[:, n * per : (n + 1) * per]

    def outer(n, carry):
        at = pl.multiple_of(n * chunk, chunk)
        m = jnp.dot(rt_s[pl.ds(at, chunk), :], left_ref[...], preferred_element_type=jnp.float32)
        low = lax.broadcasted_iota(jnp.int32, (1, 128), 1) < 64
        for bb in range(2):
            lanes = pl.ds(pl.multiple_of((n * 2 + bb) * 128, 128), 128)
            for g in range(group):
                m0, m1 = [
                    m[(2 * bb + k) * cols : (2 * bb + k + 1) * cols, g * 128 : (g + 1) * 128] for k in range(2)
                ]
                one = jnp.where(low, m0, pltpu.roll(m1, 64, 1)).astype(jnp.bfloat16)
                two = jnp.where(low, pltpu.roll(m0, 64, 1), m1).astype(jnp.bfloat16)
                m_s[(2 * g) * cols : (2 * g + 1) * cols, lanes] = one
                m_s[(2 * g + 1) * cols : (2 * g + 2) * cols, lanes] = two
        return carry

    lax.fori_loop(0, opm // 4, outer, 0)
    factor = f_s[step]
    update = jnp.dot(m_s[...], wb_s[...], preferred_element_type=jnp.float32)
    for g in range(2 * group):
        for ii in range(2):
            i = 2 * g + ii
            u = update[g * cols : (g + 1) * cols, ii * 128 : (ii + 1) * 128]
            x = pair_ref[i] + u * factor[:, i : i + 1]
            out_ref[i] = x
            x = (standardize_features(x) * gain_ref[...]).astype(jnp.bfloat16)
            b_s[:, i, :] = lax.dot_general(wd_ref[...], x, LAST_LAST, preferred_element_type=jnp.float32)
    bias_ref[...] = jnp.concatenate([b_s[h] for h in range(heads)], axis=1).astype(jnp.bfloat16)

    @pl.when(step == steps - 1)
    def _():
        for d in range(4):
            move(d).wait()
        for d in range(1, 8):
            note(d).wait()
        kept().wait()


def opm(left, right, rrow, rcol, pair, gain, kron, logit, x, mk):
    rows, cols, channels = pair.shape
    seqs = left.shape[0]
    heads = logit.shape[1]
    per = 16
    steps = rows // per
    width = kron.shape[0] // 32
    rr = rrow.reshape(1, rows)
    rc = rcol.reshape(cols, 1)
    w = kron.reshape(width, width, channels).transpose(1, 0, 2)
    gain = gain.reshape(1, channels)
    wd = logit.T
    whole = lambda a: pl.BlockSpec(a.shape, lambda i: (0,) * a.ndim, pipeline_mode=pl.Buffered(1))
    hbm = pl.BlockSpec(memory_space=pl.ANY)
    dma = pltpu.SemaphoreType.DMA
    return pl.pallas_call(
        opm_kernel,
        grid=(steps,),
        out_shape=(
            jax.ShapeDtypeStruct(pair.shape, jnp.float32),
            jax.ShapeDtypeStruct((rows, heads * cols), jnp.bfloat16),
            jax.ShapeDtypeStruct((4, x.shape[0] // 8) + x.shape[1:], jnp.bfloat16),
            jax.ShapeDtypeStruct(mk.shape, mk.dtype),
        ),
        in_specs=[
            pl.BlockSpec((seqs, per * width), lambda i: (0, i)),
            pl.BlockSpec((seqs, 128), lambda i: (0, rows * width // 128)),
            whole(right), whole(rr), whole(rc),
            pl.BlockSpec((per, cols, channels), lambda i: (i, 0, 0)),
            whole(gain), whole(w), whole(wd), hbm, whole(mk),
        ],
        out_specs=(
            pl.BlockSpec((per, cols, channels), lambda i: (i, 0, 0)),
            pl.BlockSpec((per, heads * cols), lambda i: (i, 0)),
            hbm, hbm,
        ),
        scratch_shapes=[
            pltpu.VMEM((cols * width, seqs), jnp.bfloat16),
            pltpu.VMEM((64 * width, 2 * channels), jnp.bfloat16),
            pltpu.VMEM((per // 2 * cols, 64 * width), jnp.bfloat16),
            pltpu.VMEM((steps, cols, per), jnp.float32),
            pltpu.VMEM((heads, per, cols), jnp.float32),
            dma((8,)), dma((8,)), dma((8,)), dma((8,)),
        ],
        compiler_params=pltpu.CompilerParams(
            vmem_limit_bytes=52 << 20, collective_id=2, has_side_effects=True
        ),
        name="opm",
    )(left, left, right, rr, rc, pair, gain, w, wd, x, mk)


def shards(
    aligned_family_embedding,
    aligned_slot_available,
    chain_site_available,
    duo_embedding,
    averaging_layernorm_stretch,
    lineup_layernorm_stretch,
    duo_layernorm_stretch,
    lefthand_linear_kernel,
    righthand_linear_kernel,
    kronecker_linear_kernel,
    duo_logit_kernel,
    asker_lookup_sigmoid_kernel,
    closing_linear_kernel,
):
    homolog_number, amino_position_number, discarded_carry = aligned_family_embedding.shape
    res_rows = duo_embedding.shape[0]
    opm_width = lefthand_linear_kernel.shape[1]
    head_count = duo_logit_kernel.shape[1]
    inner_width = closing_linear_kernel.shape[0]
    row_index = lax.axis_index("row")
    col_index = lax.axis_index("col")
    standardized_features = standardize_features(aligned_family_embedding.astype(jnp.float32))
    availability_real = aligned_slot_available.astype(jnp.float32)
    half_rows = res_rows
    opm_input = (standardized_features * averaging_layernorm_stretch).astype(jnp.bfloat16)
    left = jnp.einsum("src,ca->sra", opm_input, lefthand_linear_kernel, preferred_element_type=jnp.float32)
    left = (left * availability_real[:, :, None]).astype(jnp.bfloat16)
    left = left.reshape(homolog_number, 2, half_rows * opm_width).transpose(1, 0, 2)
    left_mask = availability_real.reshape(homolog_number, 2, half_rows).transpose(1, 0, 2)
    left_mask = jnp.pad(left_mask, ((0, 0), (0, 0), (0, 128 - half_rows))).astype(jnp.bfloat16)
    left = jnp.concatenate([left, left_mask], axis=2)
    right = jnp.einsum("src,ca->sar", opm_input, righthand_linear_kernel, preferred_element_type=jnp.float32)
    right = (right * availability_real[:, None, :]).astype(jnp.bfloat16)
    right_mask = jnp.pad(availability_real, ((0, 0), (0, 128 - amino_position_number))).astype(jnp.bfloat16)
    right = jnp.concatenate([right.reshape(homolog_number, -1), right_mask], axis=1)
    mask_out = jnp.pad(
        availability_real.reshape(8, homolog_number // 8, amino_position_number),
        ((0, 0), (0, 8 - homolog_number // 8), (0, 128 - amino_position_number)),
    )
    left_all, right_all, near_rows = spread(left, right, aligned_family_embedding)
    residue_float = chain_site_available.astype(jnp.float32)
    residue_rows = lax.dynamic_slice_in_dim(residue_float, row_index * res_rows, res_rows)
    residue_cols = lax.dynamic_slice_in_dim(
        residue_float, col_index * amino_position_number, amino_position_number
    )
    duo_after_averaging, bias_tile, far_rows, own_mask = opm(
        left_all, right_all, residue_rows, residue_cols, duo_embedding,
        duo_layernorm_stretch, kronecker_linear_kernel, duo_logit_kernel, aligned_family_embedding, mask_out,
    )
    lanes = inner_width // 2
    gated = attention(
        bias_tile, aligned_family_embedding, near_rows, far_rows, own_mask, lineup_layernorm_stretch,
        asker_lookup_sigmoid_kernel,
    )
    closing = closing_linear_kernel.reshape(2, lanes, -1)
    summed_increment = jnp.einsum("hsqd,hdc->sqc", gated, closing, preferred_element_type=jnp.float32)
    refreshed_family_embedding = (
        aligned_family_embedding.astype(jnp.float32) + summed_increment
    ).astype(jnp.bfloat16)
    return (refreshed_family_embedding, duo_after_averaging)


def solution(mesh):
    placed = (
        P("row", "col", None),
        P("row", "col"),
        P(),
        P("row", "col", None),
        P(),
        P(),
        P(),
        P(),
        P(),
        P(),
        P(),
        P(),
        P(),
    )
    return jax.shard_map(
        shards,
        mesh=mesh,
        in_specs=placed,
        out_specs=(P("row", "col", None), P("row", "col", None)),
        check_vma=False,
    )
```
